32 devices in a mesh: dp: 4 (over y, core), row: 4 (over z), col: 2 (over x).
Axes of the slice: x: 2, y: 2, z: 4, core: 2. Of those that a mesh axis runs over, the one named last changes fastest.
Arguments:
- inputs: bfloat16 [4096, 1024], P(('dp', 'col'), 'row'), may hold values from -6 to 6
- cotangent: bfloat16 [4096, 1024], P(('dp', 'col'), 'row'), may hold values from -6 to 6
- seg_parent: int32 [52], P('dp'), may hold values from 0 to 51, as said below
- token_depth: int32 [4096], P('dp'), may hold values from 0 to 383, as said below
- ln1_gain: float32 [1024], P('row'), may hold values from 0.25 to 1.75
- ln1_bias: float32 [1024], P('row'), may hold values from -1.5 to 1.5
- w_qkv: bfloat16 [1024, 3, 1024], P('row', None, 'col'), may hold values from -0.1875 to 0.1875
- b_qv: float32 [2, 1024], P(None, 'col'), may hold values from -1.5 to 1.5
- w_out: bfloat16 [1024, 1024], P('col', 'row'), may hold values from -0.5 to 0.5
- b_out: float32 [1024], P('row'), may hold values from -1.5 to 1.5
- ln2_gain: float32 [1024], P('row'), may hold values from 0.25 to 1.75
- ln2_bias: float32 [1024], P('row'), may hold values from -1.5 to 1.5
- w_up: bfloat16 [1024, 4096], P('row', 'col'), may hold values from -0.1875 to 0.1875
- b_up: float32 [4096], P('col'), may hold values from -1.5 to 1.5
- w_down: bfloat16 [4096, 1024], P('col', 'row'), may hold values from -0.125 to 0.125
- b_down: float32 [1024], P('row'), may hold values from -1.5 to 1.5
Outputs:
- result: float32 [4096, 1024], P(('dp', 'col'), 'row')
- input_grad: float32 [4096, 1024], P(('dp', 'col'), 'row')
- grad_ln1_gain: float32 [1024], P('row')
- grad_ln1_bias: float32 [1024], P('row')
- grad_w_qkv: float32 [1024, 3, 1024], P('row', None, 'col')
- grad_b_qv: float32 [2, 1024], P(None, 'col')
- grad_w_out: float32 [1024, 1024], P('col', 'row')
- grad_b_out: float32 [1024], P('row')
- grad_ln2_gain: float32 [1024], P('row')
- grad_ln2_bias: float32 [1024], P('row')
- grad_w_up: float32 [1024, 4096], P('row', 'col')
- grad_b_up: float32 [4096], P('col')
- grad_w_down: float32 [4096, 1024], P('col', 'row')
- grad_b_down: float32 [1024], P('row')
The draws below stay inside these ranges and needn't reach their ends.
Inputs may be any that keep to these rules, and one draw needn't show every extreme that they name: `seg_parent`: tree t holds tokens t * 1024 to (t + 1) * 1024 - 1 and segments 13 t to 13 t + 12, laid out as segment(i) says: segment 13 t is the trunk of 256 tokens and is its own parent; four of the other twelve are branches with the trunk as parent, eight are leaves, two for every branch, with that branch as parent; segment 13 t + 12 is a branch; which ids play the other parts is drawn. `token_depth`: the token at offset j of its segment has depth j in a trunk, 256 + j in a branch and 320 + j in a leaf.
All inputs are finite; a program needn't handle non-finite values.
Results may differ from the reference program's by a relative error of at most 0.011.
Values may be sent and summed in bfloat16 or wider, within the bound.
A program may use at most 192 MiB of HBM per device.

```python
import math
import jax
import jax.numpy as jnp
from jax import lax

D = 1024
HEADS = 8
HD = 128
FF = 4096
TOKENS = 4096
TREE = 1024
SEG = 64
NSEG = 52


def place_role(order, role, slot):
    slot_of_role = jnp.argsort(order, stable=True).astype(jnp.int32)
    where_now = slot_of_role[role]
    displaced = order[slot]
    return order.at[where_now].set(displaced).at[slot].set(role)


def tree_layout(key):
    trees = NSEG // 13
    tree_keys = jax.random.split(jax.random.fold_in(key, 11), trees)

    def one_tree(tree_key, tree_number):
        role_of_slot = jax.random.permutation(tree_key, 13).astype(jnp.int32)
        role_of_slot = place_role(role_of_slot, 0, 0)
        role_of_slot = place_role(role_of_slot, 1, 12)
        slot_of_role = jnp.argsort(role_of_slot, stable=True).astype(jnp.int32)
        lengths = jnp.where(role_of_slot == 0, 4 * SEG, SEG).astype(jnp.int32)
        local_start = jnp.cumsum(lengths) - lengths
        parent_role = jnp.where(role_of_slot <= 4, 0, 1 + (role_of_slot - 5) // 2).astype(jnp.int32)
        parent_slot = slot_of_role[parent_role]
        base_depth = jnp.where(role_of_slot == 0, 0, jnp.where(role_of_slot <= 4, 4 * SEG, 5 * SEG)).astype(jnp.int32)
        where_at = jnp.arange(TREE, dtype=jnp.int32)
        token_slot = jnp.sum((local_start[None, :] <= where_at[:, None]).astype(jnp.int32), axis=1) - 1
        depth_here = base_depth[token_slot] + where_at - local_start[token_slot]
        return (tree_number * 13 + parent_slot, depth_here)
    parents, depths = jax.vmap(one_tree)(tree_keys, jnp.arange(trees, dtype=jnp.int32))
    return (parents.reshape(-1), depths.reshape(-1))


def draw_seg_parent(key, part):
    return tree_layout(key)[0]


def draw_token_depth(key, part):
    return tree_layout(key)[1]


def shard_levels(key, extent, pieces, least, high):
    level = 1.0
    for dim, shards_of in pieces:
        draws = jax.random.uniform(jax.random.fold_in(jax.random.fold_in(key, 6), dim), (shards_of,), jnp.float32, least / len(pieces), high / len(pieces))
        level = level * jnp.repeat(jnp.exp(draws), extent[dim] // shards_of).reshape((-1,) + (1,) * (len(extent) - 1 - dim))
    return level


def bell_draw(rng, extent, scale, bound, shards=(), kind=jnp.bfloat16):
    gain = shard_levels(rng, extent, shards, -0.22, 0.18) if shards else 1.0
    drawn = jax.random.normal(rng, extent, jnp.float32) * scale * gain
    return jnp.minimum(jnp.maximum(drawn, -bound), bound).astype(kind)


def setup_inputs(seed: int = 0) -> dict:
    splits = jax.random.split(jax.random.key(seed), 17)
    return {
        "inputs": bell_draw(splits[0], (TOKENS, D), 1.0, 6.0, ((0, 8), (1, 4))),
        "cotangent": bell_draw(splits[1], (TOKENS, D), 1.0, 6.0, ((0, 8), (1, 4))),
        "seg_parent": draw_seg_parent(jax.random.fold_in(splits[16], 71), 0),
        "token_depth": draw_token_depth(jax.random.fold_in(splits[16], 71), 0),
        "ln1_gain": jnp.clip(1.0 + 0.15 * jax.random.normal(splits[4], (D,), jnp.float32), 0.25, 1.75),
        "ln1_bias": bell_draw(splits[5], (D,), 0.3, 1.5, ((0, 4),), jnp.float32),
        "w_qkv": bell_draw(splits[6], (D, 3, D), D ** -0.5, 0.1875, ((0, 4), (2, 2))),
        "b_qv": bell_draw(splits[7], (2, D), 0.3, 1.5, ((1, 2),), jnp.float32),
        "w_out": bell_draw(splits[8], (D, D), (D // 8) ** -0.5, 0.5, ((0, 2), (1, 4))),
        "b_out": bell_draw(splits[9], (D,), 0.3, 1.5, ((0, 4),), jnp.float32),
        "ln2_gain": jnp.clip(1.0 + 0.15 * jax.random.normal(splits[10], (D,), jnp.float32), 0.25, 1.75),
        "ln2_bias": bell_draw(splits[11], (D,), 0.3, 1.5, ((0, 4),), jnp.float32),
        "w_up": bell_draw(splits[12], (D, FF), D ** -0.5, 0.1875, ((0, 4), (1, 2))),
        "b_up": bell_draw(splits[13], (FF,), 0.3, 1.5, ((0, 2),), jnp.float32),
        "w_down": bell_draw(splits[14], (FF, D), (FF // 2) ** -0.5, 0.125, ((0, 2), (1, 4))),
        "b_down": bell_draw(splits[15], (D,), 0.3, 1.5, ((0, 4),), jnp.float32),
    }


EPS = 1e-05
MASKED = -1e+30
HIGH = lax.Precision.HIGHEST

@jax.custom_vjp
def low(v):
    return lax.optimization_barrier(v.astype(jnp.bfloat16)).astype(jnp.float32)

@jax.custom_vjp
def low_back(v):
    return v

def low_keep(v):
    return (low(v), None)

def low_pass(kept, grad):
    return (grad,)

def back_keep(v):
    return (v, None)

def back_low(kept, grad):
    return (low(grad),)
low.defvjp(low_keep, low_pass)
low_back.defvjp(back_keep, back_low)

def layer_norm(values, norm_gain, norm_bias):
    row_mean = lax.optimization_barrier(jnp.mean(values, axis=-1, keepdims=True))
    variance = lax.optimization_barrier(jnp.mean(values * values, axis=-1, keepdims=True)) - row_mean * row_mean
    return (values - row_mean) * lax.rsqrt(variance + EPS) * norm_gain + norm_bias

def matmul(left_op, right_op):
    return jnp.dot(left_op, right_op, precision=HIGH, preferred_element_type=jnp.float32)

def tree_labels(seg_parent, token_depth):
    seg_ids = jnp.arange(NSEG, dtype=jnp.int32)
    where_at = jnp.arange(TOKENS, dtype=jnp.int32)
    offset = where_at % TREE
    local_seg = jnp.where(offset < 4 * SEG, 0, 1 + (offset - 4 * SEG) // SEG).astype(jnp.int32)
    segment = (13 * (where_at // TREE) + local_seg).astype(jnp.int32)
    parent_one = lax.optimization_barrier(jnp.sum(jnp.where(segment[:, None] == seg_ids[None, :], seg_parent[None, :], 0), axis=1))
    parent_two = lax.optimization_barrier(jnp.sum(jnp.where(parent_one[:, None] == seg_ids[None, :], seg_parent[None, :], 0), axis=1))
    return (segment, parent_one, parent_two, token_depth)

def tree_attention(queries, key_rows, value_rows, labels):
    slopes = jnp.exp2(-(jnp.arange(HEADS, dtype=jnp.int32) + 1).astype(jnp.float32))
    score_scale = 1.0 / math.sqrt(HD)
    block_rows = min(512, TREE)
    blocks = TREE // block_rows
    trees = TOKENS // TREE

    def per_tree(items):
        tree_q, tree_k, tree_v, segment, parent_one, parent_two, token_depth = items

        def per_block(block_items):
            block_q, block_seg, block_one, block_two, block_depth = block_items
            allowed = ((segment[None, :] == block_seg[:, None]) | (segment[None, :] == block_one[:, None]) | (segment[None, :] == block_two[:, None])) & (token_depth[None, :] <= block_depth[:, None])
            raw = jnp.einsum('qhd,khd->hqk', block_q, tree_k, precision=HIGH)
            distance = (block_depth[:, None] - token_depth[None, :]).astype(jnp.float32)
            scores = low_back(raw * score_scale - slopes[:, None, None] * distance[None])
            scores = jnp.where(allowed[None], scores, MASKED)
            probs = jax.nn.softmax(scores, axis=-1)
            return jnp.einsum('hqk,khd->qhd', low(probs), tree_v, precision=HIGH)

        def split_block(array):
            return array.reshape((blocks, block_rows) + array.shape[1:])
        mixed = lax.map(jax.checkpoint(per_block), (split_block(tree_q), split_block(segment), split_block(parent_one), split_block(parent_two), split_block(token_depth)))
        return mixed.reshape(tree_q.shape)

    def split_tree(array):
        return array.reshape((trees, TREE) + array.shape[1:])
    segment, parent_one, parent_two, token_depth = labels
    mixed = lax.map(per_tree, (split_tree(queries), split_tree(key_rows), split_tree(value_rows), split_tree(segment), split_tree(parent_one), split_tree(parent_two), split_tree(token_depth)))
    return mixed.reshape(queries.shape)

def forward(states, params, labels):
    ln1_gain, ln1_bias, w_qkv, b_qv, w_out, b_out, ln2_gain, ln2_bias, w_up, b_up, w_down, b_down = params
    entry_one = low(layer_norm(states, ln1_gain, ln1_bias))
    projected = matmul(entry_one, w_qkv.reshape(D, 3 * D)).reshape(TOKENS, 3, D)
    queries = low_back(low(projected[:, 0] + b_qv[0]))
    key_rows = low_back(low(projected[:, 1]))
    value_rows = low_back(low(projected[:, 2] + b_qv[1]))
    mixed = tree_attention(queries.reshape(TOKENS, HEADS, HD), key_rows.reshape(TOKENS, HEADS, HD), value_rows.reshape(TOKENS, HEADS, HD), labels).reshape(TOKENS, D)
    mixed = low_back(low(mixed))
    middle = states + low_back(matmul(mixed, w_out) + b_out)
    entry_two = low(layer_norm(middle, ln2_gain, ln2_bias))
    hidden_pre = low_back(matmul(entry_two, w_up) + b_up)
    hidden = low(jax.nn.gelu(hidden_pre, approximate=False))
    return middle + low_back(matmul(hidden, w_down) + b_down)

def reference(inputs, cotangent, seg_parent, token_depth, ln1_gain, ln1_bias, w_qkv, b_qv, w_out, b_out, ln2_gain, ln2_bias, w_up, b_up, w_down, b_down):
    labels = tree_labels(seg_parent, token_depth)
    params = (ln1_gain, ln1_bias, w_qkv.astype(jnp.float32), b_qv, w_out.astype(jnp.float32), b_out, ln2_gain, ln2_bias, w_up.astype(jnp.float32), b_up, w_down.astype(jnp.float32), b_down)
    states = inputs.astype(jnp.float32)
    result, pullback = jax.vjp(lambda st, pa: forward(st, pa, labels), states, params)
    input_grad, grads = pullback(cotangent.astype(jnp.float32))
    return (result, input_grad, grads[0], grads[1], grads[2], grads[3], grads[4], grads[5], grads[6], grads[7], grads[8], grads[9], grads[10], grads[11])
```

```python
import functools
import math

import jax
import jax.numpy as jnp
from jax import lax
from jax.experimental import pallas as pl
from jax.experimental.pallas import tpu as pltpu
from jax.sharding import PartitionSpec as P

MESH = pl.DeviceIdType.MESH
BF = jnp.bfloat16
F32 = jnp.float32


HD = 128


EPS = 1e-05
MASKED = -1e30


def gelu_value(values):
    return 0.5 * values * (1.0 + jax.scipy.special.erf(values / math.sqrt(2.0)))


def gelu_slope(values):
    return 0.5 * (1.0 + jax.scipy.special.erf(values / math.sqrt(2.0))) + values * jnp.exp(
        -0.5 * values * values
    ) / math.sqrt(2.0 * math.pi)


def width_sums(first_term, second_term):
    return lax.psum((jnp.sum(first_term, axis=1), jnp.sum(second_term, axis=1)), "row")


def normalize(values, norm_gain, norm_bias, feature_count):
    row_total, square = width_sums(values, values * values)
    row_mean = row_total / feature_count
    inv_std = lax.rsqrt(square / feature_count - row_mean * row_mean + EPS)
    normed = (values - row_mean[:, None]) * inv_std[:, None]
    return (normed, inv_std, (normed * norm_gain + norm_bias).astype(jnp.bfloat16))


def normalize_back(upstream, normed, inv_std, norm_gain, feature_count):
    spread = upstream * norm_gain
    row_total, cross_sum = width_sums(spread, spread * normed)
    return inv_std[:, None] * (
        spread - row_total[:, None] / feature_count - normed * (cross_sum[:, None] / feature_count)
    )


def contract(left_op, right_op, flipped):
    if flipped:
        return lax.dot_general(
            left_op, right_op, (((1,), (1,)), ((), ())), preferred_element_type=jnp.float32
        )
    return jnp.dot(left_op, right_op, preferred_element_type=jnp.float32)


def outer_sum(left_op, right_op):
    return lax.dot_general(
        left_op, right_op, (((0,), (0,)), ((), ())), preferred_element_type=jnp.float32
    )


def across_rows(operand, weight_block, flipped):
    gathered = lax.all_gather(operand, "col", axis=0, tiled=True)
    row_count = gathered.shape[0] // lax.axis_size("row")

    def partial_term(row_start, row_num):
        return contract(gathered, weight_block, flipped)

    return (
        lax.psum_scatter(
            partial_term(jnp.int32(0), row_count * lax.axis_size("row")),
            "row",
            scatter_dimension=0,
            tiled=True,
        ),
        gathered,
    )


def across_cols(operand, weight_block, flipped):
    gathered = lax.all_gather(operand, "row", axis=0, tiled=True)
    row_count = gathered.shape[0] // lax.axis_size("col")

    def partial_term(row_start, row_num):
        return contract(gathered, weight_block, flipped)

    return (
        lax.psum_scatter(
            partial_term(jnp.int32(0), row_count * lax.axis_size("col")),
            "col",
            scatter_dimension=0,
            tiled=True,
        ),
        gathered,
    )


def tree_labels(seg_parent, token_depth):
    seg_count = seg_parent.shape[0]
    tree_len = token_depth.shape[0]
    seg_len = tree_len // 16
    slot_ids = jnp.arange(seg_count, dtype=jnp.int32)
    where_at = jnp.arange(tree_len, dtype=jnp.int32)
    segment = jnp.where(where_at < 4 * seg_len, 0, 1 + (where_at - 4 * seg_len) // seg_len)
    parent_local = seg_parent - lax.axis_index("dp") * seg_count
    parent_one = jnp.sum(
        jnp.where(segment[:, None] == slot_ids[None, :], parent_local[None, :], 0), axis=1
    )
    parent_two = jnp.sum(
        jnp.where(parent_one[:, None] == slot_ids[None, :], parent_local[None, :], 0), axis=1
    )
    return (segment, parent_one, parent_two, token_depth)


def block_scores(query_block, key_rows, labels, query_start, slopes):
    segment, parent_one, parent_two, token_depth = labels
    block_size = query_block.shape[0]
    query_seg = lax.dynamic_slice_in_dim(segment, query_start, block_size, 0)
    query_one = lax.dynamic_slice_in_dim(parent_one, query_start, block_size, 0)
    query_two = lax.dynamic_slice_in_dim(parent_two, query_start, block_size, 0)
    query_depth = lax.dynamic_slice_in_dim(token_depth, query_start, block_size, 0)
    allowed = (
        (segment[None, :] == query_seg[:, None])
        | (segment[None, :] == query_one[:, None])
        | (segment[None, :] == query_two[:, None])
    ) & (token_depth[None, :] <= query_depth[:, None])
    score_scale = query_block.shape[2] ** (-0.5)
    raw = jnp.einsum("qhd,khd->hqk", query_block, key_rows, preferred_element_type=jnp.float32)
    distance = (query_depth[:, None] - token_depth[None, :]).astype(jnp.float32)
    scores = raw * score_scale - slopes[:, None, None] * distance[None]
    return jnp.where(allowed[None], scores, MASKED)


def attention_forward(queries, key_rows, value_rows, labels, slopes, offset):
    block_size = min(512, queries.shape[0])
    blocks = queries.shape[0] // block_size

    def one_block(block_index):
        block_first = block_index * block_size
        query_block = lax.dynamic_slice_in_dim(queries, block_first, block_size, 0)
        scores = block_scores(query_block, key_rows, labels, offset + block_first, slopes)
        top_score = jnp.max(scores, axis=2, keepdims=True)
        weights = jnp.exp(scores - top_score)
        weight_total = jnp.sum(weights, axis=2, keepdims=True)
        probs = (weights / weight_total).astype(jnp.bfloat16)
        mixed = jnp.einsum("hqk,khd->qhd", probs, value_rows, preferred_element_type=jnp.float32)
        return (mixed, (top_score + jnp.log(weight_total))[:, :, 0])

    return lax.map(one_block, jnp.arange(blocks, dtype=jnp.int32))


def attention_backward(
    queries, key_rows, value_rows, grad_mixed, log_total, labels, slopes, offset
):
    block_size = min(512, queries.shape[0])
    blocks = queries.shape[0] // block_size
    score_scale = queries.shape[2] ** (-0.5)

    def one_block(carry, items):
        key_grad, value_grad = carry
        block_index, block_total = items
        block_first = block_index * block_size
        query_block = lax.dynamic_slice_in_dim(queries, block_first, block_size, 0)
        grad_block = lax.dynamic_slice_in_dim(grad_mixed, block_first, block_size, 0)
        scores = block_scores(query_block, key_rows, labels, offset + block_first, slopes)
        probs = jnp.exp(scores - block_total[:, :, None])
        grad_probs = jnp.einsum(
            "qhd,khd->hqk", grad_block, value_rows, preferred_element_type=jnp.float32
        )
        centre = jnp.sum(probs * grad_probs, axis=2, keepdims=True)
        grad_scores = (probs * (grad_probs - centre)).astype(jnp.bfloat16)
        query_grad = (
            jnp.einsum("hqk,khd->qhd", grad_scores, key_rows, preferred_element_type=jnp.float32)
            * score_scale
        )
        key_grad = (
            key_grad
            + jnp.einsum(
                "hqk,qhd->khd", grad_scores, query_block, preferred_element_type=jnp.float32
            )
            * score_scale
        )
        value_grad = value_grad + jnp.einsum(
            "hqk,qhd->khd",
            probs.astype(jnp.bfloat16),
            grad_block,
            preferred_element_type=jnp.float32,
        )
        return ((key_grad, value_grad), query_grad)

    empty = jnp.zeros(key_rows.shape, jnp.float32)
    (key_grad, value_grad), query_grad = lax.scan(
        one_block, (empty, empty), (jnp.arange(blocks, dtype=jnp.int32), log_total)
    )
    return (key_grad, value_grad, query_grad)


def on_device(
    inputs,
    cotangent,
    seg_parent,
    token_depth,
    ln1_gain,
    ln1_bias,
    w_qkv,
    b_qv,
    w_out,
    b_out,
    ln2_gain,
    ln2_bias,
    w_up,
    b_up,
    w_down,
    b_down,
):
    feature_count = inputs.shape[1] * lax.axis_size("row")
    col_width = w_qkv.shape[2]
    heads_here = col_width // HD
    qkv_flat = w_qkv.reshape(w_qkv.shape[0], 3 * col_width)
    labels = tree_labels(seg_parent, token_depth)
    heads_seen = lax.axis_index("col") * heads_here + jnp.arange(heads_here, dtype=jnp.int32)
    slopes = jnp.exp2(-(heads_seen + 1).astype(jnp.float32))
    states = inputs.astype(jnp.float32)
    normed_one, inv_one, entry_one = normalize(states, ln1_gain, ln1_bias, feature_count)
    projected, entry_one_all = across_rows(entry_one, qkv_flat, False)
    tok_rows = projected.shape[0]
    projected = projected.reshape(tok_rows, 3, col_width)
    queries = (projected[:, 0] + b_qv[0]).astype(jnp.bfloat16)
    keys_here = projected[:, 1].astype(jnp.bfloat16)
    values_here = (projected[:, 2] + b_qv[1]).astype(jnp.bfloat16)
    pair_all = lax.all_gather(
        jnp.stack([keys_here, values_here], axis=1), "row", axis=0, tiled=True
    )
    key_rows = pair_all[:, 0].reshape(-1, heads_here, HD)
    value_rows = pair_all[:, 1].reshape(-1, heads_here, HD)
    query_heads = queries.reshape(tok_rows, heads_here, HD)
    offset = lax.axis_index("row") * tok_rows
    mixed, log_total = attention_forward(query_heads, key_rows, value_rows, labels, slopes, offset)
    mixed = mixed.reshape(tok_rows, col_width).astype(jnp.bfloat16)
    attn_out, mixed_all = across_cols(mixed, w_out, False)
    middle = states + attn_out + b_out
    normed_two, inv_two, entry_two = normalize(middle, ln2_gain, ln2_bias, feature_count)
    hidden_pre, entry_two_all = across_rows(entry_two, w_up, False)
    hidden_pre = hidden_pre + b_up
    hidden = gelu_value(hidden_pre).astype(jnp.bfloat16)
    ffn_out, hidden_all = across_cols(hidden, w_down, False)
    result = middle + ffn_out + b_down
    grad_hidden, down_all = across_rows(cotangent, w_down, True)
    grad_pre = (grad_hidden * gelu_slope(hidden_pre)).astype(jnp.bfloat16)
    grad_entry_two, pre_all = across_cols(grad_pre, w_up, True)
    grad_middle = cotangent.astype(jnp.float32) + normalize_back(
        grad_entry_two, normed_two, inv_two, ln2_gain, feature_count
    )
    grad_branch = grad_middle.astype(jnp.bfloat16)
    grad_mixed, branch_all = across_rows(grad_branch, w_out, True)
    grad_mixed = grad_mixed.astype(jnp.bfloat16).reshape(tok_rows, heads_here, HD)
    key_grad, value_grad, query_grad = attention_backward(
        query_heads, key_rows, value_rows, grad_mixed, log_total, labels, slopes, offset
    )
    kv_grads = lax.psum_scatter(
        jnp.stack([key_grad.reshape(-1, col_width), value_grad.reshape(-1, col_width)], axis=1),
        "row",
        scatter_dimension=0,
        tiled=True,
    )
    grad_projected = jnp.stack(
        [
            query_grad.reshape(tok_rows, col_width).astype(jnp.bfloat16),
            kv_grads[:, 0].astype(jnp.bfloat16),
            kv_grads[:, 1].astype(jnp.bfloat16),
        ],
        axis=1,
    )
    grad_entry_one, proj_all = across_cols(
        grad_projected.reshape(tok_rows, 3 * col_width), qkv_flat, True
    )
    input_grad = grad_middle + normalize_back(
        grad_entry_one, normed_one, inv_one, ln1_gain, feature_count
    )
    proj_sums = jnp.sum(proj_all.astype(jnp.float32), axis=0).reshape(3, col_width)
    weight_terms = (
        outer_sum(entry_one_all, proj_all).reshape(w_qkv.shape),
        jnp.stack([proj_sums[0], proj_sums[2]], axis=0),
        outer_sum(mixed_all, branch_all),
        jnp.sum(branch_all.astype(jnp.float32), axis=0),
        outer_sum(entry_two_all, pre_all),
        jnp.sum(pre_all.astype(jnp.float32), axis=0),
        outer_sum(hidden_all, down_all),
        jnp.sum(down_all.astype(jnp.float32), axis=0),
    )
    (
        grad_w_qkv,
        grad_b_qv,
        grad_w_out,
        grad_b_out,
        grad_w_up,
        grad_b_up,
        grad_w_down,
        grad_b_down,
    ) = lax.psum(
        (
            weight_terms[0],
            weight_terms[1],
            weight_terms[2],
            weight_terms[3],
            weight_terms[4],
            weight_terms[5],
            weight_terms[6],
            weight_terms[7],
        ),
        "dp",
    )
    norm_terms = (
        jnp.sum(grad_entry_one * normed_one, axis=0),
        jnp.sum(grad_entry_one, axis=0),
        jnp.sum(grad_entry_two * normed_two, axis=0),
        jnp.sum(grad_entry_two, axis=0),
    )
    grad_ln1_gain, grad_ln1_bias, grad_ln2_gain, grad_ln2_bias = lax.psum(
        (norm_terms[0], norm_terms[1], norm_terms[2], norm_terms[3]), ("dp", "col")
    )
    return (
        result,
        input_grad,
        grad_ln1_gain,
        grad_ln1_bias,
        grad_w_qkv,
        grad_b_qv,
        grad_w_out,
        grad_b_out,
        grad_ln2_gain,
        grad_ln2_bias,
        grad_w_up,
        grad_b_up,
        grad_w_down,
        grad_b_down,
    )


RELS = (0, 4, 2, 6)


def dot_nn(a, b):
    return lax.dot_general(a, b, (((1,), (0,)), ((), ())), preferred_element_type=F32)


def dot_nt(a, b):
    return lax.dot_general(a, b, (((1,), (1,)), ((), ())), preferred_element_type=F32)


def dot_tn(a, b):
    return lax.dot_general(a, b, (((0,), (0,)), ((), ())), preferred_element_type=F32)


def span(index, size):
    return pl.ds(pl.multiple_of(index * size, size), size)


class Net:
    def __init__(self, ssem, rsem):
        self.dp = lax.axis_index("dp")
        self.row = lax.axis_index("row")
        self.col = lax.axis_index("col")
        self.y, self.k = self.dp // 2, self.dp % 2
        self.zh, self.zl = self.row // 2, self.row % 2
        self.x = self.col
        self.slot = self.x * 4 + self.zl * 2 + self.k
        self.chip = self.x * 2 + self.zl
        self.slice = self.zl * 2 + self.k
        self.ssem, self.rsem = ssem, rsem
        self.used = 0
        self.pending = []

    def sites(self, n):
        first = self.used
        self.used += n
        return first

    def peer(self, dy=0, dk=0, dz=0, dx=0):
        return (
            (self.y ^ dy) * 2 + (self.k ^ dk),
            self.row ^ dz,
            self.col ^ dx,
        )

    def rel(self, rel):
        return self.peer(dz=(rel >> 1) & 1, dx=rel >> 2, dk=rel & 1)

    def make(self, src, dst, site, device, recv_site=None):
        recv = site if recv_site is None else recv_site
        return pltpu.make_async_remote_copy(
            src_ref=src,
            dst_ref=dst,
            send_sem=self.ssem.at[site],
            recv_sem=self.rsem.at[recv],
            device_id=device,
            device_id_type=MESH,
        )

    def send(self, src, dst, site, device, recv_site=None, skip=None):
        remote = self.make(src, dst, site, device, recv_site)
        if skip is None:
            remote.start()
        else:
            recv = site if recv_site is None else recv_site

            @pl.when(skip)
            def _():
                pltpu.make_async_copy(src, dst, self.rsem.at[recv]).start()

            @pl.when(jnp.logical_not(skip))
            def _():
                remote.start()

        self.pending.append((remote, skip))
        return remote

    def landed(self, ref, site):
        self.make(ref, ref, site, self.peer(dk=1)).wait_recv()

    def drain(self, upto=None):
        for remote, skip in self.pending:
            if skip is None:
                remote.wait_send()
            else:

                @pl.when(jnp.logical_not(skip))
                def _(remote=remote):
                    remote.wait_send()

        self.pending = []


class Gather:
    def __init__(self, net, buf):
        self.net, self.buf = net, buf
        self.first = net.sites(7)

    def start(self):
        net, buf = self.net, self.buf
        own = buf.at[net.slot]
        net.send(own, own, self.first, net.rel(1))
        for j in (1, 2, 3):
            net.send(own, own, self.first + j, net.rel(RELS[j]))

    def relay(self, j):
        net, buf = self.net, self.buf
        part = buf.at[net.slot ^ RELS[j]]
        net.landed(part, self.first + j)
        net.send(part, part, self.first + 3 + j, net.rel(1))

    def ready(self, j):
        net, buf = self.net, self.buf
        part = buf.at[net.slot ^ RELS[j] ^ 1]
        net.landed(part, self.first if j == 0 else self.first + 3 + j)

    def block(self, j):
        chip = self.net.chip ^ (RELS[j] >> 1)
        both = self.buf[pl.ds(chip * 2, 2)]
        return both.reshape(2 * both.shape[1], both.shape[2])


class Scatter:
    def __init__(self, net, part, hop, land_one, land_two):
        self.net, self.part, self.hop_buf = net, part, hop
        self.one, self.two = land_one, land_two
        self.first = net.sites(7)
        self.sent = []

    def put(self, j, value):
        net = self.net
        chip = net.chip ^ (RELS[j] >> 1)
        shard = self.part.shape[1]
        self.part[pl.ds(chip * 2, 2)] = value.astype(BF).reshape(2, shard, value.shape[1])
        self.push(j)

    def push(self, j):
        net = self.net
        chip = net.chip ^ (RELS[j] >> 1)
        self.sent.append(
            net.send(
                self.part.at[chip * 2 + (1 - net.k)],
                self.one.at[j],
                self.first + j,
                net.rel(1),
            )
        )

    def chip_sum(self, j):
        net = self.net
        chip = net.chip ^ (RELS[j] >> 1)
        net.landed(self.one.at[j], self.first + j)
        return self.part[chip * 2 + net.k].astype(F32) + self.one[j].astype(F32)

    def hop(self, j):
        net = self.net
        self.hop_buf[j - 1] = self.chip_sum(j).astype(BF)
        self.sent.append(
            net.send(
                self.hop_buf.at[j - 1],
                self.two.at[j - 1],
                self.first + 3 + j,
                net.rel(RELS[j]),
            )
        )

    def left(self):
        for remote in self.sent:
            remote.wait_send()
        mine = {id(remote) for remote in self.sent}
        self.net.pending = [p for p in self.net.pending if id(p[0]) not in mine]

    def total(self):
        net = self.net
        value = self.chip_sum(0)
        for j in (1, 2, 3):
            net.landed(self.two.at[j - 1], self.first + 3 + j)
            value = value + self.two[j - 1].astype(F32)
        return value


class TreeSum:
    def __init__(self, net, own, land_y, hop, land_z, done, out):
        self.net, self.own, self.land_y = net, own, land_y
        self.hop_buf, self.land_z, self.done, self.out = hop, land_z, done, out
        self.first = net.sites(8)

    def start(self):
        net = self.net
        net.send(self.own.at[:, 1 - net.y], self.land_y, self.first, net.peer(dy=1))

    def across(self):
        net = self.net
        net.landed(self.land_y, self.first)
        far = 1 - net.zh
        self.hop_buf[...] = (
            self.own[far, net.y].astype(F32) + self.land_y[far].astype(F32)
        ).astype(BF)
        net.send(self.hop_buf, self.land_z, self.first + 1, net.peer(dz=2))

    def hand_out(self):
        net = self.net
        net.landed(self.land_z, self.first + 1)
        self.done[...] = (
            self.own[net.zh, net.y].astype(F32)
            + self.land_y[net.zh].astype(F32)
            + self.land_z[...].astype(F32)
        ).astype(BF)
        place = self.out.at[net.slice]
        target = net.zh * 2 + net.y
        for step in (0, 1):
            net.send(
                self.done,
                place,
                self.first + 2 + step,
                ((net.y ^ step) * 2 + net.k, target, net.col),
                recv_site=self.first + 4 + net.zl,
                skip=(target == net.row) if step == 0 else None,
            )

    def share(self):
        net = self.net
        for low in (0, 1):
            part = self.out.at[low * 2 + net.k]
            net.landed(part, self.first + 4 + low)
            net.send(part, part, self.first + 6 + low, net.rel(1))

    def finish(self):
        net = self.net
        for low in (0, 1):
            net.landed(self.out.at[low * 2 + (1 - net.k)], self.first + 6 + low)


def layer_kernel(eps, masked, sems, *refs):
    (
        inp, cot, w_q, w_o, w_d, w_u, tab, vec_in, b_up, b_qv,
        res_out, grad_out, out_q, out_o, out_d, out_u, out_tok, out_small,
        xs, e1, g, e2, gb, wq, wo, wd, wu, tab_far, vec, bias,
        q_buf, k_buf, v_buf, p_buf, mix, mix_b,
        part_a, part_b, hop_a, hop_b, one, two,
        gh, hid, gp, gm, dk_acc, dv_acc, dqkv, mid, gmid, back_a, back_b,
        dw_q, dw_o, dw_d, dw_u, ly_q, ly_o, ly_d, ly_u,
        yh_q, yh_o, yh_d, yh_u, lz_q, lz_o, lz_d, lz_u,
        fin_q, fin_o, fin_d, fin_u,
        tok, tok_one, tok_sum, tok_two, small, small_land, small_sum,
        ssem, rsem, lsem,
    ) = refs
    net = Net(ssem, rsem)
    y, k, zh, zl, x, row = net.y, net.k, net.zh, net.zl, net.x, net.row
    shard, width = xs.shape
    tokens = 8 * shard
    quarter = width // 4
    head = q_buf.shape[1]

    greet = [
        net.peer(dy=dy, dk=dk, dz=dz)
        for dy in (0, 1)
        for dk in (0, 1)
        for dz in (0, 1, 2, 3)
        if dy + dk + dz
    ]
    greet += [net.peer(dk=dk, dz=dz, dx=1) for dk in (0, 1) for dz in (0, 1)]
    barrier = pltpu.get_barrier_semaphore()
    for device in greet:
        pl.semaphore_signal(barrier, inc=1, device_id=device, device_id_type=MESH)
    pl.semaphore_wait(barrier, len(greet))

    def send_home(src, dst_of, first):
        for s in range(4):
            low, core = s // 2, s % 2
            target = 2 * k + low
            net.send(
                src.at[span(s, shard), :],
                dst_of(s).at[:, span(row, quarter)],
                first + s,
                (y * 2 + core, target, net.col),
                recv_site=first + 4 + row,
                skip=(target == row) & (k == core),
            )

    def home_ready(dst, first):
        for z in range(4):
            net.landed(dst.at[:, span(z, quarter)], first + 4 + z)

    home_x, home_g = net.sites(8), net.sites(8)
    send_home(inp, lambda s: xs, home_x)

    vec_site = net.sites(3)
    for o in (1, 2, 3):
        net.send(
            vec_in, vec.at[:, span(row, quarter)], vec_site + o - 1, net.peer(dz=o)
        )
    tab_site = net.sites(1)
    net.send(tab, tab_far, tab_site, net.rel(1))

    def slices(w_ref, full, axis):
        if axis == 0:
            rows = full.shape[0] // 4
            return rows, lambda z: full.at[span(z, rows), :]
        cols = full.shape[1] // 4
        return full.shape[0], lambda z: full.at[:, span(z, cols)]

    class Weight:
        def __init__(self, src_of, full, axis, local):
            self.src_of, self.full = src_of, full
            self.rows, self.place = slices(None, full, axis)
            self.first = net.sites(6)
            self.local = local

        def half(self, ref, which):
            rows = self.rows // 2
            return ref.at[span(which, rows), :]

        def start(self):
            own = pltpu.make_async_copy(
                self.src_of(net.slice), self.place(row), lsem.at[self.local]
            )
            own.start()
            for o in (1, 2, 3):
                far = (zl ^ (o & 1)) * 2 + k
                net.send(
                    self.half(self.src_of(far), y),
                    self.half(self.place(row), y),
                    self.first + o - 1,
                    net.peer(dz=o),
                )
            self.own = own

        def relay(self):
            for o in (1, 2, 3):
                part = self.half(self.place(row ^ o), y)
                net.landed(part, self.first + o - 1)
                net.send(part, part, self.first + 2 + o, net.peer(dy=1))

        def ready(self):
            for o in (1, 2, 3):
                net.landed(self.half(self.place(row ^ o), 1 - y), self.first + 2 + o)
            self.own.wait()

    hidden = hid.shape[1]
    weight_q = Weight(lambda s: w_q.at[s], wq, 0, 0)
    weight_o = Weight(lambda s: w_o.at[span(s, head), :], wo, 1, 1)
    weight_d = Weight(lambda s: w_d.at[span(s, hidden), :], wd, 1, 2)
    weight_u = Weight(lambda s: w_u.at[:, span(s, hidden)], wu, 0, 3)
    weight_q.start()
    send_home(cot, lambda s: g.at[x * 4 + s], home_g)
    weight_o.start()

    vec[:, span(row, quarter)] = vec_in[...]
    for o in (1, 2, 3):
        net.landed(vec.at[:, span(row ^ o, quarter)], vec_site + o - 1)

    def norm_stats(values):
        mean = jnp.sum(values, axis=1, keepdims=True) * (1.0 / width)
        msq = jnp.sum(values * values, axis=1, keepdims=True) * (1.0 / width)
        inv = lax.rsqrt(msq - mean * mean + eps)
        return (values - mean) * inv, inv

    home_ready(xs, home_x)
    normed, _ = norm_stats(xs[...].astype(F32))
    e1[net.slot] = (normed * vec[0:1, :] + vec[1:2, :]).astype(BF)
    gather_e1 = Gather(net, e1)
    gather_e1.start()
    gather_g = Gather(net, g)
    weight_d.start()
    weight_u.start()
    weight_q.relay()
    home_ready(g.at[net.slot], home_g)

    net.landed(tab_far, tab_site)
    table = jnp.where(zh == k, tab[...], tab_far[...])
    exponent = jnp.full((1, tokens), -(x * 4 + net.slice + 1), jnp.int32).astype(F32)
    slope = jnp.exp2(exponent)
    bias[...] = jnp.where(table >= 0.0, slope * table, masked)

    b_q = b_qv[0:1, span(net.slice, head)]
    b_v = b_qv[1:2, span(net.slice, head)]
    weight_q.ready()
    for j in range(4):
        if j:
            gather_e1.relay(j)
        if j == 3:
            gather_g.start()
        gather_e1.ready(j)
        rows = span(net.chip ^ (RELS[j] >> 1), 2 * shard)
        proj = dot_nn(gather_e1.block(j), wq[...])
        q_buf[rows, :] = (proj[:, :head] + b_q).astype(BF)
        k_buf[rows, :] = proj[:, head : 2 * head].astype(BF)
        v_buf[rows, :] = (proj[:, 2 * head :] + b_v).astype(BF)
    weight_o.relay()

    scale = head ** (-0.5)
    seg_len = tokens // 16
    key_at = lax.broadcasted_iota(jnp.int32, (1, tokens), 1)
    key_half = key_at // seg_len
    key_seg = jnp.maximum(key_half - 3, 0)

    def attend(i, carry):
        first = pl.multiple_of(i * shard, shard)
        raw = dot_nt(q_buf[pl.ds(first, shard), :], k_buf[...])
        parts = []
        for half in (0, 1):
            at = 2 * i + half
            seg = jnp.maximum(at - 3, 0)
            later = jnp.where(key_seg == seg, key_at, -1)
            query_at = first + half * seg_len + lax.broadcasted_iota(jnp.int32, (seg_len, 1), 0)
            scores = raw[half * seg_len : (half + 1) * seg_len] * scale + bias[pl.ds(at, 1), :]
            scores = jnp.where(later > query_at, masked, scores)
            top = jnp.max(scores, axis=1, keepdims=True)
            weights = jnp.exp(scores - top)
            norm = 1.0 / jnp.sum(weights, axis=1, keepdims=True)
            parts.append((weights * norm).astype(BF))
        probs = jnp.concatenate(parts, axis=0)
        p_buf[pl.ds(first, shard), :] = probs
        mixed = dot_nn(probs, v_buf[...])
        mix[pl.ds(first, shard), :] = mixed
        mix_b[pl.ds(first, shard), :] = mixed.astype(BF)
        return carry

    lax.fori_loop(0, 8, attend, 0)

    for j in (1, 2, 3):
        gather_g.relay(j)
    weight_o.ready()

    def rows_of(j):
        return span(net.chip ^ (RELS[j] >> 1), 2 * shard)

    order = (3, 1, 2, 0)
    scatter = Scatter(net, part_a, hop_a, one.at[0], two.at[0])
    for j in order:
        scatter.put(j, dot_nn(mix_b[rows_of(j), :], wo[...]))
    for j in (3, 1, 2):
        scatter.hop(j)
    weight_d.relay()
    weight_u.relay()
    weight_d.ready()
    gather_g.ready(0)
    gather_g.ready(1)
    gather_g.ready(2)
    gather_g.ready(3)

    def hidden_grad(c, carry):
        rows = span(c, 2 * shard)
        both = g[pl.ds(c * 2, 2)].reshape(2 * shard, width)
        gh[rows, :] = dot_nt(both, wd[...])
        return carry

    lax.fori_loop(0, 4, hidden_grad, 0)

    middle = xs[...].astype(F32) + scatter.total() + vec[2:3, :]
    mid[...] = middle
    normed, _ = norm_stats(middle)
    e2[net.slot] = (normed * vec[3:4, :] + vec[4:5, :]).astype(BF)
    gather_e2 = Gather(net, e2)
    gather_e2.start()
    scatter.left()

    b_u = b_up[0:1, span(net.slice, hidden)]
    weight_u.ready()
    scatter_two = Scatter(net, part_a, hop_a, one.at[1], two.at[1])
    for j in range(4):
        if j:
            gather_e2.relay(j)
        gather_e2.ready(j)
        pre = dot_nn(gather_e2.block(j), wu[...]) + b_u
        bell = 0.5 * (1.0 + lax.erf(pre * (1.0 / math.sqrt(2.0))))
        hid[rows_of(j), :] = (pre * bell).astype(BF)
        rise = bell + pre * jnp.exp(-0.5 * pre * pre) * (1.0 / math.sqrt(2.0 * math.pi))
        gp[rows_of(j), :] = (gh[rows_of(j), :] * rise).astype(BF)
        scatter_two.put(j, dot_nt(gp[rows_of(j), :], wu[...]))
        if j > 1:
            scatter_two.hop(j - 1)
    scatter_two.hop(3)

    sum_d = TreeSum(net, dw_d, ly_d, yh_d, lz_d, fin_d, out_d)
    sum_u = TreeSum(net, dw_u, ly_u, yh_u, lz_u, fin_u, out_u)
    sum_o = TreeSum(net, dw_o, ly_o, yh_o, lz_o, fin_o, out_o)
    sum_q = TreeSum(net, dw_q, ly_q, yh_q, lz_q, fin_q, out_q)

    def columns(buf, z):
        part = buf[:, :, span(z, quarter)]
        return part.reshape(tokens, quarter)

    def grad_down(z, carry):
        dw_d[z // 2, z % 2] = dot_tn(hid[...], columns(g, z)).astype(BF)
        return carry

    lax.fori_loop(0, 4, grad_down, 0)
    sum_d.start()

    grad = scatter_two.total()
    middle = mid[...]
    normed, inv = norm_stats(middle)
    tok[2:3, :] = jnp.sum(grad * normed, axis=0, keepdims=True)
    tok[3:4, :] = jnp.sum(grad, axis=0, keepdims=True)
    spread = grad * vec[3:4, :]
    mean_one = jnp.sum(spread, axis=1, keepdims=True) * (1.0 / width)
    mean_two = jnp.sum(spread * normed, axis=1, keepdims=True) * (1.0 / width)
    cot_own = g[net.slot].astype(F32)
    tok[5:6, :] = jnp.sum(cot_own, axis=0, keepdims=True)
    total = cot_own + inv * (spread - mean_one - normed * mean_two)
    gmid[...] = total
    branch = total.astype(BF)
    gb[net.slot] = branch
    tok[4:5, :] = jnp.sum(branch.astype(F32), axis=0, keepdims=True)
    tok[6:8, :] = jnp.zeros((2, width), F32)
    gather_gb = Gather(net, gb)
    gather_gb.start()

    scatter_three = Scatter(net, part_b, hop_b, one.at[2], two.at[2])
    for j in order:
        scatter_three.put(j, dot_nn(hid[rows_of(j), :], wd[...]))

    dk_acc[...] = jnp.zeros_like(dk_acc)
    dv_acc[...] = jnp.zeros_like(dv_acc)

    def attend_back(first):
        rows = pl.ds(first, shard)
        grad_mix = gm[rows, :]
        probs = p_buf[rows, :]
        grad_probs = dot_nt(grad_mix, v_buf[...])
        centre = jnp.sum(mix[rows, :] * grad_mix.astype(F32), axis=1, keepdims=True)
        grad_scores = (probs.astype(F32) * (grad_probs - centre)).astype(BF)
        dqkv[rows, :head] = (dot_nn(grad_scores, k_buf[...]) * scale).astype(BF)
        dk_acc[...] += dot_tn(grad_scores, q_buf[rows, :])
        dv_acc[...] += dot_tn(probs, grad_mix)

    for j in range(4):
        if j:
            gather_gb.relay(j)
        gather_gb.ready(j)
        chip = net.chip ^ (RELS[j] >> 1)
        gm[rows_of(j), :] = dot_nt(gather_gb.block(j), wo[...]).astype(BF)

        def two_tiles(t, carry, chip=chip):
            attend_back(pl.multiple_of((chip * 2 + t) * shard, shard))
            return carry

        lax.fori_loop(0, 2, two_tiles, 0)
    dqkv[:, head : 2 * head] = (dk_acc[...] * scale).astype(BF)
    dqkv[:, 2 * head :] = dv_acc[...].astype(BF)

    for j in (3, 1, 2):
        scatter_three.hop(j)
    scatter_two.left()
    scatter_four = Scatter(net, part_a, hop_a, one.at[3], two.at[3])
    for j in order:
        scatter_four.put(j, dot_nt(dqkv[rows_of(j), :], wq[...]))
    for j in (3, 1, 2):
        scatter_four.hop(j)

    def grad_qkv(z, carry):
        dw_q[z // 2, z % 2] = dot_tn(columns(e1, z), dqkv[...]).astype(BF)
        return carry

    lax.fori_loop(0, 4, grad_qkv, 0)
    sum_q.start()

    def grad_up(z, carry):
        dw_u[z // 2, z % 2] = dot_tn(columns(e2, z), gp[...]).astype(BF)
        return carry

    lax.fori_loop(0, 4, grad_up, 0)
    sum_u.start()

    def grad_o(z, carry):
        dw_o[z // 2, z % 2] = dot_tn(mix_b[...], columns(gb, z)).astype(BF)
        return carry

    lax.fori_loop(0, 4, grad_o, 0)
    sum_o.start()

    small[...] = jnp.zeros_like(small)
    small[0:1, :] = jnp.sum(gp[...].astype(F32), axis=0, keepdims=True)
    small[1:2, :head] = jnp.sum(dqkv[:, :head].astype(F32), axis=0, keepdims=True)
    small[1:2, head : 2 * head] = jnp.sum(dqkv[:, 2 * head :].astype(F32), axis=0, keepdims=True)
    small_site = net.sites(6)
    others = ((1, 0), (0, 2), (1, 2))
    for n, (dy, dz) in enumerate(others):
        net.send(small, small_land.at[n], small_site + n, net.peer(dy=dy, dz=dz))

    def send_out(src, dst, first):
        for z in range(4):
            net.send(
                src.at[:, span(z, quarter)],
                dst.at[span(net.slice, shard), :],
                first + z,
                (y * 2 + zh, z, net.col),
                recv_site=first + 4 + net.slice,
                skip=(row == z) & (k == zh),
            )

    def out_ready(dst, first):
        for s in range(4):
            net.landed(dst.at[span(s, shard), :], first + 4 + s)

    res_site, grad_site = net.sites(8), net.sites(8)
    back_a[...] = (mid[...] + scatter_three.total() + vec[5:6, :]).astype(BF)
    send_out(back_a, res_out, res_site)

    grad = scatter_four.total()
    normed, inv = norm_stats(xs[...].astype(F32))
    tok[0:1, :] = jnp.sum(grad * normed, axis=0, keepdims=True)
    tok[1:2, :] = jnp.sum(grad, axis=0, keepdims=True)
    tok_site = net.sites(10)
    for n in range(1, 8):
        net.send(tok, tok_one.at[n - 1], tok_site + n - 1, net.rel(n))
    spread = grad * vec[0:1, :]
    mean_one = jnp.sum(spread, axis=1, keepdims=True) * (1.0 / width)
    mean_two = jnp.sum(spread * normed, axis=1, keepdims=True) * (1.0 / width)
    back_b[...] = (gmid[...] + inv * (spread - mean_one - normed * mean_two)).astype(BF)
    send_out(back_b, grad_out, grad_site)

    sums = (sum_d, sum_q, sum_u, sum_o)
    for one_sum in sums:
        one_sum.across()
    acc = small[...]
    for n in range(3):
        net.landed(small_land.at[n], small_site + n)
        acc = acc + small_land[n]
    small_sum[...] = acc
    out_small[net.slice] = acc
    for n, (dk, dz) in enumerate(((1, 0), (0, 1), (1, 1))):
        net.send(
            small_sum, out_small.at[net.slice], small_site + 3 + n, net.peer(dk=dk, dz=dz)
        )
    acc = tok[...]
    for n in range(7):
        net.landed(tok_one.at[n], tok_site + n)
        acc = acc + tok_one[n]
    tok_sum[...] = acc
    for n, (dy, dz) in enumerate(others):
        net.send(tok_sum, tok_two.at[n], tok_site + 7 + n, net.peer(dy=dy, dz=dz))
    for one_sum in sums:
        one_sum.hand_out()
    for one_sum in sums:
        one_sum.share()
    for n in range(3):
        net.landed(tok_two.at[n], tok_site + 7 + n)
        acc = acc + tok_two[n]
    out_tok[...] = acc
    for n, flip in enumerate((1, 2, 3)):
        net.landed(out_small.at[net.slice ^ flip], small_site + 3 + n)
    for one_sum in sums:
        one_sum.finish()
    out_ready(res_out, res_site)
    out_ready(grad_out, grad_site)
    net.drain()
    sems.append(net.used)


def layer_on_square(
    inputs, cotangent, seg_parent, token_depth, ln1_gain, ln1_bias, w_qkv, b_qv, w_out, b_out,
    ln2_gain, ln2_bias, w_up, b_up, w_down, b_down,
):
    half_tokens, quarter = inputs.shape
    tokens, width = token_depth.shape[0], 4 * quarter
    shard = tokens // 8
    head = HD
    slices = w_qkv.shape[2] // head
    hidden = w_up.shape[1] // slices
    row = lax.axis_index("row")

    seg_len = tokens // 16
    parent = seg_parent - lax.axis_index("dp") * seg_parent.shape[0]
    seg = jnp.maximum(jnp.arange(16, dtype=jnp.int32) - 3, 0)
    key_seg = jnp.repeat(seg, seg_len)
    ids = jnp.arange(seg_parent.shape[0], dtype=jnp.int32)
    up_one = jnp.sum(jnp.where(seg[:, None] == ids[None, :], parent[None, :], 0), axis=1)
    up_two = jnp.sum(jnp.where(up_one[:, None] == ids[None, :], parent[None, :], 0), axis=1)
    keys = key_seg[None, :]
    allowed = (keys == seg[:, None]) | (keys == up_one[:, None]) | (keys == up_two[:, None])
    table = jnp.where(allowed, token_depth[None, :].astype(F32), -1.0)

    w_q = w_qkv.reshape(quarter, 3, slices, head).transpose(2, 0, 1, 3)
    w_q = w_q.reshape(slices, quarter, 3 * head)
    blank = jnp.zeros_like(ln1_gain)
    vectors = jnp.stack([ln1_gain, ln1_bias, b_out, ln2_gain, ln2_bias, b_down, blank, blank])

    any_ = pl.BlockSpec(memory_space=pl.ANY)
    vmem = pl.BlockSpec(memory_space=pltpu.VMEM)
    sds = jax.ShapeDtypeStruct

    def vm(*dims, dtype=BF):
        return pltpu.VMEM(dims, dtype)

    blocks = {"q": (quarter, 3 * head), "o": (head, quarter), "d": (hidden, quarter), "u": (quarter, hidden)}
    names = ("q", "o", "d", "u")
    scratch = [
        vm(shard, width),
        *[vm(8, shard, width) for _ in range(4)],
        vm(width, 3 * head), vm(head, width), vm(hidden, width), vm(width, hidden),
        vm(16, tokens, dtype=F32), vm(8, width, dtype=F32), vm(16, tokens, dtype=F32),
        *[vm(tokens, head) for _ in range(3)], vm(tokens, tokens),
        vm(tokens, head, dtype=F32), vm(tokens, head),
        vm(8, shard, width), vm(8, shard, width), vm(3, shard, width), vm(3, shard, width),
        vm(4, 4, shard, width), vm(4, 3, shard, width),
        vm(tokens, hidden, dtype=F32), vm(tokens, hidden), vm(tokens, hidden),
        vm(tokens, head), vm(tokens, head, dtype=F32), vm(tokens, head, dtype=F32),
        vm(tokens, 3 * head),
        vm(shard, width, dtype=F32), vm(shard, width, dtype=F32), vm(shard, width), vm(shard, width),
        *[vm(2, 2, *blocks[n]) for n in names],
        *[vm(2, *blocks[n]) for n in names],
        *[vm(*blocks[n]) for n in names],
        *[vm(*blocks[n]) for n in names],
        *[vm(*blocks[n]) for n in names],
        vm(8, width, dtype=F32), vm(7, 8, width, dtype=F32), vm(8, width, dtype=F32),
        vm(3, 8, width, dtype=F32),
        vm(8, hidden, dtype=F32), vm(3, 8, hidden, dtype=F32), vm(8, hidden, dtype=F32),
        pltpu.SemaphoreType.DMA((180,)), pltpu.SemaphoreType.DMA((180,)),
        pltpu.SemaphoreType.DMA((4,)),
    ]
    used = []
    outs = pl.pallas_call(
        functools.partial(layer_kernel, EPS, MASKED, used),
        out_shape=(
            sds((half_tokens, quarter), BF), sds((half_tokens, quarter), BF),
            *[sds((slices, *blocks[n]), BF) for n in names],
            sds((8, width), F32), sds((slices, 8, hidden), F32),
        ),
        in_specs=[any_] * 6 + [vmem] * 4,
        out_specs=(any_,) * 6 + (vmem,) * 2,
        scratch_shapes=scratch,
        compiler_params=pltpu.CompilerParams(
            collective_id=0, has_side_effects=True, vmem_limit_bytes=60 << 20
        ),
        name="tree_layer",
    )(
        inputs, cotangent, w_q, w_out, w_down, w_up, table, vectors,
        b_up.reshape(1, -1), b_qv,
    )
    result, input_grad, g_q, g_o, g_u, g_d, by_token, small = (
        outs[0], outs[1], outs[2], outs[3], outs[5], outs[4], outs[6], outs[7],
    )
    by_token = lax.dynamic_slice_in_dim(by_token, row * quarter, quarter, 1)
    grad_w_qkv = g_q.reshape(slices, quarter, 3, head).transpose(1, 2, 0, 3)
    grad_w_qkv = grad_w_qkv.reshape(quarter, 3, slices * head).astype(F32)
    grad_w_up = g_u.transpose(1, 0, 2).reshape(quarter, slices * hidden).astype(F32)
    grad_b_qv = jnp.stack(
        [small[:, 1, :head].reshape(-1), small[:, 1, head : 2 * head].reshape(-1)]
    )
    return (
        result.astype(F32),
        input_grad.astype(F32),
        by_token[0],
        by_token[1],
        grad_w_qkv,
        grad_b_qv,
        g_o.reshape(slices * head, quarter).astype(F32),
        by_token[4],
        by_token[2],
        by_token[3],
        grad_w_up,
        small[:, 0].reshape(-1),
        g_d.reshape(slices * hidden, quarter).astype(F32),
        by_token[5],
    )


def fits_square(mesh, *arrays):
    sizes = tuple(mesh.shape[name] for name in ("dp", "row", "col"))
    return (
        sizes == (4, 4, 2)
        and arrays[0].shape == (512, 256)
        and arrays[2].shape == (13,)
        and arrays[3].shape == (1024,)
        and arrays[6].shape == (256, 3, 512)
        and arrays[12].shape == (256, 2048)
    )


def solution(mesh):
    placed = (
        P(("dp", "col"), "row"),
        P(("dp", "col"), "row"),
        P("dp"),
        P("dp"),
        P("row"),
        P("row"),
        P("row", None, "col"),
        P(None, "col"),
        P("col", "row"),
        P("row"),
        P("row"),
        P("row"),
        P("row", "col"),
        P("col"),
        P("col", "row"),
        P("row"),
    )

    def on_each(*arrays):
        return (layer_on_square if fits_square(mesh, *arrays) else on_device)(*arrays)

    return jax.shard_map(
        on_each,
        mesh=mesh,
        in_specs=placed,
        out_specs=(
            P(("dp", "col"), "row"),
            P(("dp", "col"), "row"),
            P("row"),
            P("row"),
            P("row", None, "col"),
            P(None, "col"),
            P("col", "row"),
            P("row"),
            P("row"),
            P("row"),
            P("row", "col"),
            P("col"),
            P("col", "row"),
            P("row"),
        ),
        check_vma=False,
    )
```

```python
import functools
import math

import jax
import jax.numpy as jnp
from jax import lax
from jax.experimental import pallas as pl
from jax.experimental.pallas import tpu as pltpu
from jax.sharding import PartitionSpec as P

MESH = pl.DeviceIdType.MESH
BF = jnp.bfloat16
F32 = jnp.float32


HD = 128


EPS = 1e-05
MASKED = -1e30


def gelu_value(values):
    return 0.5 * values * (1.0 + jax.scipy.special.erf(values / math.sqrt(2.0)))


def gelu_slope(values):
    return 0.5 * (1.0 + jax.scipy.special.erf(values / math.sqrt(2.0))) + values * jnp.exp(
        -0.5 * values * values
    ) / math.sqrt(2.0 * math.pi)


def width_sums(first_term, second_term):
    return lax.psum((jnp.sum(first_term, axis=1), jnp.sum(second_term, axis=1)), "row")


def normalize(values, norm_gain, norm_bias, feature_count):
    row_total, square = width_sums(values, values * values)
    row_mean = row_total / feature_count
    inv_std = lax.rsqrt(square / feature_count - row_mean * row_mean + EPS)
    normed = (values - row_mean[:, None]) * inv_std[:, None]
    return (normed, inv_std, (normed * norm_gain + norm_bias).astype(jnp.bfloat16))


def normalize_back(upstream, normed, inv_std, norm_gain, feature_count):
    spread = upstream * norm_gain
    row_total, cross_sum = width_sums(spread, spread * normed)
    return inv_std[:, None] * (
        spread - row_total[:, None] / feature_count - normed * (cross_sum[:, None] / feature_count)
    )


def contract(left_op, right_op, flipped):
    if flipped:
        return lax.dot_general(
            left_op, right_op, (((1,), (1,)), ((), ())), preferred_element_type=jnp.float32
        )
    return jnp.dot(left_op, right_op, preferred_element_type=jnp.float32)


def outer_sum(left_op, right_op):
    return lax.dot_general(
        left_op, right_op, (((0,), (0,)), ((), ())), preferred_element_type=jnp.float32
    )


def across_rows(operand, weight_block, flipped):
    gathered = lax.all_gather(operand, "col", axis=0, tiled=True)
    row_count = gathered.shape[0] // lax.axis_size("row")

    def partial_term(row_start, row_num):
        return contract(gathered, weight_block, flipped)

    return (
        lax.psum_scatter(
            partial_term(jnp.int32(0), row_count * lax.axis_size("row")),
            "row",
            scatter_dimension=0,
            tiled=True,
        ),
        gathered,
    )


def across_cols(operand, weight_block, flipped):
    gathered = lax.all_gather(operand, "row", axis=0, tiled=True)
    row_count = gathered.shape[0] // lax.axis_size("col")

    def partial_term(row_start, row_num):
        return contract(gathered, weight_block, flipped)

    return (
        lax.psum_scatter(
            partial_term(jnp.int32(0), row_count * lax.axis_size("col")),
            "col",
            scatter_dimension=0,
            tiled=True,
        ),
        gathered,
    )


def tree_labels(seg_parent, token_depth):
    seg_count = seg_parent.shape[0]
    tree_len = token_depth.shape[0]
    seg_len = tree_len // 16
    slot_ids = jnp.arange(seg_count, dtype=jnp.int32)
    where_at = jnp.arange(tree_len, dtype=jnp.int32)
    segment = jnp.where(where_at < 4 * seg_len, 0, 1 + (where_at - 4 * seg_len) // seg_len)
    parent_local = seg_parent - lax.axis_index("dp") * seg_count
    parent_one = jnp.sum(
        jnp.where(segment[:, None] == slot_ids[None, :], parent_local[None, :], 0), axis=1
    )
    parent_two = jnp.sum(
        jnp.where(parent_one[:, None] == slot_ids[None, :], parent_local[None, :], 0), axis=1
    )
    return (segment, parent_one, parent_two, token_depth)


def block_scores(query_block, key_rows, labels, query_start, slopes):
    segment, parent_one, parent_two, token_depth = labels
    block_size = query_block.shape[0]
    query_seg = lax.dynamic_slice_in_dim(segment, query_start, block_size, 0)
    query_one = lax.dynamic_slice_in_dim(parent_one, query_start, block_size, 0)
    query_two = lax.dynamic_slice_in_dim(parent_two, query_start, block_size, 0)
    query_depth = lax.dynamic_slice_in_dim(token_depth, query_start, block_size, 0)
    allowed = (
        (segment[None, :] == query_seg[:, None])
        | (segment[None, :] == query_one[:, None])
        | (segment[None, :] == query_two[:, None])
    ) & (token_depth[None, :] <= query_depth[:, None])
    score_scale = query_block.shape[2] ** (-0.5)
    raw = jnp.einsum("qhd,khd->hqk", query_block, key_rows, preferred_element_type=jnp.float32)
    distance = (query_depth[:, None] - token_depth[None, :]).astype(jnp.float32)
    scores = raw * score_scale - slopes[:, None, None] * distance[None]
    return jnp.where(allowed[None], scores, MASKED)


def attention_forward(queries, key_rows, value_rows, labels, slopes, offset):
    block_size = min(512, queries.shape[0])
    blocks = queries.shape[0] // block_size

    def one_block(block_index):
        block_first = block_index * block_size
        query_block = lax.dynamic_slice_in_dim(queries, block_first, block_size, 0)
        scores = block_scores(query_block, key_rows, labels, offset + block_first, slopes)
        top_score = jnp.max(scores, axis=2, keepdims=True)
        weights = jnp.exp(scores - top_score)
        weight_total = jnp.sum(weights, axis=2, keepdims=True)
        probs = (weights / weight_total).astype(jnp.bfloat16)
        mixed = jnp.einsum("hqk,khd->qhd", probs, value_rows, preferred_element_type=jnp.float32)
        return (mixed, (top_score + jnp.log(weight_total))[:, :, 0])

    return lax.map(one_block, jnp.arange(blocks, dtype=jnp.int32))


def attention_backward(
    queries, key_rows, value_rows, grad_mixed, log_total, labels, slopes, offset
):
    block_size = min(512, queries.shape[0])
    blocks = queries.shape[0] // block_size
    score_scale = queries.shape[2] ** (-0.5)

    def one_block(carry, items):
        key_grad, value_grad = carry
        block_index, block_total = items
        block_first = block_index * block_size
        query_block = lax.dynamic_slice_in_dim(queries, block_first, block_size, 0)
        grad_block = lax.dynamic_slice_in_dim(grad_mixed, block_first, block_size, 0)
        scores = block_scores(query_block, key_rows, labels, offset + block_first, slopes)
        probs = jnp.exp(scores - block_total[:, :, None])
        grad_probs = jnp.einsum(
            "qhd,khd->hqk", grad_block, value_rows, preferred_element_type=jnp.float32
        )
        centre = jnp.sum(probs * grad_probs, axis=2, keepdims=True)
        grad_scores = (probs * (grad_probs - centre)).astype(jnp.bfloat16)
        query_grad = (
            jnp.einsum("hqk,khd->qhd", grad_scores, key_rows, preferred_element_type=jnp.float32)
            * score_scale
        )
        key_grad = (
            key_grad
            + jnp.einsum(
                "hqk,qhd->khd", grad_scores, query_block, preferred_element_type=jnp.float32
            )
            * score_scale
        )
        value_grad = value_grad + jnp.einsum(
            "hqk,qhd->khd",
            probs.astype(jnp.bfloat16),
            grad_block,
            preferred_element_type=jnp.float32,
        )
        return ((key_grad, value_grad), query_grad)

    empty = jnp.zeros(key_rows.shape, jnp.float32)
    (key_grad, value_grad), query_grad = lax.scan(
        one_block, (empty, empty), (jnp.arange(blocks, dtype=jnp.int32), log_total)
    )
    return (key_grad, value_grad, query_grad)


def on_device(
    inputs,
    cotangent,
    seg_parent,
    token_depth,
    ln1_gain,
    ln1_bias,
    w_qkv,
    b_qv,
    w_out,
    b_out,
    ln2_gain,
    ln2_bias,
    w_up,
    b_up,
    w_down,
    b_down,
):
    feature_count = inputs.shape[1] * lax.axis_size("row")
    col_width = w_qkv.shape[2]
    heads_here = col_width // HD
    qkv_flat = w_qkv.reshape(w_qkv.shape[0], 3 * col_width)
    labels = tree_labels(seg_parent, token_depth)
    heads_seen = lax.axis_index("col") * heads_here + jnp.arange(heads_here, dtype=jnp.int32)
    slopes = jnp.exp2(-(heads_seen + 1).astype(jnp.float32))
    states = inputs.astype(jnp.float32)
    normed_one, inv_one, entry_one = normalize(states, ln1_gain, ln1_bias, feature_count)
    projected, entry_one_all = across_rows(entry_one, qkv_flat, False)
    tok_rows = projected.shape[0]
    projected = projected.reshape(tok_rows, 3, col_width)
    queries = (projected[:, 0] + b_qv[0]).astype(jnp.bfloat16)
    keys_here = projected[:, 1].astype(jnp.bfloat16)
    values_here = (projected[:, 2] + b_qv[1]).astype(jnp.bfloat16)
    pair_all = lax.all_gather(
        jnp.stack([keys_here, values_here], axis=1), "row", axis=0, tiled=True
    )
    key_rows = pair_all[:, 0].reshape(-1, heads_here, HD)
    value_rows = pair_all[:, 1].reshape(-1, heads_here, HD)
    query_heads = queries.reshape(tok_rows, heads_here, HD)
    offset = lax.axis_index("row") * tok_rows
    mixed, log_total = attention_forward(query_heads, key_rows, value_rows, labels, slopes, offset)
    mixed = mixed.reshape(tok_rows, col_width).astype(jnp.bfloat16)
    attn_out, mixed_all = across_cols(mixed, w_out, False)
    middle = states + attn_out + b_out
    normed_two, inv_two, entry_two = normalize(middle, ln2_gain, ln2_bias, feature_count)
    hidden_pre, entry_two_all = across_rows(entry_two, w_up, False)
    hidden_pre = hidden_pre + b_up
    hidden = gelu_value(hidden_pre).astype(jnp.bfloat16)
    ffn_out, hidden_all = across_cols(hidden, w_down, False)
    result = middle + ffn_out + b_down
    grad_hidden, down_all = across_rows(cotangent, w_down, True)
    grad_pre = (grad_hidden * gelu_slope(hidden_pre)).astype(jnp.bfloat16)
    grad_entry_two, pre_all = across_cols(grad_pre, w_up, True)
    grad_middle = cotangent.astype(jnp.float32) + normalize_back(
        grad_entry_two, normed_two, inv_two, ln2_gain, feature_count
    )
    grad_branch = grad_middle.astype(jnp.bfloat16)
    grad_mixed, branch_all = across_rows(grad_branch, w_out, True)
    grad_mixed = grad_mixed.astype(jnp.bfloat16).reshape(tok_rows, heads_here, HD)
    key_grad, value_grad, query_grad = attention_backward(
        query_heads, key_rows, value_rows, grad_mixed, log_total, labels, slopes, offset
    )
    kv_grads = lax.psum_scatter(
        jnp.stack([key_grad.reshape(-1, col_width), value_grad.reshape(-1, col_width)], axis=1),
        "row",
        scatter_dimension=0,
        tiled=True,
    )
    grad_projected = jnp.stack(
        [
            query_grad.reshape(tok_rows, col_width).astype(jnp.bfloat16),
            kv_grads[:, 0].astype(jnp.bfloat16),
            kv_grads[:, 1].astype(jnp.bfloat16),
        ],
        axis=1,
    )
    grad_entry_one, proj_all = across_cols(
        grad_projected.reshape(tok_rows, 3 * col_width), qkv_flat, True
    )
    input_grad = grad_middle + normalize_back(
        grad_entry_one, normed_one, inv_one, ln1_gain, feature_count
    )
    proj_sums = jnp.sum(proj_all.astype(jnp.float32), axis=0).reshape(3, col_width)
    weight_terms = (
        outer_sum(entry_one_all, proj_all).reshape(w_qkv.shape),
        jnp.stack([proj_sums[0], proj_sums[2]], axis=0),
        outer_sum(mixed_all, branch_all),
        jnp.sum(branch_all.astype(jnp.float32), axis=0),
        outer_sum(entry_two_all, pre_all),
        jnp.sum(pre_all.astype(jnp.float32), axis=0),
        outer_sum(hidden_all, down_all),
        jnp.sum(down_all.astype(jnp.float32), axis=0),
    )
    (
        grad_w_qkv,
        grad_b_qv,
        grad_w_out,
        grad_b_out,
        grad_w_up,
        grad_b_up,
        grad_w_down,
        grad_b_down,
    ) = lax.psum(
        (
            weight_terms[0],
            weight_terms[1],
            weight_terms[2],
            weight_terms[3],
            weight_terms[4],
            weight_terms[5],
            weight_terms[6],
            weight_terms[7],
        ),
        "dp",
    )
    norm_terms = (
        jnp.sum(grad_entry_one * normed_one, axis=0),
        jnp.sum(grad_entry_one, axis=0),
        jnp.sum(grad_entry_two * normed_two, axis=0),
        jnp.sum(grad_entry_two, axis=0),
    )
    grad_ln1_gain, grad_ln1_bias, grad_ln2_gain, grad_ln2_bias = lax.psum(
        (norm_terms[0], norm_terms[1], norm_terms[2], norm_terms[3]), ("dp", "col")
    )
    return (
        result,
        input_grad,
        grad_ln1_gain,
        grad_ln1_bias,
        grad_w_qkv,
        grad_b_qv,
        grad_w_out,
        grad_b_out,
        grad_ln2_gain,
        grad_ln2_bias,
        grad_w_up,
        grad_b_up,
        grad_w_down,
        grad_b_down,
    )


RELS = (0, 4, 2, 6)


def dot_nn(a, b):
    return lax.dot_general(a, b, (((1,), (0,)), ((), ())), preferred_element_type=F32)


def dot_nt(a, b):
    return lax.dot_general(a, b, (((1,), (1,)), ((), ())), preferred_element_type=F32)


def dot_tn(a, b):
    return lax.dot_general(a, b, (((0,), (0,)), ((), ())), preferred_element_type=F32)


def span(index, size):
    return pl.ds(pl.multiple_of(index * size, size), size)


class Net:
    def __init__(self, ssem, rsem):
        self.dp = lax.axis_index("dp")
        self.row = lax.axis_index("row")
        self.col = lax.axis_index("col")
        self.y, self.k = self.dp // 2, self.dp % 2
        self.zh, self.zl = self.row // 2, self.row % 2
        self.x = self.col
        self.slot = self.x * 4 + self.zl * 2 + self.k
        self.chip = self.x * 2 + self.zl
        self.slice = self.zl * 2 + self.k
        self.ssem, self.rsem = ssem, rsem
        self.used = 0
        self.pending = []

    def sites(self, n):
        first = self.used
        self.used += n
        return first

    def peer(self, dy=0, dk=0, dz=0, dx=0):
        return (
            (self.y ^ dy) * 2 + (self.k ^ dk),
            self.row ^ dz,
            self.col ^ dx,
        )

    def rel(self, rel):
        return self.peer(dz=(rel >> 1) & 1, dx=rel >> 2, dk=rel & 1)

    def make(self, src, dst, site, device, recv_site=None):
        recv = site if recv_site is None else recv_site
        return pltpu.make_async_remote_copy(
            src_ref=src,
            dst_ref=dst,
            send_sem=self.ssem.at[site],
            recv_sem=self.rsem.at[recv],
            device_id=device,
            device_id_type=MESH,
        )

    def send(self, src, dst, site, device, recv_site=None, skip=None):
        remote = self.make(src, dst, site, device, recv_site)
        if skip is None:
            remote.start()
        else:
            recv = site if recv_site is None else recv_site

            @pl.when(skip)
            def _():
                pltpu.make_async_copy(src, dst, self.rsem.at[recv]).start()

            @pl.when(jnp.logical_not(skip))
            def _():
                remote.start()

        self.pending.append((remote, skip))
        return remote

    def landed(self, ref, site):
        self.make(ref, ref, site, self.peer(dk=1)).wait_recv()

    def drain(self, upto=None):
        for remote, skip in self.pending:
            if skip is None:
                remote.wait_send()
            else:

                @pl.when(jnp.logical_not(skip))
                def _(remote=remote):
                    remote.wait_send()

        self.pending = []


class Gather:
    def __init__(self, net, buf, by_low, over_y=False):
        self.net, self.buf, self.over_y = net, buf, over_y
        self.slot = net.x * 4 + net.y * 2 + net.k if over_y else net.slot
        self.first = net.sites(8)
        rows = buf.shape[1]
        self.low_rows = pl.ds(0, by_low) if by_low else None
        self.x_rows = pl.ds(by_low, rows - by_low) if by_low < rows else None

    def to(self, rel):
        low = (rel >> 1) & 1
        where = {"dy": low} if self.over_y else {"dz": low}
        return self.net.peer(dk=rel & 1, dx=rel >> 2, **where)

    def start(self):
        own = self.buf.at[self.slot]
        for n, rel in enumerate((1, 4, 2)):
            self.net.send(own, own, self.first + n, self.to(rel))

    def relay(self, j):
        net = self.net
        part = self.buf.at[self.slot ^ RELS[j]]
        if j < 3:
            net.landed(part, self.first + j)
            rows, rel = ((self.low_rows, 2), (self.x_rows, 4))[j - 1]
            if rows is not None:
                some = part.at[rows, :]
                net.send(some, some, self.first + 2 + j, self.to(rel))
        else:
            for n, rows in enumerate((self.low_rows, self.x_rows)):
                if rows is not None:
                    net.landed(part.at[rows, :], self.first + 3 + n)
        net.send(part, part, self.first + 4 + j, self.to(1))

    def ready(self, j):
        part = self.buf.at[self.slot ^ RELS[j] ^ 1]
        self.net.landed(part, self.first if j == 0 else self.first + 4 + j)

    def block(self, j):
        chip = (self.slot ^ RELS[j]) // 2
        both = self.buf[pl.ds(chip * 2, 2)]
        return both.reshape(2 * both.shape[1], both.shape[2])


class Exchange:
    def __init__(self, net, src_of, dst_of):
        self.net, self.src_of, self.dst_of = net, src_of, dst_of
        self.first = net.sites(7)

    def start(self):
        net = self.net
        for n in (6, 7, 4, 5, 2, 3, 1):
            net.send(
                self.src_of(net.slot ^ n), self.dst_of(net.slot), self.first + n - 1, net.rel(n)
            )

    def ready(self):
        net = self.net
        for n in range(1, 8):
            net.landed(self.dst_of(net.slot ^ n), self.first + n - 1)


class Scatter:
    def __init__(self, net, bufs, land):
        self.net = net
        self.part, self.hops, self.kept, self.last = bufs
        self.one, self.two, self.three = land
        self.first = net.sites(10)
        self.sent = []

    def send(self, src, dst, site, rel):
        self.sent.append(self.net.send(src, dst, self.first + site, self.net.rel(rel)))

    def put(self, j, value):
        net = self.net
        chip = net.chip ^ (RELS[j] >> 1)
        shard = self.part.shape[1]
        self.part[pl.ds(chip * 2, 2)] = value.astype(BF).reshape(2, shard, value.shape[1])
        self.send(self.part.at[chip * 2 + (1 - net.k)], self.one.at[j], j, 1)

    def chip_sum(self, j):
        net = self.net
        chip = net.chip ^ (RELS[j] >> 1)
        net.landed(self.one.at[j], self.first + j)
        return self.part[chip * 2 + net.k].astype(F32) + self.one[j].astype(F32)

    def hop(self, j):
        half = self.part.shape[1] // 2
        value = self.chip_sum(j)
        if j == 2:
            self.kept[0] = value[:half]
        else:
            n = 0 if j == 1 else 1
            self.hops[n] = value[:half].astype(BF)
            self.send(self.hops.at[n], self.two.at[n], 4 + n, 4)
        if j == 1:
            self.kept[1] = value[half:]
        else:
            n = 2 if j == 2 else 3
            self.hops[n] = value[half:].astype(BF)
            self.send(self.hops.at[n], self.two.at[n], 4 + n, 2)

    def hop_on(self):
        net = self.net
        for n, rel in enumerate((2, 4)):
            net.landed(self.two.at[1 + 2 * n], self.first + 5 + 2 * n)
            self.last[n] = (self.kept[n] + self.two[1 + 2 * n].astype(F32)).astype(BF)
            self.send(self.last.at[n], self.three.at[n], 8 + n, rel)

    def left(self):
        for remote in self.sent:
            remote.wait_send()
        mine = {id(remote) for remote in self.sent}
        self.net.pending = [p for p in self.net.pending if id(p[0]) not in mine]

    def total(self):
        net = self.net
        value = self.chip_sum(0)
        half = value.shape[0] // 2
        parts = []
        for n in (0, 1):
            net.landed(self.two.at[2 * n], self.first + 4 + 2 * n)
            net.landed(self.three.at[n], self.first + 8 + n)
            parts.append(
                value[n * half : (n + 1) * half]
                + self.two[2 * n].astype(F32)
                + self.three[n].astype(F32)
            )
        return jnp.concatenate(parts, axis=0)


class TreeSum:
    def __init__(self, net, own, land_y, hop, land_z, done, out, local_sem):
        self.net, self.own, self.land_y = net, own, land_y
        self.hop_buf, self.land_z, self.done, self.out = hop, land_z, done, out
        self.first = net.sites(7)
        self.local_sem = local_sem

    def put(self, z, value):
        rows = self.own.shape[3]
        self.own[z // 2, z % 2] = value.astype(BF).reshape(2, rows, value.shape[1])

    def half(self, piece, which):
        return self.out.at[piece, span(which, self.own.shape[3]), :]

    def start(self):
        net = self.net
        net.send(self.own.at[:, :, 1 - net.y], self.land_y, self.first, net.peer(dy=1))

    def across(self):
        net = self.net
        net.landed(self.land_y, self.first)
        far = 1 - net.zh
        for low in (0, 1):
            self.hop_buf[low] = (
                self.own[far, low, net.y].astype(F32) + self.land_y[far, low].astype(F32)
            ).astype(BF)
        net.send(self.hop_buf, self.land_z, self.first + 1, net.peer(dz=2))

    def hand_out(self):
        net = self.net
        net.landed(self.land_z, self.first + 1)
        for low in (0, 1):
            self.done[low] = (
                self.own[net.zh, low, net.y].astype(F32)
                + self.land_y[net.zh, low].astype(F32)
                + self.land_z[low].astype(F32)
            ).astype(BF)
        place = self.half(net.slice, net.y)
        net.send(self.done.at[1 - net.zl], place, self.first + 2, net.peer(dz=1))
        net.send(self.done.at[net.zl], place, self.first + 3, net.peer(dy=1))
        self.kept = pltpu.make_async_copy(self.done.at[net.zl], place, self.local_sem)
        self.kept.start()

    def pass_on(self):
        net = self.net
        part = self.half(net.slice ^ 2, net.y)
        net.landed(part, self.first + 2)
        net.send(part, part, self.first + 4, net.peer(dy=1))

    def share(self):
        net = self.net
        self.kept.wait()
        for n, piece in enumerate((net.slice, net.slice ^ 2)):
            net.landed(self.half(piece, 1 - net.y), self.first + 3 + n)
            part = self.out.at[piece]
            net.send(part, part, self.first + 5 + n, net.rel(1))

    def finish(self):
        net = self.net
        for n, piece in enumerate((net.slice ^ 1, net.slice ^ 3)):
            net.landed(self.out.at[piece], self.first + 5 + n)


def layer_kernel(eps, masked, sems, *refs):
    (
        inp, cot, w_q, w_o, w_d, w_u, tab, vec_in, b_up, b_qv,
        res_out, grad_out, out_q, out_o, out_d, out_u, out_tok, out_small,
        xs, e1, g, e2, gb, wf, wq, wd, wu, mixed_all, grad_all, tab_far, vec, bias,
        q_buf, k_buf, v_buf, p_buf, mix, mix_b,
        part_a, hops_a, kept_a, last_a, part_b, hops_b, kept_b, last_b, one, two, three,
        gh, hid, gp, gm, dk_acc, dv_acc, dqkv, mid, gmid, back_a, back_b,
        dw_q, dw_o, dw_d, dw_u, ly_q, ly_o, ly_d, ly_u,
        yh_q, yh_o, yh_d, yh_u, lz_q, lz_o, lz_d, lz_u,
        fin_q, fin_o, fin_d, fin_u,
        tok, tok_one, tok_sum, tok_two, small, small_land, small_sum,
        ssem, rsem, lsem,
    ) = refs
    net = Net(ssem, rsem)
    y, k, zh, zl, x, row = net.y, net.k, net.zh, net.zl, net.x, net.row
    shard, width = xs.shape
    tokens = 8 * shard
    quarter = width // 4
    head = q_buf.shape[1]

    greet = [
        net.peer(dy=dy, dk=dk, dz=dz)
        for dy in (0, 1)
        for dk in (0, 1)
        for dz in (0, 1, 2, 3)
        if dy + dk + dz
    ]
    greet += [net.peer(dk=dk, dz=dz, dx=1) for dk in (0, 1) for dz in (0, 1)]
    barrier = pltpu.get_barrier_semaphore()
    for device in greet:
        pl.semaphore_signal(barrier, inc=1, device_id=device, device_id_type=MESH)
    pl.semaphore_wait(barrier, len(greet))

    def send_home(src, dst_of, first):
        for s in range(4):
            low, core = s // 2, s % 2
            target = 2 * k + low
            net.send(
                src.at[span(s, shard), :],
                dst_of(s).at[:, span(row, quarter)],
                first + s,
                (y * 2 + core, target, net.col),
                recv_site=first + 4 + row,
                skip=(target == row) & (k == core),
            )

    def home_ready(dst, first):
        for z in range(4):
            net.landed(dst.at[:, span(z, quarter)], first + 4 + z)

    vec_site = net.sites(3)
    for o in (1, 2, 3):
        net.send(vec_in, vec.at[:, span(row, quarter)], vec_site + o - 1, net.peer(dz=o))
    home_x, home_g = net.sites(8), net.sites(8)
    send_home(inp, lambda s: xs, home_x)
    tab_site = net.sites(1)
    net.send(tab, tab_far, tab_site, net.rel(1))

    def slices(w_ref, full, axis):
        if axis == 0:
            rows = full.shape[0] // 4
            return rows, lambda z: full.at[span(z, rows), :]
        cols = full.shape[1] // 4
        return full.shape[0], lambda z: full.at[:, span(z, cols)]

    class Weight:
        def __init__(self, src_of, full, axis, local):
            self.src_of, self.full = src_of, full
            self.rows, self.place = slices(None, full, axis)
            self.first = net.sites(6)
            self.local = local

        def half(self, ref, which):
            rows = self.rows // 2
            return ref.at[span(which, rows), :]

        def start(self):
            own = pltpu.make_async_copy(
                self.src_of(net.slice), self.place(row), lsem.at[self.local]
            )
            own.start()
            for o in (1, 2, 3):
                far = (zl ^ (o & 1)) * 2 + k
                net.send(
                    self.half(self.src_of(far), y),
                    self.half(self.place(row), y),
                    self.first + o - 1,
                    net.peer(dz=o),
                )
            self.own = own

        def relay(self):
            for o in (1, 2, 3):
                part = self.half(self.place(row ^ o), y)
                net.landed(part, self.first + o - 1)
                net.send(part, part, self.first + 2 + o, net.peer(dy=1))

        def ready(self):
            for o in (1, 2, 3):
                net.landed(self.half(self.place(row ^ o), 1 - y), self.first + 2 + o)
            self.own.wait()

    hidden = hid.shape[1]
    weight_q = Weight(lambda s: w_q.at[s], wq, 0, 0)
    weight_d = Weight(lambda s: w_d.at[span(s, hidden), :], wd, 1, 2)
    weight_u = Weight(lambda s: w_u.at[:, span(s, hidden)], wu, 0, 3)
    weight_q.start()

    gather_w = Gather(net, wf, shard // 2, over_y=True)
    wf_own = wf.at[gather_w.slot]
    wf_site = net.sites(3)
    wf_src = w_o.at[span(y * 2 + k, shard), :]
    wf_copy = pltpu.make_async_copy(wf_src, wf_own.at[:, span(row, quarter)], lsem.at[1])
    wf_copy.start()
    for o in (1, 2, 3):
        net.send(wf_src, wf_own.at[:, span(row, quarter)], wf_site + o - 1, net.peer(dz=o))

    vec[:, span(row, quarter)] = vec_in[...]
    for o in (1, 2, 3):
        net.landed(vec.at[:, span(row ^ o, quarter)], vec_site + o - 1)

    def norm_stats(values):
        mean = jnp.sum(values, axis=1, keepdims=True) * (1.0 / width)
        msq = jnp.sum(values * values, axis=1, keepdims=True) * (1.0 / width)
        inv = lax.rsqrt(msq - mean * mean + eps)
        return (values - mean) * inv, inv

    home_ready(xs, home_x)
    normed, _ = norm_stats(xs[...].astype(F32))
    e1[net.slot] = (normed * vec[0:1, :] + vec[1:2, :]).astype(BF)
    gather_e1 = Gather(net, e1, 0)
    gather_e1.start()
    gather_g = Gather(net, g, 0)
    send_home(cot, lambda s: g.at[x * 4 + s], home_g)
    weight_u.start()
    weight_d.start()
    weight_q.relay()

    net.landed(tab_far, tab_site)
    table = jnp.where(zh == k, tab[...], tab_far[...])
    exponent = jnp.full((1, tokens), -(x * 4 + net.slice + 1), jnp.int32).astype(F32)
    slope = jnp.exp2(exponent)
    bias[...] = jnp.where(table >= 0.0, slope * table, masked)

    b_q = b_qv[0:1, span(net.slice, head)]
    b_v = b_qv[1:2, span(net.slice, head)]
    gather_e1.relay(1)
    gather_e1.relay(2)
    weight_q.ready()
    for j in range(4):
        if j == 3:
            for o in (1, 2, 3):
                net.landed(wf_own.at[:, span(row ^ o, quarter)], wf_site + o - 1)
            wf_copy.wait()
            gather_w.start()
            gather_e1.relay(3)
        gather_e1.ready(j)
        rows = pl.ds((net.chip ^ (RELS[j] >> 1)) * 2 * shard, 2 * shard)
        proj = dot_nn(gather_e1.block(j), wq[...])
        q_buf[rows, :] = (proj[:, :head] + b_q).astype(BF)
        k_buf[rows, :] = proj[:, head : 2 * head].astype(BF)
        v_buf[rows, :] = (proj[:, 2 * head :] + b_v).astype(BF)

    scale = head ** (-0.5)
    seg_len = tokens // 16
    key_at = lax.broadcasted_iota(jnp.int32, (1, tokens), 1)
    key_half = key_at // seg_len
    key_seg = jnp.maximum(key_half - 3, 0)

    def attend(i, carry):
        first = pl.multiple_of(i * shard, shard)
        raw = dot_nt(q_buf[pl.ds(first, shard), :], k_buf[...])
        parts = []
        for half in (0, 1):
            at = 2 * i + half
            seg = jnp.maximum(at - 3, 0)
            later = jnp.where(key_seg == seg, key_at, -1)
            query_at = first + half * seg_len + lax.broadcasted_iota(jnp.int32, (seg_len, 1), 0)
            scores = raw[half * seg_len : (half + 1) * seg_len] * scale + bias[pl.ds(at, 1), :]
            scores = jnp.where(later > query_at, masked, scores)
            top = jnp.max(scores, axis=1, keepdims=True)
            weights = jnp.exp(scores - top)
            norm = 1.0 / jnp.sum(weights, axis=1, keepdims=True)
            parts.append((weights * norm).astype(BF))
        probs = jnp.concatenate(parts, axis=0)
        p_buf[pl.ds(first, shard), :] = probs
        mixed = dot_nn(probs, v_buf[...])
        mix[pl.ds(first, shard), :] = mixed
        mix_b[pl.ds(first, shard), :] = mixed.astype(BF)
        return carry

    lax.fori_loop(0, 6, attend, 0)
    gather_w.relay(1)
    gather_w.relay(2)
    lax.fori_loop(6, 8, attend, 0)

    def rows_of(j):
        return span(net.chip ^ (RELS[j] >> 1), 2 * shard)

    order = (3, 1, 2, 0)
    part_set_a = (part_a, hops_a, kept_a, last_a)
    part_set_b = (part_b, hops_b, kept_b, last_b)

    def landings(n):
        return (one.at[n], two.at[n], three.at[n])

    swap = Exchange(
        net, lambda q: mix_b.at[span(q, shard), :], lambda h: mixed_all.at[:, span(h, head)]
    )
    swap.start()
    mixed_all[:, span(net.slot, head)] = mix_b[span(net.slot, shard), :]
    home_ready(g.at[net.slot], home_g)
    gather_g.start()
    gather_w.relay(3)
    weight_u.relay()
    for j in range(4):
        gather_w.ready(j)
    swap.ready()
    w_out = wf[...].reshape(width, width)

    middle = xs[...].astype(F32) + dot_nn(mixed_all[...], w_out) + vec[2:3, :]
    mid[...] = middle
    normed, _ = norm_stats(middle)
    e2[net.slot] = (normed * vec[3:4, :] + vec[4:5, :]).astype(BF)
    gather_e2 = Gather(net, e2, shard // 2)
    gather_e2.start()
    weight_d.relay()
    gather_g.relay(1)
    gather_g.relay(2)
    gather_e2.relay(1)
    gather_e2.relay(2)
    gather_g.relay(3)
    weight_d.ready()
    for j in range(4):
        gather_g.ready(j)

    def hidden_grad(c, carry):
        rows = span(c, 2 * shard)
        both = g[pl.ds(c * 2, 2)].reshape(2 * shard, width)
        gh[rows, :] = dot_nt(both, wd[...])
        return carry

    lax.fori_loop(0, 4, hidden_grad, 0)

    b_u = b_up[0:1, span(net.slice, hidden)]
    weight_u.ready()
    scatter_two = Scatter(net, part_set_a, landings(0))
    for j in range(4):
        if j == 3:
            gather_e2.relay(3)
        gather_e2.ready(j)
        pre = dot_nn(gather_e2.block(j), wu[...]) + b_u
        bell = 0.5 * (1.0 + lax.erf(pre * (1.0 / math.sqrt(2.0))))
        hid[rows_of(j), :] = (pre * bell).astype(BF)
        rise = bell + pre * jnp.exp(-0.5 * pre * pre) * (1.0 / math.sqrt(2.0 * math.pi))
        gp[rows_of(j), :] = (gh[rows_of(j), :] * rise).astype(BF)
        scatter_two.put(j, dot_nt(gp[rows_of(j), :], wu[...]))
        if j == 2:
            scatter_two.hop(1)
    scatter_two.hop(2)
    scatter_two.hop(3)

    sum_d = TreeSum(net, dw_d, ly_d, yh_d, lz_d, fin_d, out_d, lsem.at[4])
    sum_u = TreeSum(net, dw_u, ly_u, yh_u, lz_u, fin_u, out_u, lsem.at[5])
    sum_o = TreeSum(net, dw_o, ly_o, yh_o, lz_o, fin_o, out_o, lsem.at[6])
    sum_q = TreeSum(net, dw_q, ly_q, yh_q, lz_q, fin_q, out_q, lsem.at[7])

    def columns(buf, z):
        part = buf[:, :, span(z, quarter)]
        return part.reshape(tokens, quarter)

    def grad_down(z, carry):
        sum_d.put(z, dot_tn(hid[...], columns(g, z)))
        return carry

    lax.fori_loop(0, 4, grad_down, 0)
    sum_d.start()
    scatter_two.hop_on()

    def grad_up(z, carry):
        sum_u.put(z, dot_tn(columns(e2, z), gp[...]))
        return carry

    lax.fori_loop(0, 4, grad_up, 0)
    sum_u.start()

    grad = scatter_two.total()
    middle = mid[...]
    normed, inv = norm_stats(middle)
    tok[2:3, :] = jnp.sum(grad * normed, axis=0, keepdims=True)
    tok[3:4, :] = jnp.sum(grad, axis=0, keepdims=True)
    spread = grad * vec[3:4, :]
    mean_one = jnp.sum(spread, axis=1, keepdims=True) * (1.0 / width)
    mean_two = jnp.sum(spread * normed, axis=1, keepdims=True) * (1.0 / width)
    cot_own = g[net.slot].astype(F32)
    tok[5:6, :] = jnp.sum(cot_own, axis=0, keepdims=True)
    total = cot_own + inv * (spread - mean_one - normed * mean_two)
    gmid[...] = total
    branch = total.astype(BF)
    gb[net.slot] = branch
    tok[4:5, :] = jnp.sum(branch.astype(F32), axis=0, keepdims=True)
    tok[6:8, :] = jnp.zeros((2, width), F32)
    grad_all[...] = dot_nt(branch, w_out).astype(BF)
    swap_back = Exchange(
        net, lambda h: grad_all.at[:, span(h, head)], lambda q: gm.at[span(q, shard), :]
    )
    swap_back.start()
    gm[span(net.slot, shard), :] = grad_all[:, span(net.slot, head)]
    gather_gb = Gather(net, gb, shard // 2)
    gather_gb.start()

    dk_acc[...] = jnp.zeros_like(dk_acc)
    dv_acc[...] = jnp.zeros_like(dv_acc)

    def attend_back(first):
        rows = pl.ds(first, shard)
        grad_mix = gm[rows, :]
        probs = p_buf[rows, :]
        grad_probs = dot_nt(grad_mix, v_buf[...])
        centre = jnp.sum(mix[rows, :] * grad_mix.astype(F32), axis=1, keepdims=True)
        grad_scores = (probs.astype(F32) * (grad_probs - centre)).astype(BF)
        dqkv[rows, :head] = (dot_nn(grad_scores, k_buf[...]) * scale).astype(BF)
        dk_acc[...] += dot_tn(grad_scores, q_buf[rows, :])
        dv_acc[...] += dot_tn(probs, grad_mix)

    swap_back.ready()

    def tile_back(t, carry):
        attend_back(pl.multiple_of(t * shard, shard))
        return carry

    lax.fori_loop(0, 5, tile_back, 0)
    gather_gb.relay(1)
    gather_gb.relay(2)
    lax.fori_loop(5, 8, tile_back, 0)
    dqkv[:, head : 2 * head] = (dk_acc[...] * scale).astype(BF)
    dqkv[:, 2 * head :] = dv_acc[...].astype(BF)

    scatter_four = Scatter(net, part_set_a, landings(1))
    scatter_two.left()
    for j in order:
        scatter_four.put(j, dot_nt(dqkv[rows_of(j), :], wq[...]))
    for j in (3, 1, 2):
        scatter_four.hop(j)
    sum_d.across()

    def grad_qkv(z, carry):
        sum_q.put(z, dot_tn(columns(e1, z), dqkv[...]))
        return carry

    lax.fori_loop(0, 4, grad_qkv, 0)
    sum_q.start()
    scatter_four.hop_on()
    sum_u.across()

    small[...] = jnp.zeros_like(small)
    small[0:1, :] = jnp.sum(gp[...].astype(F32), axis=0, keepdims=True)
    small[1:2, :head] = jnp.sum(dqkv[:, :head].astype(F32), axis=0, keepdims=True)
    small[1:2, head : 2 * head] = jnp.sum(dqkv[:, 2 * head :].astype(F32), axis=0, keepdims=True)
    small_site = net.sites(6)
    others = ((1, 0), (0, 2), (1, 2))
    for n, (dy, dz) in enumerate(others):
        net.send(small, small_land.at[n], small_site + n, net.peer(dy=dy, dz=dz))

    def send_out(src, dst, first):
        for z in range(4):
            net.send(
                src.at[:, span(z, quarter)],
                dst.at[span(net.slice, shard), :],
                first + z,
                (y * 2 + zh, z, net.col),
                recv_site=first + 4 + net.slice,
                skip=(row == z) & (k == zh),
            )

    def out_ready(dst, first):
        for s in range(4):
            net.landed(dst.at[span(s, shard), :], first + 4 + s)

    res_site, grad_site = net.sites(8), net.sites(8)
    grad = scatter_four.total()
    normed, inv = norm_stats(xs[...].astype(F32))
    tok[0:1, :] = jnp.sum(grad * normed, axis=0, keepdims=True)
    tok[1:2, :] = jnp.sum(grad, axis=0, keepdims=True)
    tok_site = net.sites(10)
    for n in range(1, 8):
        net.send(tok, tok_one.at[n - 1], tok_site + n - 1, net.rel(n))
    spread = grad * vec[0:1, :]
    mean_one = jnp.sum(spread, axis=1, keepdims=True) * (1.0 / width)
    mean_two = jnp.sum(spread * normed, axis=1, keepdims=True) * (1.0 / width)
    back_b[...] = (gmid[...] + inv * (spread - mean_one - normed * mean_two)).astype(BF)
    send_out(back_b, grad_out, grad_site)

    sum_d.hand_out()
    sum_q.across()
    gather_gb.relay(3)
    for j in range(4):
        gather_gb.ready(j)

    def grad_o(z, carry):
        sum_o.put(z, dot_tn(mix_b[...], columns(gb, z)))
        return carry

    lax.fori_loop(0, 4, grad_o, 0)
    sum_o.start()
    scatter_three = Scatter(net, part_set_b, landings(2))
    for j in order:
        scatter_three.put(j, dot_nn(hid[rows_of(j), :], wd[...]))
    for j in (3, 1, 2):
        scatter_three.hop(j)
    sum_u.hand_out()
    sum_d.pass_on()
    sum_o.across()
    scatter_three.hop_on()
    sum_q.hand_out()
    sum_u.pass_on()
    sum_d.share()
    acc = small[...]
    for n in range(3):
        net.landed(small_land.at[n], small_site + n)
        acc = acc + small_land[n]
    small_sum[...] = acc
    out_small[net.slice] = acc
    for n, (dk, dz) in enumerate(((1, 0), (0, 1), (1, 1))):
        net.send(
            small_sum, out_small.at[net.slice], small_site + 3 + n, net.peer(dk=dk, dz=dz)
        )
    acc = tok[...]
    for n in range(7):
        net.landed(tok_one.at[n], tok_site + n)
        acc = acc + tok_one[n]
    tok_sum[...] = acc
    for n, (dy, dz) in enumerate(others):
        net.send(tok_sum, tok_two.at[n], tok_site + 7 + n, net.peer(dy=dy, dz=dz))
    sum_o.hand_out()
    sum_q.pass_on()
    sum_u.share()
    sum_o.pass_on()
    back_a[...] = (mid[...] + scatter_three.total() + vec[5:6, :]).astype(BF)
    send_out(back_a, res_out, res_site)
    sum_q.share()
    sum_o.share()
    for n in range(3):
        net.landed(tok_two.at[n], tok_site + 7 + n)
        acc = acc + tok_two[n]
    out_tok[...] = acc
    for n, flip in enumerate((1, 2, 3)):
        net.landed(out_small.at[net.slice ^ flip], small_site + 3 + n)
    for one_sum in (sum_d, sum_u, sum_q, sum_o):
        one_sum.finish()
    out_ready(res_out, res_site)
    out_ready(grad_out, grad_site)
    net.drain()
    sems.append(net.used)


def layer_on_square(
    inputs, cotangent, seg_parent, token_depth, ln1_gain, ln1_bias, w_qkv, b_qv, w_out, b_out,
    ln2_gain, ln2_bias, w_up, b_up, w_down, b_down,
):
    half_tokens, quarter = inputs.shape
    tokens, width = token_depth.shape[0], 4 * quarter
    shard = tokens // 8
    head = HD
    slices = w_qkv.shape[2] // head
    hidden = w_up.shape[1] // slices
    row = lax.axis_index("row")

    seg_len = tokens // 16
    parent = seg_parent - lax.axis_index("dp") * seg_parent.shape[0]
    seg = jnp.maximum(jnp.arange(16, dtype=jnp.int32) - 3, 0)
    key_seg = jnp.repeat(seg, seg_len)
    ids = jnp.arange(seg_parent.shape[0], dtype=jnp.int32)
    up_one = jnp.sum(jnp.where(seg[:, None] == ids[None, :], parent[None, :], 0), axis=1)
    up_two = jnp.sum(jnp.where(up_one[:, None] == ids[None, :], parent[None, :], 0), axis=1)
    keys = key_seg[None, :]
    allowed = (keys == seg[:, None]) | (keys == up_one[:, None]) | (keys == up_two[:, None])
    table = jnp.where(allowed, token_depth[None, :].astype(F32), -1.0)

    w_q = w_qkv.reshape(quarter, 3, slices, head).transpose(2, 0, 1, 3)
    w_q = w_q.reshape(slices, quarter, 3 * head)
    blank = jnp.zeros_like(ln1_gain)
    vectors = jnp.stack([ln1_gain, ln1_bias, b_out, ln2_gain, ln2_bias, b_down, blank, blank])

    any_ = pl.BlockSpec(memory_space=pl.ANY)
    vmem = pl.BlockSpec(memory_space=pltpu.VMEM)
    sds = jax.ShapeDtypeStruct

    def vm(*dims, dtype=BF):
        return pltpu.VMEM(dims, dtype)

    blocks = {"q": (quarter, 3 * head), "o": (head, quarter), "d": (hidden, quarter), "u": (quarter, hidden)}
    names = ("q", "o", "d", "u")
    halves = {n: (blocks[n][0] // 2, blocks[n][1]) for n in names}
    scratch = [
        vm(shard, width),
        *[vm(8, shard, width) for _ in range(5)],
        vm(width, 3 * head), vm(hidden, width), vm(width, hidden),
        vm(shard, width), vm(shard, width),
        vm(16, tokens, dtype=F32), vm(8, width, dtype=F32), vm(16, tokens, dtype=F32),
        *[vm(tokens, head) for _ in range(3)], vm(tokens, tokens),
        vm(tokens, head, dtype=F32), vm(tokens, head),
        *[
            spec
            for _ in range(2)
            for spec in (
                vm(8, shard, width), vm(4, shard // 2, width),
                vm(2, shard // 2, width, dtype=F32), vm(2, shard // 2, width),
            )
        ],
        vm(3, 4, shard, width), vm(3, 4, shard // 2, width), vm(3, 2, shard // 2, width),
        vm(tokens, hidden, dtype=F32), vm(tokens, hidden), vm(tokens, hidden),
        vm(tokens, head), vm(tokens, head, dtype=F32), vm(tokens, head, dtype=F32),
        vm(tokens, 3 * head),
        vm(shard, width, dtype=F32), vm(shard, width, dtype=F32), vm(shard, width), vm(shard, width),
        *[vm(2, 2, 2, *halves[n]) for n in names],
        *[vm(2, 2, *halves[n]) for n in names],
        *[vm(2, *halves[n]) for n in names],
        *[vm(2, *halves[n]) for n in names],
        *[vm(2, *halves[n]) for n in names],
        vm(8, width, dtype=F32), vm(7, 8, width, dtype=F32), vm(8, width, dtype=F32),
        vm(3, 8, width, dtype=F32),
        vm(8, hidden, dtype=F32), vm(3, 8, hidden, dtype=F32), vm(8, hidden, dtype=F32),
        pltpu.SemaphoreType.DMA((200,)), pltpu.SemaphoreType.DMA((200,)),
        pltpu.SemaphoreType.DMA((8,)),
    ]
    used = []
    outs = pl.pallas_call(
        functools.partial(layer_kernel, EPS, MASKED, used),
        out_shape=(
            sds((half_tokens, quarter), BF), sds((half_tokens, quarter), BF),
            *[sds((slices, *blocks[n]), BF) for n in names],
            sds((8, width), F32), sds((slices, 8, hidden), F32),
        ),
        in_specs=[any_] * 6 + [vmem] * 4,
        out_specs=(any_,) * 6 + (vmem,) * 2,
        scratch_shapes=scratch,
        compiler_params=pltpu.CompilerParams(
            collective_id=0, has_side_effects=True, vmem_limit_bytes=60 << 20
        ),
        name="tree_layer",
    )(
        inputs, cotangent, w_q, w_out, w_down, w_up, table, vectors,
        b_up.reshape(1, -1), b_qv,
    )
    result, input_grad, g_q, g_o, g_u, g_d, by_token, small = (
        outs[0], outs[1], outs[2], outs[3], outs[5], outs[4], outs[6], outs[7],
    )
    by_token = lax.dynamic_slice_in_dim(by_token, row * quarter, quarter, 1)
    grad_w_qkv = g_q.reshape(slices, quarter, 3, head).transpose(1, 2, 0, 3)
    grad_w_qkv = grad_w_qkv.reshape(quarter, 3, slices * head).astype(F32)
    grad_w_up = g_u.transpose(1, 0, 2).reshape(quarter, slices * hidden).astype(F32)
    grad_b_qv = jnp.stack(
        [small[:, 1, :head].reshape(-1), small[:, 1, head : 2 * head].reshape(-1)]
    )
    return (
        result.astype(F32),
        input_grad.astype(F32),
        by_token[0],
        by_token[1],
        grad_w_qkv,
        grad_b_qv,
        g_o.reshape(slices * head, quarter).astype(F32),
        by_token[4],
        by_token[2],
        by_token[3],
        grad_w_up,
        small[:, 0].reshape(-1),
        g_d.reshape(slices * hidden, quarter).astype(F32),
        by_token[5],
    )


def fits_square(mesh, *arrays):
    sizes = tuple(mesh.shape[name] for name in ("dp", "row", "col"))
    return (
        sizes == (4, 4, 2)
        and arrays[0].shape == (512, 256)
        and arrays[2].shape == (13,)
        and arrays[3].shape == (1024,)
        and arrays[6].shape == (256, 3, 512)
        and arrays[12].shape == (256, 2048)
    )


def solution(mesh):
    placed = (
        P(("dp", "col"), "row"),
        P(("dp", "col"), "row"),
        P("dp"),
        P("dp"),
        P("row"),
        P("row"),
        P("row", None, "col"),
        P(None, "col"),
        P("col", "row"),
        P("row"),
        P("row"),
        P("row"),
        P("row", "col"),
        P("col"),
        P("col", "row"),
        P("row"),
    )

    def on_each(*arrays):
        return (layer_on_square if fits_square(mesh, *arrays) else on_device)(*arrays)

    return jax.shard_map(
        on_each,
        mesh=mesh,
        in_specs=placed,
        out_specs=(
            P(("dp", "col"), "row"),
            P(("dp", "col"), "row"),
            P("row"),
            P("row"),
            P("row", None, "col"),
            P(None, "col"),
            P("col", "row"),
            P("row"),
            P("row"),
            P("row"),
            P("row", "col"),
            P("col"),
            P("col", "row"),
            P("row"),
        ),
        check_vma=False,
    )
```

```python
import functools
import math

import jax
import jax.numpy as jnp
from jax import lax
from jax.experimental import pallas as pl
from jax.experimental.pallas import tpu as pltpu
from jax.sharding import PartitionSpec as P

MESH = pl.DeviceIdType.MESH
BF = jnp.bfloat16
F32 = jnp.float32


HD = 128


EPS = 1e-05
MASKED = -1e30


def gelu_value(values):
    return 0.5 * values * (1.0 + jax.scipy.special.erf(values / math.sqrt(2.0)))


def gelu_slope(values):
    return 0.5 * (1.0 + jax.scipy.special.erf(values / math.sqrt(2.0))) + values * jnp.exp(
        -0.5 * values * values
    ) / math.sqrt(2.0 * math.pi)


def width_sums(first_term, second_term):
    return lax.psum((jnp.sum(first_term, axis=1), jnp.sum(second_term, axis=1)), "row")


def normalize(values, norm_gain, norm_bias, feature_count):
    row_total, square = width_sums(values, values * values)
    row_mean = row_total / feature_count
    inv_std = lax.rsqrt(square / feature_count - row_mean * row_mean + EPS)
    normed = (values - row_mean[:, None]) * inv_std[:, None]
    return (normed, inv_std, (normed * norm_gain + norm_bias).astype(jnp.bfloat16))


def normalize_back(upstream, normed, inv_std, norm_gain, feature_count):
    spread = upstream * norm_gain
    row_total, cross_sum = width_sums(spread, spread * normed)
    return inv_std[:, None] * (
        spread - row_total[:, None] / feature_count - normed * (cross_sum[:, None] / feature_count)
    )


def contract(left_op, right_op, flipped):
    if flipped:
        return lax.dot_general(
            left_op, right_op, (((1,), (1,)), ((), ())), preferred_element_type=jnp.float32
        )
    return jnp.dot(left_op, right_op, preferred_element_type=jnp.float32)


def outer_sum(left_op, right_op):
    return lax.dot_general(
        left_op, right_op, (((0,), (0,)), ((), ())), preferred_element_type=jnp.float32
    )


def across_rows(operand, weight_block, flipped):
    gathered = lax.all_gather(operand, "col", axis=0, tiled=True)
    row_count = gathered.shape[0] // lax.axis_size("row")

    def partial_term(row_start, row_num):
        return contract(gathered, weight_block, flipped)

    return (
        lax.psum_scatter(
            partial_term(jnp.int32(0), row_count * lax.axis_size("row")),
            "row",
            scatter_dimension=0,
            tiled=True,
        ),
        gathered,
    )


def across_cols(operand, weight_block, flipped):
    gathered = lax.all_gather(operand, "row", axis=0, tiled=True)
    row_count = gathered.shape[0] // lax.axis_size("col")

    def partial_term(row_start, row_num):
        return contract(gathered, weight_block, flipped)

    return (
        lax.psum_scatter(
            partial_term(jnp.int32(0), row_count * lax.axis_size("col")),
            "col",
            scatter_dimension=0,
            tiled=True,
        ),
        gathered,
    )


def tree_labels(seg_parent, token_depth):
    seg_count = seg_parent.shape[0]
    tree_len = token_depth.shape[0]
    seg_len = tree_len // 16
    slot_ids = jnp.arange(seg_count, dtype=jnp.int32)
    where_at = jnp.arange(tree_len, dtype=jnp.int32)
    segment = jnp.where(where_at < 4 * seg_len, 0, 1 + (where_at - 4 * seg_len) // seg_len)
    parent_local = seg_parent - lax.axis_index("dp") * seg_count
    parent_one = jnp.sum(
        jnp.where(segment[:, None] == slot_ids[None, :], parent_local[None, :], 0), axis=1
    )
    parent_two = jnp.sum(
        jnp.where(parent_one[:, None] == slot_ids[None, :], parent_local[None, :], 0), axis=1
    )
    return (segment, parent_one, parent_two, token_depth)


def block_scores(query_block, key_rows, labels, query_start, slopes):
    segment, parent_one, parent_two, token_depth = labels
    block_size = query_block.shape[0]
    query_seg = lax.dynamic_slice_in_dim(segment, query_start, block_size, 0)
    query_one = lax.dynamic_slice_in_dim(parent_one, query_start, block_size, 0)
    query_two = lax.dynamic_slice_in_dim(parent_two, query_start, block_size, 0)
    query_depth = lax.dynamic_slice_in_dim(token_depth, query_start, block_size, 0)
    allowed = (
        (segment[None, :] == query_seg[:, None])
        | (segment[None, :] == query_one[:, None])
        | (segment[None, :] == query_two[:, None])
    ) & (token_depth[None, :] <= query_depth[:, None])
    score_scale = query_block.shape[2] ** (-0.5)
    raw = jnp.einsum("qhd,khd->hqk", query_block, key_rows, preferred_element_type=jnp.float32)
    distance = (query_depth[:, None] - token_depth[None, :]).astype(jnp.float32)
    scores = raw * score_scale - slopes[:, None, None] * distance[None]
    return jnp.where(allowed[None], scores, MASKED)


def attention_forward(queries, key_rows, value_rows, labels, slopes, offset):
    block_size = min(512, queries.shape[0])
    blocks = queries.shape[0] // block_size

    def one_block(block_index):
        block_first = block_index * block_size
        query_block = lax.dynamic_slice_in_dim(queries, block_first, block_size, 0)
        scores = block_scores(query_block, key_rows, labels, offset + block_first, slopes)
        top_score = jnp.max(scores, axis=2, keepdims=True)
        weights = jnp.exp(scores - top_score)
        weight_total = jnp.sum(weights, axis=2, keepdims=True)
        probs = (weights / weight_total).astype(jnp.bfloat16)
        mixed = jnp.einsum("hqk,khd->qhd", probs, value_rows, preferred_element_type=jnp.float32)
        return (mixed, (top_score + jnp.log(weight_total))[:, :, 0])

    return lax.map(one_block, jnp.arange(blocks, dtype=jnp.int32))


def attention_backward(
    queries, key_rows, value_rows, grad_mixed, log_total, labels, slopes, offset
):
    block_size = min(512, queries.shape[0])
    blocks = queries.shape[0] // block_size
    score_scale = queries.shape[2] ** (-0.5)

    def one_block(carry, items):
        key_grad, value_grad = carry
        block_index, block_total = items
        block_first = block_index * block_size
        query_block = lax.dynamic_slice_in_dim(queries, block_first, block_size, 0)
        grad_block = lax.dynamic_slice_in_dim(grad_mixed, block_first, block_size, 0)
        scores = block_scores(query_block, key_rows, labels, offset + block_first, slopes)
        probs = jnp.exp(scores - block_total[:, :, None])
        grad_probs = jnp.einsum(
            "qhd,khd->hqk", grad_block, value_rows, preferred_element_type=jnp.float32
        )
        centre = jnp.sum(probs * grad_probs, axis=2, keepdims=True)
        grad_scores = (probs * (grad_probs - centre)).astype(jnp.bfloat16)
        query_grad = (
            jnp.einsum("hqk,khd->qhd", grad_scores, key_rows, preferred_element_type=jnp.float32)
            * score_scale
        )
        key_grad = (
            key_grad
            + jnp.einsum(
                "hqk,qhd->khd", grad_scores, query_block, preferred_element_type=jnp.float32
            )
            * score_scale
        )
        value_grad = value_grad + jnp.einsum(
            "hqk,qhd->khd",
            probs.astype(jnp.bfloat16),
            grad_block,
            preferred_element_type=jnp.float32,
        )
        return ((key_grad, value_grad), query_grad)

    empty = jnp.zeros(key_rows.shape, jnp.float32)
    (key_grad, value_grad), query_grad = lax.scan(
        one_block, (empty, empty), (jnp.arange(blocks, dtype=jnp.int32), log_total)
    )
    return (key_grad, value_grad, query_grad)


def on_device(
    inputs,
    cotangent,
    seg_parent,
    token_depth,
    ln1_gain,
    ln1_bias,
    w_qkv,
    b_qv,
    w_out,
    b_out,
    ln2_gain,
    ln2_bias,
    w_up,
    b_up,
    w_down,
    b_down,
):
    feature_count = inputs.shape[1] * lax.axis_size("row")
    col_width = w_qkv.shape[2]
    heads_here = col_width // HD
    qkv_flat = w_qkv.reshape(w_qkv.shape[0], 3 * col_width)
    labels = tree_labels(seg_parent, token_depth)
    heads_seen = lax.axis_index("col") * heads_here + jnp.arange(heads_here, dtype=jnp.int32)
    slopes = jnp.exp2(-(heads_seen + 1).astype(jnp.float32))
    states = inputs.astype(jnp.float32)
    normed_one, inv_one, entry_one = normalize(states, ln1_gain, ln1_bias, feature_count)
    projected, entry_one_all = across_rows(entry_one, qkv_flat, False)
    tok_rows = projected.shape[0]
    projected = projected.reshape(tok_rows, 3, col_width)
    queries = (projected[:, 0] + b_qv[0]).astype(jnp.bfloat16)
    keys_here = projected[:, 1].astype(jnp.bfloat16)
    values_here = (projected[:, 2] + b_qv[1]).astype(jnp.bfloat16)
    pair_all = lax.all_gather(
        jnp.stack([keys_here, values_here], axis=1), "row", axis=0, tiled=True
    )
    key_rows = pair_all[:, 0].reshape(-1, heads_here, HD)
    value_rows = pair_all[:, 1].reshape(-1, heads_here, HD)
    query_heads = queries.reshape(tok_rows, heads_here, HD)
    offset = lax.axis_index("row") * tok_rows
    mixed, log_total = attention_forward(query_heads, key_rows, value_rows, labels, slopes, offset)
    mixed = mixed.reshape(tok_rows, col_width).astype(jnp.bfloat16)
    attn_out, mixed_all = across_cols(mixed, w_out, False)
    middle = states + attn_out + b_out
    normed_two, inv_two, entry_two = normalize(middle, ln2_gain, ln2_bias, feature_count)
    hidden_pre, entry_two_all = across_rows(entry_two, w_up, False)
    hidden_pre = hidden_pre + b_up
    hidden = gelu_value(hidden_pre).astype(jnp.bfloat16)
    ffn_out, hidden_all = across_cols(hidden, w_down, False)
    result = middle + ffn_out + b_down
    grad_hidden, down_all = across_rows(cotangent, w_down, True)
    grad_pre = (grad_hidden * gelu_slope(hidden_pre)).astype(jnp.bfloat16)
    grad_entry_two, pre_all = across_cols(grad_pre, w_up, True)
    grad_middle = cotangent.astype(jnp.float32) + normalize_back(
        grad_entry_two, normed_two, inv_two, ln2_gain, feature_count
    )
    grad_branch = grad_middle.astype(jnp.bfloat16)
    grad_mixed, branch_all = across_rows(grad_branch, w_out, True)
    grad_mixed = grad_mixed.astype(jnp.bfloat16).reshape(tok_rows, heads_here, HD)
    key_grad, value_grad, query_grad = attention_backward(
        query_heads, key_rows, value_rows, grad_mixed, log_total, labels, slopes, offset
    )
    kv_grads = lax.psum_scatter(
        jnp.stack([key_grad.reshape(-1, col_width), value_grad.reshape(-1, col_width)], axis=1),
        "row",
        scatter_dimension=0,
        tiled=True,
    )
    grad_projected = jnp.stack(
        [
            query_grad.reshape(tok_rows, col_width).astype(jnp.bfloat16),
            kv_grads[:, 0].astype(jnp.bfloat16),
            kv_grads[:, 1].astype(jnp.bfloat16),
        ],
        axis=1,
    )
    grad_entry_one, proj_all = across_cols(
        grad_projected.reshape(tok_rows, 3 * col_width), qkv_flat, True
    )
    input_grad = grad_middle + normalize_back(
        grad_entry_one, normed_one, inv_one, ln1_gain, feature_count
    )
    proj_sums = jnp.sum(proj_all.astype(jnp.float32), axis=0).reshape(3, col_width)
    weight_terms = (
        outer_sum(entry_one_all, proj_all).reshape(w_qkv.shape),
        jnp.stack([proj_sums[0], proj_sums[2]], axis=0),
        outer_sum(mixed_all, branch_all),
        jnp.sum(branch_all.astype(jnp.float32), axis=0),
        outer_sum(entry_two_all, pre_all),
        jnp.sum(pre_all.astype(jnp.float32), axis=0),
        outer_sum(hidden_all, down_all),
        jnp.sum(down_all.astype(jnp.float32), axis=0),
    )
    (
        grad_w_qkv,
        grad_b_qv,
        grad_w_out,
        grad_b_out,
        grad_w_up,
        grad_b_up,
        grad_w_down,
        grad_b_down,
    ) = lax.psum(
        (
            weight_terms[0],
            weight_terms[1],
            weight_terms[2],
            weight_terms[3],
            weight_terms[4],
            weight_terms[5],
            weight_terms[6],
            weight_terms[7],
        ),
        "dp",
    )
    norm_terms = (
        jnp.sum(grad_entry_one * normed_one, axis=0),
        jnp.sum(grad_entry_one, axis=0),
        jnp.sum(grad_entry_two * normed_two, axis=0),
        jnp.sum(grad_entry_two, axis=0),
    )
    grad_ln1_gain, grad_ln1_bias, grad_ln2_gain, grad_ln2_bias = lax.psum(
        (norm_terms[0], norm_terms[1], norm_terms[2], norm_terms[3]), ("dp", "col")
    )
    return (
        result,
        input_grad,
        grad_ln1_gain,
        grad_ln1_bias,
        grad_w_qkv,
        grad_b_qv,
        grad_w_out,
        grad_b_out,
        grad_ln2_gain,
        grad_ln2_bias,
        grad_w_up,
        grad_b_up,
        grad_w_down,
        grad_b_down,
    )


RELS = (0, 4, 2, 6)


def dot_nn(a, b):
    return lax.dot_general(a, b, (((1,), (0,)), ((), ())), preferred_element_type=F32)


def dot_nt(a, b):
    return lax.dot_general(a, b, (((1,), (1,)), ((), ())), preferred_element_type=F32)


def dot_tn(a, b):
    return lax.dot_general(a, b, (((0,), (0,)), ((), ())), preferred_element_type=F32)


def span(index, size):
    return pl.ds(pl.multiple_of(index * size, size), size)


class Net:
    def __init__(self, ssem, rsem):
        self.dp = lax.axis_index("dp")
        self.row = lax.axis_index("row")
        self.col = lax.axis_index("col")
        self.y, self.k = self.dp // 2, self.dp % 2
        self.zh, self.zl = self.row // 2, self.row % 2
        self.x = self.col
        self.slot = self.x * 4 + self.zl * 2 + self.k
        self.chip = self.x * 2 + self.zl
        self.slice = self.zl * 2 + self.k
        self.ssem, self.rsem = ssem, rsem
        self.used = 0
        self.pending = []

    def sites(self, n):
        first = self.used
        self.used += n
        return first

    def peer(self, dy=0, dk=0, dz=0, dx=0):
        return (
            (self.y ^ dy) * 2 + (self.k ^ dk),
            self.row ^ dz,
            self.col ^ dx,
        )

    def rel(self, rel):
        return self.peer(dz=(rel >> 1) & 1, dx=rel >> 2, dk=rel & 1)

    def make(self, src, dst, site, device, recv_site=None):
        recv = site if recv_site is None else recv_site
        return pltpu.make_async_remote_copy(
            src_ref=src,
            dst_ref=dst,
            send_sem=self.ssem.at[site],
            recv_sem=self.rsem.at[recv],
            device_id=device,
            device_id_type=MESH,
        )

    def send(self, src, dst, site, device, recv_site=None, skip=None):
        remote = self.make(src, dst, site, device, recv_site)
        if skip is None:
            remote.start()
        else:
            recv = site if recv_site is None else recv_site

            @pl.when(skip)
            def _():
                pltpu.make_async_copy(src, dst, self.rsem.at[recv]).start()

            @pl.when(jnp.logical_not(skip))
            def _():
                remote.start()

        self.pending.append((remote, skip))
        return remote

    def landed(self, ref, site):
        self.make(ref, ref, site, self.peer(dk=1)).wait_recv()

    def drain(self, upto=None):
        for remote, skip in self.pending:
            if skip is None:
                remote.wait_send()
            else:

                @pl.when(jnp.logical_not(skip))
                def _(remote=remote):
                    remote.wait_send()

        self.pending = []


class Gather:
    def __init__(self, net, buf, by_low, over_y=False):
        self.net, self.buf, self.over_y = net, buf, over_y
        self.slot = net.x * 4 + net.y * 2 + net.k if over_y else net.slot
        self.first = net.sites(8)
        rows = buf.shape[1]
        self.low_rows = pl.ds(0, by_low) if by_low else None
        self.x_rows = pl.ds(by_low, rows - by_low) if by_low < rows else None

    def to(self, rel):
        low = (rel >> 1) & 1
        where = {"dy": low} if self.over_y else {"dz": low}
        return self.net.peer(dk=rel & 1, dx=rel >> 2, **where)

    def start(self):
        own = self.buf.at[self.slot]
        for n, rel in enumerate((1, 4, 2)):
            self.net.send(own, own, self.first + n, self.to(rel))

    def relay(self, j):
        net = self.net
        part = self.buf.at[self.slot ^ RELS[j]]
        if j < 3:
            net.landed(part, self.first + j)
            rows, rel = ((self.low_rows, 2), (self.x_rows, 4))[j - 1]
            if rows is not None:
                some = part.at[rows, :]
                net.send(some, some, self.first + 2 + j, self.to(rel))
        else:
            for n, rows in enumerate((self.low_rows, self.x_rows)):
                if rows is not None:
                    net.landed(part.at[rows, :], self.first + 3 + n)
        net.send(part, part, self.first + 4 + j, self.to(1))

    def ready(self, j):
        part = self.buf.at[self.slot ^ RELS[j] ^ 1]
        self.net.landed(part, self.first if j == 0 else self.first + 4 + j)

    def block(self, j):
        chip = (self.slot ^ RELS[j]) // 2
        both = self.buf[pl.ds(chip * 2, 2)]
        return both.reshape(2 * both.shape[1], both.shape[2])


class Exchange:
    def __init__(self, net, src_of, dst_of):
        self.net, self.src_of, self.dst_of = net, src_of, dst_of
        self.first = net.sites(7)

    def start(self):
        net = self.net
        for n in (6, 7, 4, 5, 2, 3, 1):
            net.send(
                self.src_of(net.slot ^ n), self.dst_of(net.slot), self.first + n - 1, net.rel(n)
            )

    def ready(self):
        net = self.net
        for n in range(1, 8):
            net.landed(self.dst_of(net.slot ^ n), self.first + n - 1)


class Scatter:
    def __init__(self, net, bufs, land, cut):
        self.net, self.cut = net, cut
        self.part, self.hops, self.kept, self.last = bufs
        self.one, self.two, self.three = land
        self.first = net.sites(10)
        self.sent = []
        rows = self.part.shape[1]
        self.ways = [
            way
            for way in ((0, pl.ds(0, cut), 1, 2), (1, pl.ds(cut, rows - cut), 2, 1))
            if way[1].size
        ]

    def send(self, src, dst, site, rel):
        self.sent.append(self.net.send(src, dst, self.first + site, self.net.rel(rel)))

    def put(self, j, value):
        net = self.net
        chip = net.chip ^ (RELS[j] >> 1)
        shard = self.part.shape[1]
        self.part[pl.ds(chip * 2, 2)] = value.astype(BF).reshape(2, shard, value.shape[1])
        self.send(self.part.at[chip * 2 + (1 - net.k)], self.one.at[j], j, 1)

    def chip_sum(self, j):
        net = self.net
        chip = net.chip ^ (RELS[j] >> 1)
        net.landed(self.one.at[j], self.first + j)
        return self.part[chip * 2 + net.k].astype(F32) + self.one[j].astype(F32)

    def hop(self, j):
        value = self.chip_sum(j)
        for n, rows, near, far in self.ways:
            mine = value[rows.start : rows.start + rows.size]
            if j == far:
                self.kept[rows, :] = mine
            else:
                place = 0 if j == near else 1
                self.hops[place, rows, :] = mine.astype(BF)
                self.send(
                    self.hops.at[place, rows, :],
                    self.two.at[place, rows, :],
                    4 + 2 * n + place,
                    RELS[near],
                )

    def hop_on(self):
        net = self.net
        for n, rows, near, far in self.ways:
            net.landed(self.two.at[1, rows, :], self.first + 5 + 2 * n)
            self.last[rows, :] = (
                self.kept[rows, :] + self.two[1, rows, :].astype(F32)
            ).astype(BF)
            self.send(self.last.at[rows, :], self.three.at[rows, :], 8 + n, RELS[far])

    def left(self):
        for remote in self.sent:
            remote.wait_send()
        mine = {id(remote) for remote in self.sent}
        self.net.pending = [p for p in self.net.pending if id(p[0]) not in mine]

    def total(self):
        net = self.net
        value = self.chip_sum(0)
        for n, rows, near, far in self.ways:
            net.landed(self.two.at[0, rows, :], self.first + 4 + 2 * n)
            net.landed(self.three.at[rows, :], self.first + 8 + n)
        return value + self.two[0].astype(F32) + self.three[...].astype(F32)


class TreeSum:
    def __init__(self, net, own, land_y, hop, land_z, done, out, local_sem):
        self.net, self.own, self.land_y = net, own, land_y
        self.hop_buf, self.land_z, self.done, self.out = hop, land_z, done, out
        self.first = net.sites(7)
        self.local_sem = local_sem

    def put(self, z, value):
        rows = self.own.shape[3]
        self.own[z // 2, z % 2] = value.astype(BF).reshape(2, rows, value.shape[1])

    def half(self, piece, which):
        return self.out.at[piece, span(which, self.own.shape[3]), :]

    def start(self):
        net = self.net
        net.send(self.own.at[:, :, 1 - net.y], self.land_y, self.first, net.peer(dy=1))

    def across(self):
        net = self.net
        net.landed(self.land_y, self.first)
        far = 1 - net.zh
        for low in (0, 1):
            self.hop_buf[low] = (
                self.own[far, low, net.y].astype(F32) + self.land_y[far, low].astype(F32)
            ).astype(BF)
        net.send(self.hop_buf, self.land_z, self.first + 1, net.peer(dz=2))

    def hand_out(self):
        net = self.net
        net.landed(self.land_z, self.first + 1)
        for low in (0, 1):
            self.done[low] = (
                self.own[net.zh, low, net.y].astype(F32)
                + self.land_y[net.zh, low].astype(F32)
                + self.land_z[low].astype(F32)
            ).astype(BF)
        place = self.half(net.slice, net.y)
        net.send(self.done.at[1 - net.zl], place, self.first + 2, net.peer(dz=1))
        net.send(self.done.at[net.zl], place, self.first + 3, net.peer(dy=1))
        self.kept = pltpu.make_async_copy(self.done.at[net.zl], place, self.local_sem)
        self.kept.start()

    def pass_on(self):
        net = self.net
        part = self.half(net.slice ^ 2, net.y)
        net.landed(part, self.first + 2)
        net.send(part, part, self.first + 4, net.peer(dy=1))

    def share(self):
        net = self.net
        self.kept.wait()
        for n, piece in enumerate((net.slice, net.slice ^ 2)):
            net.landed(self.half(piece, 1 - net.y), self.first + 3 + n)
            part = self.out.at[piece]
            net.send(part, part, self.first + 5 + n, net.rel(1))

    def finish(self):
        net = self.net
        for n, piece in enumerate((net.slice ^ 1, net.slice ^ 3)):
            net.landed(self.out.at[piece], self.first + 5 + n)


def layer_kernel(eps, masked, used, *refs):
    (
        inp, cot, w_q, w_o, w_d, w_u, vec_0, vec_1, vec_2, vec_3, vec_4, vec_5, parents, b_up, b_qv,
        res_out, grad_out, out_a, out_b, out_o, out_d, out_u, out_tok, out_small,
        xs, e1, g, e2, gb, wf, wq, wd, wu, mixed_all, grad_all, links, vec_in, vec, bias,
        q_buf, k_buf, v_buf, p_buf, mix, mix_b,
        part_a, hops_a, kept_a, last_a, part_b, hops_b, kept_b, last_b, one, two, three,
        hid, gp, gm, dk_acc, dv_acc, dqkv, mid, gmid, back_a, back_b,
        dw_a, dw_b, dw_o, dw_d, dw_u, ly_a, ly_b, ly_o, ly_d, ly_u,
        yh_a, yh_b, yh_o, yh_d, yh_u, lz_a, lz_b, lz_o, lz_d, lz_u,
        fin_a, fin_b, fin_o, fin_d, fin_u,
        tok, tok_one, tok_sum, tok_two, small, small_land, small_sum,
        ssem, rsem, lsem,
    ) = refs
    net = Net(ssem, rsem)
    y, k, zh, zl, x, row = net.y, net.k, net.zh, net.zl, net.x, net.row
    shard, width = xs.shape
    tokens = 8 * shard
    quarter = width // 4
    head = q_buf.shape[1]

    greet = [
        net.peer(dy=dy, dk=dk, dz=dz)
        for dy in (0, 1)
        for dk in (0, 1)
        for dz in (0, 1, 2, 3)
        if dy + dk + dz
    ]
    greet += [net.peer(dk=dk, dz=dz, dx=1) for dk in (0, 1) for dz in (0, 1)]
    vec_parts = (vec_0, vec_1, vec_2, vec_3, vec_4, vec_5)
    for n, part in enumerate(vec_parts):
        pltpu.make_async_copy(part, vec_in.at[pl.ds(n, 1), :], lsem.at[9]).start()
    seg_count = parents.shape[0]
    half_at = lax.broadcasted_iota(jnp.int32, links.shape[1:], 0)
    mine = jnp.zeros(links.shape[1:], F32)
    for s in range(1, seg_count):
        parent = parents[s] - net.dp * seg_count
        mine = jnp.where(half_at == s + 3, parent.astype(F32), mine)
    links[0] = mine

    barrier = pltpu.get_barrier_semaphore()
    for device in greet:
        pl.semaphore_signal(barrier, inc=1, device_id=device, device_id_type=MESH)
    pl.semaphore_wait(barrier, len(greet))

    def send_home(src, dst_of, first):
        for s in range(4):
            low, core = s // 2, s % 2
            target = 2 * k + low
            net.send(
                src.at[span(s, shard), :],
                dst_of(s).at[:, span(row, quarter)],
                first + s,
                (y * 2 + core, target, net.col),
                recv_site=first + 4 + row,
                skip=(target == row) & (k == core),
            )

    def home_ready(dst, first):
        for z in range(4):
            net.landed(dst.at[:, span(z, quarter)], first + 4 + z)

    vec_site = net.sites(3)
    pltpu.make_async_copy(vec_in.at[pl.ds(0, 6), :], vec_in.at[pl.ds(0, 6), :], lsem.at[9]).wait()
    for o in (1, 2, 3):
        net.send(
            vec_in.at[pl.ds(0, 8), :], vec.at[:, span(row, quarter)], vec_site + o - 1, net.peer(dz=o)
        )
    links_site = net.sites(1)
    net.send(links.at[0], links.at[1], links_site, net.rel(1))
    home_x, home_g = net.sites(8), net.sites(8)
    send_home(inp, lambda s: xs, home_x)

    def slices(w_ref, full, axis):
        if axis == 0:
            rows = full.shape[0] // 4
            return rows, lambda z: full.at[span(z, rows), :]
        cols = full.shape[1] // 4
        return full.shape[0], lambda z: full.at[:, span(z, cols)]

    class Weight:
        def __init__(self, src_of, full, axis, local):
            self.src_of, self.full = src_of, full
            self.rows, self.place = slices(None, full, axis)
            self.first = net.sites(6)
            self.local = local

        def half(self, ref, which):
            rows = self.rows // 2
            return ref.at[span(which, rows), :]

        def start(self):
            own = pltpu.make_async_copy(
                self.place(row), self.place(row), lsem.at[self.local]
            )
            for src, cols in self.src_of(net.slice):
                pltpu.make_async_copy(
                    src, self.place(row).at[:, cols], lsem.at[self.local]
                ).start()
            for o in (1, 2, 3):
                far = (zl ^ (o & 1)) * 2 + k
                for src, cols in self.src_of(far):
                    net.send(
                        self.half(src, y),
                        self.half(self.place(row), y).at[:, cols],
                        self.first + o - 1,
                        net.peer(dz=o),
                    )
            self.own = own

        def relay(self):
            for o in (1, 2, 3):
                part = self.half(self.place(row ^ o), y)
                net.landed(part, self.first + o - 1)
                net.send(part, part, self.first + 2 + o, net.peer(dy=1))

        def ready(self):
            for o in (1, 2, 3):
                net.landed(self.half(self.place(row ^ o), 1 - y), self.first + 2 + o)
            self.own.wait()

    hidden = hid.shape[1]
    whole = slice(None)

    def qkv_parts(s):
        return [
            (w_q.at[n, :, span(s, head)], pl.ds(n * head, head)) for n in range(3)
        ]

    weight_q = Weight(qkv_parts, wq, 0, 0)
    weight_d = Weight(lambda s: [(w_d.at[span(s, hidden), :], whole)], wd, 1, 2)
    weight_u = Weight(lambda s: [(w_u.at[:, span(s, hidden)], whole)], wu, 0, 3)
    weight_q.start()

    gather_w = Gather(net, wf, shard // 2, over_y=True)
    wf_own = wf.at[gather_w.slot]
    wf_site = net.sites(3)
    wf_src = w_o.at[span(y * 2 + k, shard), :]
    wf_copy = pltpu.make_async_copy(wf_src, wf_own.at[:, span(row, quarter)], lsem.at[1])
    wf_copy.start()
    for o in (1, 2, 3):
        net.send(wf_src, wf_own.at[:, span(row, quarter)], wf_site + o - 1, net.peer(dz=o))

    vec[:, span(row, quarter)] = vec_in[...]
    for o in (1, 2, 3):
        net.landed(vec.at[:, span(row ^ o, quarter)], vec_site + o - 1)

    def norm_stats(values):
        mean = jnp.sum(values, axis=1, keepdims=True) * (1.0 / width)
        msq = jnp.sum(values * values, axis=1, keepdims=True) * (1.0 / width)
        inv = lax.rsqrt(msq - mean * mean + eps)
        return (values - mean) * inv, inv

    home_ready(xs, home_x)
    normed, _ = norm_stats(xs[...].astype(F32))
    e1[net.slot] = (normed * vec[0:1, :] + vec[1:2, :]).astype(BF)
    gather_e1 = Gather(net, e1, 0)
    gather_e1.start()
    gather_g = Gather(net, g, 0)
    send_home(cot, lambda s: g.at[x * 4 + s], home_g)
    weight_u.start()
    weight_d.start()
    weight_q.relay()

    net.landed(links.at[1], links_site)
    parent = jnp.where(zh == k, links[0], links[1])[:, 0:1]
    seg_len = tokens // 16
    key_at = lax.broadcasted_iota(jnp.int32, (1, tokens), 1)
    key_half = key_at // seg_len
    key_seg = jnp.maximum(key_half - 3, 0)
    half_row = lax.broadcasted_iota(jnp.int32, (16, 1), 0)
    seg_row = jnp.maximum(half_row - 3, 0)
    key_parent = jnp.sum(jnp.where(key_half == half_row, parent, 0.0), axis=0, keepdims=True)
    start = jnp.where(key_parent > 0.0, 5 * seg_len, 4 * seg_len)
    depth = jnp.where(key_seg == 0, key_at, start + key_at % seg_len)
    allowed = (key_seg == 0) | (key_seg == seg_row) | (key_seg == parent.astype(jnp.int32))
    exponent = jnp.full((1, tokens), -(x * 4 + net.slice + 1), jnp.int32).astype(F32)
    slope = jnp.exp2(exponent)
    bias[...] = jnp.where(allowed, slope * depth.astype(F32), masked)

    b_q = b_qv[0:1, span(net.slice, head)]
    b_v = b_qv[1:2, span(net.slice, head)]
    gather_e1.relay(1)
    gather_e1.relay(2)
    weight_q.ready()
    for j in range(4):
        if j == 3:
            for o in (1, 2, 3):
                net.landed(wf_own.at[:, span(row ^ o, quarter)], wf_site + o - 1)
            wf_copy.wait()
            gather_w.start()
            gather_e1.relay(3)
        gather_e1.ready(j)
        rows = pl.ds((net.chip ^ (RELS[j] >> 1)) * 2 * shard, 2 * shard)
        proj = dot_nn(gather_e1.block(j), wq[...])
        q_buf[rows, :] = (proj[:, :head] + b_q).astype(BF)
        k_buf[rows, :] = proj[:, head : 2 * head].astype(BF)
        v_buf[rows, :] = (proj[:, 2 * head :] + b_v).astype(BF)

    scale = head ** (-0.5)

    def attend(i, carry):
        first = pl.multiple_of(i * shard, shard)
        raw = dot_nt(q_buf[pl.ds(first, shard), :], k_buf[...])
        parts = []
        for half in (0, 1):
            at = 2 * i + half
            seg = jnp.maximum(at - 3, 0)
            later = jnp.where(key_seg == seg, key_at, -1)
            query_at = first + half * seg_len + lax.broadcasted_iota(jnp.int32, (seg_len, 1), 0)
            scores = raw[half * seg_len : (half + 1) * seg_len] * scale + bias[pl.ds(at, 1), :]
            scores = jnp.where(later > query_at, masked, scores)
            top = jnp.max(scores, axis=1, keepdims=True)
            weights = jnp.exp(scores - top)
            norm = 1.0 / jnp.sum(weights, axis=1, keepdims=True)
            parts.append((weights * norm).astype(BF))
        probs = jnp.concatenate(parts, axis=0)
        p_buf[pl.ds(first, shard), :] = probs
        mixed = dot_nn(probs, v_buf[...])
        mix[pl.ds(first, shard), :] = mixed
        mix_b[pl.ds(first, shard), :] = mixed.astype(BF)
        return carry

    lax.fori_loop(0, 6, attend, 0)
    gather_w.relay(1)
    gather_w.relay(2)
    lax.fori_loop(6, 8, attend, 0)

    def rows_of(j):
        return span(net.chip ^ (RELS[j] >> 1), 2 * shard)

    order = (3, 1, 2, 0)
    part_set_a = (part_a, hops_a, kept_a, last_a)
    part_set_b = (part_b, hops_b, kept_b, last_b)

    def landings(n):
        return (one.at[n], two.at[n], three.at[n])

    swap = Exchange(
        net, lambda q: mix_b.at[span(q, shard), :], lambda h: mixed_all.at[:, span(h, head)]
    )
    swap.start()
    mixed_all[:, span(net.slot, head)] = mix_b[span(net.slot, shard), :]
    home_ready(g.at[net.slot], home_g)
    gather_g.start()
    gather_w.relay(3)
    weight_u.relay()
    for j in range(4):
        gather_w.ready(j)
    swap.ready()
    w_out = wf[...].reshape(width, width)

    middle = xs[...].astype(F32) + dot_nn(mixed_all[...], w_out) + vec[2:3, :]
    mid[...] = middle
    normed, _ = norm_stats(middle)
    e2[net.slot] = (normed * vec[3:4, :] + vec[4:5, :]).astype(BF)
    gather_e2 = Gather(net, e2, shard // 2)
    gather_e2.start()
    weight_d.relay()
    gather_g.relay(1)
    gather_g.relay(2)
    gather_e2.relay(1)
    gather_e2.relay(2)


    b_u = b_up[0:1, span(net.slice, hidden)]
    weight_u.ready()
    scatter_two = Scatter(net, part_set_a, landings(0), shard // 2)
    for j in range(4):
        if j == 3:
            gather_e2.relay(3)
        gather_e2.ready(j)
        pre = dot_nn(gather_e2.block(j), wu[...]) + b_u
        bell = 0.5 * (1.0 + lax.erf(pre * (1.0 / math.sqrt(2.0))))
        hid[rows_of(j), :] = (pre * bell).astype(BF)
        if j == 0:
            weight_d.ready()
        if j == 3:
            gather_g.relay(3)
        gather_g.ready(j)
        rise = bell + pre * jnp.exp(-0.5 * pre * pre) * (1.0 / math.sqrt(2.0 * math.pi))
        gp[rows_of(j), :] = (dot_nt(gather_g.block(j), wd[...]) * rise).astype(BF)
        scatter_two.put(j, dot_nt(gp[rows_of(j), :], wu[...]))
        if j == 2:
            scatter_two.hop(1)
    scatter_two.hop(2)
    scatter_two.hop(3)

    sums = {
        name: TreeSum(net, own, land_y, hop, land_z, done, out, lsem.at[4 + n])
        for n, (name, own, land_y, hop, land_z, done, out) in enumerate(
            (
                ("a", dw_a, ly_a, yh_a, lz_a, fin_a, out_a),
                ("b", dw_b, ly_b, yh_b, lz_b, fin_b, out_b),
                ("o", dw_o, ly_o, yh_o, lz_o, fin_o, out_o),
                ("d", dw_d, ly_d, yh_d, lz_d, fin_d, out_d),
                ("u", dw_u, ly_u, yh_u, lz_u, fin_u, out_u),
            )
        )
    }

    def columns(buf, z):
        part = buf[:, :, span(z, quarter)]
        return part.reshape(tokens, quarter)

    def grad_down(z, carry):
        sums["d"].put(z, dot_tn(hid[...], columns(g, z)))
        return carry

    def grad_up(z, carry):
        sums["u"].put(z, dot_tn(columns(e2, z), gp[...]))
        return carry

    def grad_qkv(z, carry):
        value = dot_tn(columns(e1, z), dqkv[...])
        sums["a"].put(z, value[:, :head])
        sums["b"].put(z, value[:, head:])
        return carry

    def grad_o(z, carry):
        sums["o"].put(z, dot_tn(mix_b[...], columns(gb, z)))
        return carry

    lax.fori_loop(0, 4, grad_down, 0)
    sums["d"].start()
    scatter_two.hop_on()
    lax.fori_loop(0, 4, grad_up, 0)

    grad = scatter_two.total()
    middle = mid[...]
    normed, inv = norm_stats(middle)
    spread = grad * vec[3:4, :]
    mean_one = jnp.sum(spread, axis=1, keepdims=True) * (1.0 / width)
    mean_two = jnp.sum(spread * normed, axis=1, keepdims=True) * (1.0 / width)
    cot_own = g[net.slot].astype(F32)
    total = cot_own + inv * (spread - mean_one - normed * mean_two)
    gmid[...] = total
    branch = total.astype(BF)
    gb[net.slot] = branch
    grad_all[...] = dot_nt(branch, w_out).astype(BF)
    swap_back = Exchange(
        net, lambda h: grad_all.at[:, span(h, head)], lambda q: gm.at[span(q, shard), :]
    )
    swap_back.start()
    gm[span(net.slot, shard), :] = grad_all[:, span(net.slot, head)]
    tok[2:3, :] = jnp.sum(grad * normed, axis=0, keepdims=True)
    tok[3:4, :] = jnp.sum(grad, axis=0, keepdims=True)
    tok[4:5, :] = jnp.sum(branch.astype(F32), axis=0, keepdims=True)
    tok[5:6, :] = jnp.sum(cot_own, axis=0, keepdims=True)
    tok[6:8, :] = jnp.zeros((2, width), F32)
    dk_acc[...] = jnp.zeros_like(dk_acc)
    dv_acc[...] = jnp.zeros_like(dv_acc)
    small[...] = jnp.zeros_like(small)
    small[0:1, :] = jnp.sum(gp[...].astype(F32), axis=0, keepdims=True)
    gather_gb = Gather(net, gb, 0)

    def tile_back(t, carry):
        rows = span(t, shard)
        grad_mix = gm[rows, :]
        probs = p_buf[rows, :]
        grad_probs = dot_nt(grad_mix, v_buf[...])
        centre = jnp.sum(mix[rows, :] * grad_mix.astype(F32), axis=1, keepdims=True)
        grad_scores = (probs.astype(F32) * (grad_probs - centre)).astype(BF)
        dqkv[rows, :head] = (dot_nn(grad_scores, k_buf[...]) * scale).astype(BF)
        dk_acc[...] += dot_tn(grad_scores, q_buf[rows, :])
        dv_acc[...] += dot_tn(probs, grad_mix)
        return carry

    swap_back.ready()
    gather_gb.start()
    sums["d"].across()
    sums["u"].start()
    lax.fori_loop(0, 8, tile_back, 0)
    dqkv[:, head : 2 * head] = (dk_acc[...] * scale).astype(BF)
    dqkv[:, 2 * head :] = dv_acc[...].astype(BF)
    gather_gb.relay(1)
    gather_gb.relay(2)

    scatter_four = Scatter(net, part_set_a, landings(1), shard // 2)
    scatter_two.left()
    for j in order:
        scatter_four.put(j, dot_nt(dqkv[rows_of(j), :], wq[...]))
    for j in (3, 1, 2):
        scatter_four.hop(j)
    lax.fori_loop(0, 4, grad_qkv, 0)
    scatter_four.hop_on()
    sums["u"].across()
    sums["b"].start()
    sums["a"].start()
    sums["d"].hand_out()

    small[1:2, :head] = jnp.sum(dqkv[:, :head].astype(F32), axis=0, keepdims=True)
    small[1:2, head : 2 * head] = jnp.sum(dqkv[:, 2 * head :].astype(F32), axis=0, keepdims=True)
    small_site = net.sites(6)
    others = ((1, 0), (0, 2), (1, 2))
    for n, (dy, dz) in enumerate(others):
        net.send(small, small_land.at[n], small_site + n, net.peer(dy=dy, dz=dz))
    gather_gb.relay(3)
    for j in range(4):
        gather_gb.ready(j)
    lax.fori_loop(0, 4, grad_o, 0)

    def send_out(src, dst, first):
        for z in range(4):
            net.send(
                src.at[:, span(z, quarter)],
                dst.at[span(net.slice, shard), :],
                first + z,
                (y * 2 + zh, z, net.col),
                recv_site=first + 4 + net.slice,
                skip=(row == z) & (k == zh),
            )

    def out_ready(dst, first):
        for s in range(4):
            net.landed(dst.at[span(s, shard), :], first + 4 + s)

    res_site, grad_site = net.sites(8), net.sites(8)
    grad = scatter_four.total()
    normed, inv = norm_stats(xs[...].astype(F32))
    tok[0:1, :] = jnp.sum(grad * normed, axis=0, keepdims=True)
    tok[1:2, :] = jnp.sum(grad, axis=0, keepdims=True)
    tok_site = net.sites(10)
    for n in range(1, 8):
        net.send(tok, tok_one.at[n - 1], tok_site + n - 1, net.rel(n))
    spread = grad * vec[0:1, :]
    mean_one = jnp.sum(spread, axis=1, keepdims=True) * (1.0 / width)
    mean_two = jnp.sum(spread * normed, axis=1, keepdims=True) * (1.0 / width)
    back_b[...] = (gmid[...] + inv * (spread - mean_one - normed * mean_two)).astype(BF)
    send_out(back_b, grad_out, grad_site)

    scatter_three = Scatter(net, part_set_b, landings(2), shard)
    for j in order:
        scatter_three.put(j, dot_nn(hid[rows_of(j), :], wd[...]))
    for j in (3, 1, 2):
        scatter_three.hop(j)
    sums["d"].pass_on()
    sums["b"].across()
    sums["a"].across()
    sums["o"].start()
    sums["u"].hand_out()
    scatter_three.hop_on()
    sums["o"].across()
    sums["b"].hand_out()
    sums["a"].hand_out()
    sums["u"].pass_on()
    sums["d"].share()
    back_a[...] = (mid[...] + scatter_three.total() + vec[5:6, :]).astype(BF)
    send_out(back_a, res_out, res_site)
    sums["b"].pass_on()
    sums["a"].pass_on()
    sums["o"].hand_out()
    sums["u"].share()
    acc = small[...]
    for n in range(3):
        net.landed(small_land.at[n], small_site + n)
        acc = acc + small_land[n]
    small_sum[...] = acc
    out_small[net.slice] = acc
    for n, (dk, dz) in enumerate(((1, 0), (0, 1), (1, 1))):
        net.send(
            small_sum, out_small.at[net.slice], small_site + 3 + n, net.peer(dk=dk, dz=dz)
        )
    acc = tok[...]
    for n in range(7):
        net.landed(tok_one.at[n], tok_site + n)
        acc = acc + tok_one[n]
    tok_sum[...] = acc
    tok_sent = [
        net.send(tok_sum, tok_two.at[n], tok_site + 7 + n, net.peer(dy=dy, dz=dz))
        for n, (dy, dz) in enumerate(others)
    ]
    gone = {id(remote) for remote in tok_sent}
    net.pending = [p for p in net.pending if id(p[0]) not in gone]
    sums["o"].pass_on()
    sums["b"].share()
    sums["a"].share()
    sums["o"].share()
    for n in range(3):
        net.landed(tok_two.at[n], tok_site + 7 + n)
        acc = acc + tok_two[n]
    for remote in tok_sent:
        remote.wait_send()
    tok_sum[...] = acc
    out_tok[...] = tok_sum[:, span(row, quarter)]
    for n, flip in enumerate((1, 2, 3)):
        net.landed(out_small.at[net.slice ^ flip], small_site + 3 + n)
    for one_sum in sums.values():
        one_sum.finish()
    out_ready(res_out, res_site)
    out_ready(grad_out, grad_site)
    net.drain()
    used.append(net.used)


def layer_on_square(
    inputs, cotangent, seg_parent, token_depth, ln1_gain, ln1_bias, w_qkv, b_qv, w_out, b_out,
    ln2_gain, ln2_bias, w_up, b_up, w_down, b_down,
):
    half_tokens, quarter = inputs.shape
    tokens, width = token_depth.shape[0], 4 * quarter
    shard = tokens // 8
    head = HD
    slices = w_qkv.shape[2] // head
    hidden = w_up.shape[1] // slices
    row = lax.axis_index("row")

    any_ = pl.BlockSpec(memory_space=pl.ANY)
    vmem = pl.BlockSpec(memory_space=pltpu.VMEM)
    sds = jax.ShapeDtypeStruct

    def vm(*dims, dtype=BF):
        return pltpu.VMEM(dims, dtype)

    blocks = {
        "a": (quarter, head), "b": (quarter, 2 * head), "o": (head, quarter),
        "d": (hidden, quarter), "u": (quarter, hidden),
    }
    names = ("a", "b", "o", "d", "u")
    halves = {n: (blocks[n][0] // 2, blocks[n][1]) for n in names}
    scratch = [
        vm(shard, width),
        *[vm(8, shard, width) for _ in range(5)],
        vm(width, 3 * head), vm(hidden, width), vm(width, hidden),
        vm(shard, width), vm(shard, width),
        vm(2, 16, 128, dtype=F32), vm(8, quarter, dtype=F32), vm(8, width, dtype=F32),
        vm(16, tokens, dtype=F32),
        *[vm(tokens, head) for _ in range(3)], vm(tokens, tokens),
        vm(tokens, head, dtype=F32), vm(tokens, head),
        *[
            spec
            for _ in range(2)
            for spec in (
                vm(8, shard, width), vm(2, shard, width),
                vm(shard, width, dtype=F32), vm(shard, width),
            )
        ],
        vm(3, 4, shard, width), vm(3, 2, shard, width), vm(3, shard, width),
        vm(tokens, hidden), vm(tokens, hidden),
        vm(tokens, head), vm(tokens, head, dtype=F32), vm(tokens, head, dtype=F32),
        vm(tokens, 3 * head),
        vm(shard, width, dtype=F32), vm(shard, width, dtype=F32), vm(shard, width), vm(shard, width),
        *[vm(2, 2, 2, *halves[n]) for n in names],
        *[vm(2, 2, *halves[n]) for n in names],
        *[vm(2, *halves[n]) for n in names],
        *[vm(2, *halves[n]) for n in names],
        *[vm(2, *halves[n]) for n in names],
        vm(8, width, dtype=F32), vm(7, 8, width, dtype=F32), vm(8, width, dtype=F32),
        vm(3, 8, width, dtype=F32),
        vm(8, hidden, dtype=F32), vm(3, 8, hidden, dtype=F32), vm(8, hidden, dtype=F32),
        pltpu.SemaphoreType.DMA((208,)), pltpu.SemaphoreType.DMA((208,)),
        pltpu.SemaphoreType.DMA((10,)),
    ]
    used = []
    outs = pl.pallas_call(
        functools.partial(layer_kernel, EPS, MASKED, used),
        out_shape=(
            sds((half_tokens, quarter), BF), sds((half_tokens, quarter), BF),
            *[sds((slices, *blocks[n]), BF) for n in names],
            sds((8, quarter), F32), sds((slices, 8, hidden), F32),
        ),
        in_specs=[any_] * 12 + [pl.BlockSpec(memory_space=pltpu.SMEM)] + [vmem] * 2,
        out_specs=(any_,) * 7 + (vmem,) * 2,
        scratch_shapes=scratch,
        compiler_params=pltpu.CompilerParams(
            collective_id=0, has_side_effects=True, vmem_limit_bytes=60 << 20
        ),
        name="tree_layer",
    )(
        inputs, cotangent, w_qkv.transpose(1, 0, 2), w_out, w_down, w_up,
        *[v.reshape(1, -1) for v in (ln1_gain, ln1_bias, b_out, ln2_gain, ln2_bias, b_down)],
        seg_parent, b_up.reshape(1, -1), b_qv,
    )
    result, input_grad, g_a, g_b, g_o, g_d, g_u, by_token, small = outs
    steps = 2

    def finish(res_in, grad_in, a_in, b_in, o_in, d_in, u_in, tok_in, small_in, *into):
        res, grad, q, o, d, u, tok_0, tok_1, tok_2, tok_3, tok_4, tok_5, up, qv = into
        res[...] = res_in[...].astype(F32)
        grad[...] = grad_in[...].astype(F32)
        o[...] = o_in[...].astype(F32)
        d[...] = d_in[...].astype(F32)
        for s in range(slices):
            u[:, s * hidden : (s + 1) * hidden] = u_in[s].astype(F32)
            at = slice(s * head, (s + 1) * head)
            q[0, :, at] = a_in[s].astype(F32)
            for n in range(2):
                q[n + 1, :, at] = b_in[s, :, n * head : (n + 1) * head].astype(F32)
            up[0:1, s * hidden : (s + 1) * hidden] = small_in[s, 0:1, :]
            for n in range(2):
                qv[n : n + 1, at] = small_in[
                    s, 1:2, n * head : (n + 1) * head
                ]
        for n, one in enumerate((tok_0, tok_1, tok_2, tok_3, tok_4, tok_5)):
            one[...] = tok_in[n : n + 1, :]

    def rows(*dims):
        return pl.BlockSpec((dims[0] // steps, *dims[1:]), lambda i: (i,) + (0,) * (len(dims) - 1))

    def middle(*dims):
        return pl.BlockSpec((dims[0], dims[1] // steps, *dims[2:]), lambda i: (0, i, 0))

    def fixed(*dims):
        return pl.BlockSpec(dims, lambda i: (0,) * len(dims))

    tall_o, tall_d = (slices * head, quarter), (slices * hidden, quarter)
    done = pl.pallas_call(
        finish,
        grid=(steps,),
        out_shape=(
            sds((half_tokens, quarter), F32), sds((half_tokens, quarter), F32),
            sds((3, quarter, slices * head), F32), sds(tall_o, F32), sds(tall_d, F32),
            sds((quarter, slices * hidden), F32), *[sds((1, quarter), F32)] * 6,
            sds((1, slices * hidden), F32), sds((2, slices * head), F32),
        ),
        in_specs=[
            rows(half_tokens, quarter), rows(half_tokens, quarter),
            middle(slices, *blocks["a"]), middle(slices, *blocks["b"]), rows(*tall_o), rows(*tall_d), middle(slices, *blocks["u"]),
            fixed(8, quarter), fixed(slices, 8, hidden),
        ],
        out_specs=(
            rows(half_tokens, quarter), rows(half_tokens, quarter),
            middle(3, quarter, slices * head), rows(*tall_o), rows(*tall_d),
            rows(quarter, slices * hidden), *[fixed(1, quarter)] * 6,
            fixed(1, slices * hidden), fixed(2, slices * head),
        ),
        compiler_params=pltpu.CompilerParams(vmem_limit_bytes=60 << 20),
        name="finish",
    )(
        result, input_grad, g_a, g_b, g_o.reshape(tall_o), g_d.reshape(tall_d), g_u, by_token, small
    )
    by_token = [v.reshape(-1) for v in done[6:12]]
    return (
        done[0], done[1], by_token[0], by_token[1], done[2].transpose(1, 0, 2), done[13], done[3], by_token[4],
        by_token[2], by_token[3], done[5], done[12].reshape(-1), done[4], by_token[5],
    )


def fits_square(mesh, *arrays):
    sizes = tuple(mesh.shape[name] for name in ("dp", "row", "col"))
    return (
        sizes == (4, 4, 2)
        and arrays[0].shape == (512, 256)
        and arrays[2].shape == (13,)
        and arrays[3].shape == (1024,)
        and arrays[6].shape == (256, 3, 512)
        and arrays[12].shape == (256, 2048)
    )


def solution(mesh):
    placed = (
        P(("dp", "col"), "row"),
        P(("dp", "col"), "row"),
        P("dp"),
        P("dp"),
        P("row"),
        P("row"),
        P("row", None, "col"),
        P(None, "col"),
        P("col", "row"),
        P("row"),
        P("row"),
        P("row"),
        P("row", "col"),
        P("col"),
        P("col", "row"),
        P("row"),
    )

    def on_each(*arrays):
        return (layer_on_square if fits_square(mesh, *arrays) else on_device)(*arrays)

    return jax.shard_map(
        on_each,
        mesh=mesh,
        in_specs=placed,
        out_specs=(
            P(("dp", "col"), "row"),
            P(("dp", "col"), "row"),
            P("row"),
            P("row"),
            P("row", None, "col"),
            P(None, "col"),
            P("col", "row"),
            P("row"),
            P("row"),
            P("row"),
            P("row", "col"),
            P("col"),
            P("col", "row"),
            P("row"),
        ),
        check_vma=False,
    )
```

```python
import functools
import math

import jax
import jax.numpy as jnp
from jax import lax
from jax.experimental import pallas as pl
from jax.experimental.pallas import tpu as pltpu
from jax.sharding import PartitionSpec as P

MESH = pl.DeviceIdType.MESH
BF = jnp.bfloat16
F32 = jnp.float32


HD = 128


EPS = 1e-05
MASKED = -1e30


def gelu_value(values):
    return 0.5 * values * (1.0 + jax.scipy.special.erf(values / math.sqrt(2.0)))


def gelu_slope(values):
    return 0.5 * (1.0 + jax.scipy.special.erf(values / math.sqrt(2.0))) + values * jnp.exp(
        -0.5 * values * values
    ) / math.sqrt(2.0 * math.pi)


def width_sums(first_term, second_term):
    return lax.psum((jnp.sum(first_term, axis=1), jnp.sum(second_term, axis=1)), "row")


def normalize(values, norm_gain, norm_bias, feature_count):
    row_total, square = width_sums(values, values * values)
    row_mean = row_total / feature_count
    inv_std = lax.rsqrt(square / feature_count - row_mean * row_mean + EPS)
    normed = (values - row_mean[:, None]) * inv_std[:, None]
    return (normed, inv_std, (normed * norm_gain + norm_bias).astype(jnp.bfloat16))


def normalize_back(upstream, normed, inv_std, norm_gain, feature_count):
    spread = upstream * norm_gain
    row_total, cross_sum = width_sums(spread, spread * normed)
    return inv_std[:, None] * (
        spread - row_total[:, None] / feature_count - normed * (cross_sum[:, None] / feature_count)
    )


def contract(left_op, right_op, flipped):
    if flipped:
        return lax.dot_general(
            left_op, right_op, (((1,), (1,)), ((), ())), preferred_element_type=jnp.float32
        )
    return jnp.dot(left_op, right_op, preferred_element_type=jnp.float32)


def outer_sum(left_op, right_op):
    return lax.dot_general(
        left_op, right_op, (((0,), (0,)), ((), ())), preferred_element_type=jnp.float32
    )


def across_rows(operand, weight_block, flipped):
    gathered = lax.all_gather(operand, "col", axis=0, tiled=True)
    row_count = gathered.shape[0] // lax.axis_size("row")

    def partial_term(row_start, row_num):
        return contract(gathered, weight_block, flipped)

    return (
        lax.psum_scatter(
            partial_term(jnp.int32(0), row_count * lax.axis_size("row")),
            "row",
            scatter_dimension=0,
            tiled=True,
        ),
        gathered,
    )


def across_cols(operand, weight_block, flipped):
    gathered = lax.all_gather(operand, "row", axis=0, tiled=True)
    row_count = gathered.shape[0] // lax.axis_size("col")

    def partial_term(row_start, row_num):
        return contract(gathered, weight_block, flipped)

    return (
        lax.psum_scatter(
            partial_term(jnp.int32(0), row_count * lax.axis_size("col")),
            "col",
            scatter_dimension=0,
            tiled=True,
        ),
        gathered,
    )


def tree_labels(seg_parent, token_depth):
    seg_count = seg_parent.shape[0]
    tree_len = token_depth.shape[0]
    seg_len = tree_len // 16
    slot_ids = jnp.arange(seg_count, dtype=jnp.int32)
    where_at = jnp.arange(tree_len, dtype=jnp.int32)
    segment = jnp.where(where_at < 4 * seg_len, 0, 1 + (where_at - 4 * seg_len) // seg_len)
    parent_local = seg_parent - lax.axis_index("dp") * seg_count
    parent_one = jnp.sum(
        jnp.where(segment[:, None] == slot_ids[None, :], parent_local[None, :], 0), axis=1
    )
    parent_two = jnp.sum(
        jnp.where(parent_one[:, None] == slot_ids[None, :], parent_local[None, :], 0), axis=1
    )
    return (segment, parent_one, parent_two, token_depth)


def block_scores(query_block, key_rows, labels, query_start, slopes):
    segment, parent_one, parent_two, token_depth = labels
    block_size = query_block.shape[0]
    query_seg = lax.dynamic_slice_in_dim(segment, query_start, block_size, 0)
    query_one = lax.dynamic_slice_in_dim(parent_one, query_start, block_size, 0)
    query_two = lax.dynamic_slice_in_dim(parent_two, query_start, block_size, 0)
    query_depth = lax.dynamic_slice_in_dim(token_depth, query_start, block_size, 0)
    allowed = (
        (segment[None, :] == query_seg[:, None])
        | (segment[None, :] == query_one[:, None])
        | (segment[None, :] == query_two[:, None])
    ) & (token_depth[None, :] <= query_depth[:, None])
    score_scale = query_block.shape[2] ** (-0.5)
    raw = jnp.einsum("qhd,khd->hqk", query_block, key_rows, preferred_element_type=jnp.float32)
    distance = (query_depth[:, None] - token_depth[None, :]).astype(jnp.float32)
    scores = raw * score_scale - slopes[:, None, None] * distance[None]
    return jnp.where(allowed[None], scores, MASKED)


def attention_forward(queries, key_rows, value_rows, labels, slopes, offset):
    block_size = min(512, queries.shape[0])
    blocks = queries.shape[0] // block_size

    def one_block(block_index):
        block_first = block_index * block_size
        query_block = lax.dynamic_slice_in_dim(queries, block_first, block_size, 0)
        scores = block_scores(query_block, key_rows, labels, offset + block_first, slopes)
        top_score = jnp.max(scores, axis=2, keepdims=True)
        weights = jnp.exp(scores - top_score)
        weight_total = jnp.sum(weights, axis=2, keepdims=True)
        probs = (weights / weight_total).astype(jnp.bfloat16)
        mixed = jnp.einsum("hqk,khd->qhd", probs, value_rows, preferred_element_type=jnp.float32)
        return (mixed, (top_score + jnp.log(weight_total))[:, :, 0])

    return lax.map(one_block, jnp.arange(blocks, dtype=jnp.int32))


def attention_backward(
    queries, key_rows, value_rows, grad_mixed, log_total, labels, slopes, offset
):
    block_size = min(512, queries.shape[0])
    blocks = queries.shape[0] // block_size
    score_scale = queries.shape[2] ** (-0.5)

    def one_block(carry, items):
        key_grad, value_grad = carry
        block_index, block_total = items
        block_first = block_index * block_size
        query_block = lax.dynamic_slice_in_dim(queries, block_first, block_size, 0)
        grad_block = lax.dynamic_slice_in_dim(grad_mixed, block_first, block_size, 0)
        scores = block_scores(query_block, key_rows, labels, offset + block_first, slopes)
        probs = jnp.exp(scores - block_total[:, :, None])
        grad_probs = jnp.einsum(
            "qhd,khd->hqk", grad_block, value_rows, preferred_element_type=jnp.float32
        )
        centre = jnp.sum(probs * grad_probs, axis=2, keepdims=True)
        grad_scores = (probs * (grad_probs - centre)).astype(jnp.bfloat16)
        query_grad = (
            jnp.einsum("hqk,khd->qhd", grad_scores, key_rows, preferred_element_type=jnp.float32)
            * score_scale
        )
        key_grad = (
            key_grad
            + jnp.einsum(
                "hqk,qhd->khd", grad_scores, query_block, preferred_element_type=jnp.float32
            )
            * score_scale
        )
        value_grad = value_grad + jnp.einsum(
            "hqk,qhd->khd",
            probs.astype(jnp.bfloat16),
            grad_block,
            preferred_element_type=jnp.float32,
        )
        return ((key_grad, value_grad), query_grad)

    empty = jnp.zeros(key_rows.shape, jnp.float32)
    (key_grad, value_grad), query_grad = lax.scan(
        one_block, (empty, empty), (jnp.arange(blocks, dtype=jnp.int32), log_total)
    )
    return (key_grad, value_grad, query_grad)


def on_device(
    inputs,
    cotangent,
    seg_parent,
    token_depth,
    ln1_gain,
    ln1_bias,
    w_qkv,
    b_qv,
    w_out,
    b_out,
    ln2_gain,
    ln2_bias,
    w_up,
    b_up,
    w_down,
    b_down,
):
    feature_count = inputs.shape[1] * lax.axis_size("row")
    col_width = w_qkv.shape[2]
    heads_here = col_width // HD
    qkv_flat = w_qkv.reshape(w_qkv.shape[0], 3 * col_width)
    labels = tree_labels(seg_parent, token_depth)
    heads_seen = lax.axis_index("col") * heads_here + jnp.arange(heads_here, dtype=jnp.int32)
    slopes = jnp.exp2(-(heads_seen + 1).astype(jnp.float32))
    states = inputs.astype(jnp.float32)
    normed_one, inv_one, entry_one = normalize(states, ln1_gain, ln1_bias, feature_count)
    projected, entry_one_all = across_rows(entry_one, qkv_flat, False)
    tok_rows = projected.shape[0]
    projected = projected.reshape(tok_rows, 3, col_width)
    queries = (projected[:, 0] + b_qv[0]).astype(jnp.bfloat16)
    keys_here = projected[:, 1].astype(jnp.bfloat16)
    values_here = (projected[:, 2] + b_qv[1]).astype(jnp.bfloat16)
    pair_all = lax.all_gather(
        jnp.stack([keys_here, values_here], axis=1), "row", axis=0, tiled=True
    )
    key_rows = pair_all[:, 0].reshape(-1, heads_here, HD)
    value_rows = pair_all[:, 1].reshape(-1, heads_here, HD)
    query_heads = queries.reshape(tok_rows, heads_here, HD)
    offset = lax.axis_index("row") * tok_rows
    mixed, log_total = attention_forward(query_heads, key_rows, value_rows, labels, slopes, offset)
    mixed = mixed.reshape(tok_rows, col_width).astype(jnp.bfloat16)
    attn_out, mixed_all = across_cols(mixed, w_out, False)
    middle = states + attn_out + b_out
    normed_two, inv_two, entry_two = normalize(middle, ln2_gain, ln2_bias, feature_count)
    hidden_pre, entry_two_all = across_rows(entry_two, w_up, False)
    hidden_pre = hidden_pre + b_up
    hidden = gelu_value(hidden_pre).astype(jnp.bfloat16)
    ffn_out, hidden_all = across_cols(hidden, w_down, False)
    result = middle + ffn_out + b_down
    grad_hidden, down_all = across_rows(cotangent, w_down, True)
    grad_pre = (grad_hidden * gelu_slope(hidden_pre)).astype(jnp.bfloat16)
    grad_entry_two, pre_all = across_cols(grad_pre, w_up, True)
    grad_middle = cotangent.astype(jnp.float32) + normalize_back(
        grad_entry_two, normed_two, inv_two, ln2_gain, feature_count
    )
    grad_branch = grad_middle.astype(jnp.bfloat16)
    grad_mixed, branch_all = across_rows(grad_branch, w_out, True)
    grad_mixed = grad_mixed.astype(jnp.bfloat16).reshape(tok_rows, heads_here, HD)
    key_grad, value_grad, query_grad = attention_backward(
        query_heads, key_rows, value_rows, grad_mixed, log_total, labels, slopes, offset
    )
    kv_grads = lax.psum_scatter(
        jnp.stack([key_grad.reshape(-1, col_width), value_grad.reshape(-1, col_width)], axis=1),
        "row",
        scatter_dimension=0,
        tiled=True,
    )
    grad_projected = jnp.stack(
        [
            query_grad.reshape(tok_rows, col_width).astype(jnp.bfloat16),
            kv_grads[:, 0].astype(jnp.bfloat16),
            kv_grads[:, 1].astype(jnp.bfloat16),
        ],
        axis=1,
    )
    grad_entry_one, proj_all = across_cols(
        grad_projected.reshape(tok_rows, 3 * col_width), qkv_flat, True
    )
    input_grad = grad_middle + normalize_back(
        grad_entry_one, normed_one, inv_one, ln1_gain, feature_count
    )
    proj_sums = jnp.sum(proj_all.astype(jnp.float32), axis=0).reshape(3, col_width)
    weight_terms = (
        outer_sum(entry_one_all, proj_all).reshape(w_qkv.shape),
        jnp.stack([proj_sums[0], proj_sums[2]], axis=0),
        outer_sum(mixed_all, branch_all),
        jnp.sum(branch_all.astype(jnp.float32), axis=0),
        outer_sum(entry_two_all, pre_all),
        jnp.sum(pre_all.astype(jnp.float32), axis=0),
        outer_sum(hidden_all, down_all),
        jnp.sum(down_all.astype(jnp.float32), axis=0),
    )
    (
        grad_w_qkv,
        grad_b_qv,
        grad_w_out,
        grad_b_out,
        grad_w_up,
        grad_b_up,
        grad_w_down,
        grad_b_down,
    ) = lax.psum(
        (
            weight_terms[0],
            weight_terms[1],
            weight_terms[2],
            weight_terms[3],
            weight_terms[4],
            weight_terms[5],
            weight_terms[6],
            weight_terms[7],
        ),
        "dp",
    )
    norm_terms = (
        jnp.sum(grad_entry_one * normed_one, axis=0),
        jnp.sum(grad_entry_one, axis=0),
        jnp.sum(grad_entry_two * normed_two, axis=0),
        jnp.sum(grad_entry_two, axis=0),
    )
    grad_ln1_gain, grad_ln1_bias, grad_ln2_gain, grad_ln2_bias = lax.psum(
        (norm_terms[0], norm_terms[1], norm_terms[2], norm_terms[3]), ("dp", "col")
    )
    return (
        result,
        input_grad,
        grad_ln1_gain,
        grad_ln1_bias,
        grad_w_qkv,
        grad_b_qv,
        grad_w_out,
        grad_b_out,
        grad_ln2_gain,
        grad_ln2_bias,
        grad_w_up,
        grad_b_up,
        grad_w_down,
        grad_b_down,
    )


RELS = (0, 4, 2, 6)


def dot_nn(a, b):
    return lax.dot_general(a, b, (((1,), (0,)), ((), ())), preferred_element_type=F32)


def dot_nt(a, b):
    return lax.dot_general(a, b, (((1,), (1,)), ((), ())), preferred_element_type=F32)


def dot_tn(a, b):
    return lax.dot_general(a, b, (((0,), (0,)), ((), ())), preferred_element_type=F32)


def span(index, size):
    return pl.ds(pl.multiple_of(index * size, size), size)


class Net:
    def __init__(self, ssem, rsem):
        self.dp = lax.axis_index("dp")
        self.row = lax.axis_index("row")
        self.col = lax.axis_index("col")
        self.y, self.k = self.dp // 2, self.dp % 2
        self.zh, self.zl = self.row // 2, self.row % 2
        self.x = self.col
        self.slot = self.x * 4 + self.zl * 2 + self.k
        self.chip = self.x * 2 + self.zl
        self.slice = self.zl * 2 + self.k
        self.ssem, self.rsem = ssem, rsem
        self.used = 0
        self.pending = []

    def sites(self, n):
        first = self.used
        self.used += n
        return first

    def peer(self, dy=0, dk=0, dz=0, dx=0):
        return (
            (self.y ^ dy) * 2 + (self.k ^ dk),
            self.row ^ dz,
            self.col ^ dx,
        )

    def rel(self, rel):
        return self.peer(dz=(rel >> 1) & 1, dx=rel >> 2, dk=rel & 1)

    def make(self, src, dst, site, device, recv_site=None):
        recv = site if recv_site is None else recv_site
        return pltpu.make_async_remote_copy(
            src_ref=src,
            dst_ref=dst,
            send_sem=self.ssem.at[site],
            recv_sem=self.rsem.at[recv],
            device_id=device,
            device_id_type=MESH,
        )

    def send(self, src, dst, site, device, recv_site=None, skip=None):
        remote = self.make(src, dst, site, device, recv_site)
        if skip is None:
            remote.start()
        else:
            recv = site if recv_site is None else recv_site

            @pl.when(skip)
            def _():
                pltpu.make_async_copy(src, dst, self.rsem.at[recv]).start()

            @pl.when(jnp.logical_not(skip))
            def _():
                remote.start()

        self.pending.append((remote, skip))
        return remote

    def landed(self, ref, site):
        self.make(ref, ref, site, self.peer(dk=1)).wait_recv()

    def drain(self, upto=None):
        for remote, skip in self.pending:
            if skip is None:
                remote.wait_send()
            else:

                @pl.when(jnp.logical_not(skip))
                def _(remote=remote):
                    remote.wait_send()

        self.pending = []


class Gather:
    def __init__(self, net, buf, by_low, over_y=False):
        self.net, self.buf, self.over_y = net, buf, over_y
        self.slot = net.x * 4 + net.y * 2 + net.k if over_y else net.slot
        self.first = net.sites(8)
        rows = buf.shape[1]
        self.low_rows = pl.ds(0, by_low) if by_low else None
        self.x_rows = pl.ds(by_low, rows - by_low) if by_low < rows else None

    def to(self, rel):
        low = (rel >> 1) & 1
        where = {"dy": low} if self.over_y else {"dz": low}
        return self.net.peer(dk=rel & 1, dx=rel >> 2, **where)

    def start(self):
        own = self.buf.at[self.slot]
        for n, rel in enumerate((1, 4, 2)):
            self.net.send(own, own, self.first + n, self.to(rel))

    def relay(self, j):
        net = self.net
        part = self.buf.at[self.slot ^ RELS[j]]
        if j < 3:
            net.landed(part, self.first + j)
            rows, rel = ((self.low_rows, 2), (self.x_rows, 4))[j - 1]
            if rows is not None:
                some = part.at[rows, :]
                net.send(some, some, self.first + 2 + j, self.to(rel))
        else:
            for n, rows in enumerate((self.low_rows, self.x_rows)):
                if rows is not None:
                    net.landed(part.at[rows, :], self.first + 3 + n)
        net.send(part, part, self.first + 4 + j, self.to(1))

    def ready(self, j):
        part = self.buf.at[self.slot ^ RELS[j] ^ 1]
        self.net.landed(part, self.first if j == 0 else self.first + 4 + j)

    def block(self, j):
        chip = (self.slot ^ RELS[j]) // 2
        both = self.buf[pl.ds(chip * 2, 2)]
        return both.reshape(2 * both.shape[1], both.shape[2])


class Exchange:
    def __init__(self, net, src_of, dst_of):
        self.net, self.src_of, self.dst_of = net, src_of, dst_of
        self.first = net.sites(7)

    def start(self):
        net = self.net
        for n in (6, 7, 4, 5, 2, 3, 1):
            net.send(
                self.src_of(net.slot ^ n), self.dst_of(net.slot), self.first + n - 1, net.rel(n)
            )

    def ready(self):
        net = self.net
        for n in range(1, 8):
            net.landed(self.dst_of(net.slot ^ n), self.first + n - 1)


class Scatter:
    def __init__(self, net, bufs, land, cut):
        self.net, self.cut = net, cut
        self.part, self.hops, self.kept, self.last = bufs
        self.one, self.two, self.three = land
        self.first = net.sites(10)
        self.sent = []
        rows = self.part.shape[1]
        self.ways = [
            way
            for way in ((0, pl.ds(0, cut), 1, 2), (1, pl.ds(cut, rows - cut), 2, 1))
            if way[1].size
        ]

    def send(self, src, dst, site, rel):
        self.sent.append(self.net.send(src, dst, self.first + site, self.net.rel(rel)))

    def put(self, j, value):
        net = self.net
        chip = net.chip ^ (RELS[j] >> 1)
        shard = self.part.shape[1]
        self.part[pl.ds(chip * 2, 2)] = value.astype(BF).reshape(2, shard, value.shape[1])
        self.send(self.part.at[chip * 2 + (1 - net.k)], self.one.at[j], j, 1)

    def chip_sum(self, j):
        net = self.net
        chip = net.chip ^ (RELS[j] >> 1)
        net.landed(self.one.at[j], self.first + j)
        return self.part[chip * 2 + net.k].astype(F32) + self.one[j].astype(F32)

    def hop(self, j):
        value = self.chip_sum(j)
        for n, rows, near, far in self.ways:
            mine = value[rows.start : rows.start + rows.size]
            if j == far:
                self.kept[rows, :] = mine
            else:
                place = 0 if j == near else 1
                self.hops[place, rows, :] = mine.astype(BF)
                self.send(
                    self.hops.at[place, rows, :],
                    self.two.at[place, rows, :],
                    4 + 2 * n + place,
                    RELS[near],
                )

    def hop_on(self):
        net = self.net
        for n, rows, near, far in self.ways:
            net.landed(self.two.at[1, rows, :], self.first + 5 + 2 * n)
            self.last[rows, :] = (
                self.kept[rows, :] + self.two[1, rows, :].astype(F32)
            ).astype(BF)
            self.send(self.last.at[rows, :], self.three.at[rows, :], 8 + n, RELS[far])

    def left(self):
        for remote in self.sent:
            remote.wait_send()
        mine = {id(remote) for remote in self.sent}
        self.net.pending = [p for p in self.net.pending if id(p[0]) not in mine]

    def total(self):
        net = self.net
        value = self.chip_sum(0)
        for n, rows, near, far in self.ways:
            net.landed(self.two.at[0, rows, :], self.first + 4 + 2 * n)
            net.landed(self.three.at[rows, :], self.first + 8 + n)
        return value + self.two[0].astype(F32) + self.three[...].astype(F32)


class TreeSum:
    def __init__(self, net, own, land_y, hop, land_z, done, out, local_sem, direct):
        self.net, self.own, self.land_y = net, own, land_y
        self.hop_buf, self.land_z, self.done, self.out = hop, land_z, done, out
        self.first = net.sites(7)
        self.local_sem, self.direct = local_sem, direct

    def put(self, z, value):
        rows = self.own.shape[3]
        self.own[z // 2, z % 2] = value.astype(BF).reshape(2, rows, value.shape[1])

    def half(self, piece, which):
        return self.out.at[piece, span(which, self.own.shape[3]), :]

    def start(self):
        net = self.net
        net.send(self.own.at[:, :, 1 - net.y], self.land_y, self.first, net.peer(dy=1))

    def across(self):
        net = self.net
        net.landed(self.land_y, self.first)
        far = 1 - net.zh
        for low in (0, 1):
            self.hop_buf[low] = (
                self.own[far, low, net.y].astype(F32) + self.land_y[far, low].astype(F32)
            ).astype(BF)
        net.send(self.hop_buf, self.land_z, self.first + 1, net.peer(dz=2))

    def hand_out(self):
        net = self.net
        net.landed(self.land_z, self.first + 1)
        for low in (0, 1):
            self.done[low] = (
                self.own[net.zh, low, net.y].astype(F32)
                + self.land_y[net.zh, low].astype(F32)
                + self.land_z[low].astype(F32)
            ).astype(BF)
        place = self.half(net.slice, net.y)
        net.send(self.done.at[1 - net.zl], place, self.first + 2, net.peer(dz=1))
        net.send(self.done.at[net.zl], place, self.first + 3, net.peer(dy=1))
        if self.direct:
            net.send(self.done.at[1 - net.zl], place, self.first + 4, net.peer(dy=1, dz=1))
        self.kept = pltpu.make_async_copy(self.done.at[net.zl], place, self.local_sem)
        self.kept.start()

    def pass_on(self):
        net = self.net
        part = self.half(net.slice ^ 2, net.y)
        net.landed(part, self.first + 2)
        if not self.direct:
            net.send(part, part, self.first + 4, net.peer(dy=1))

    def share(self):
        net = self.net
        self.kept.wait()
        for n, piece in enumerate((net.slice, net.slice ^ 2)):
            net.landed(self.half(piece, 1 - net.y), self.first + 3 + n)
            part = self.out.at[piece]
            net.send(part, part, self.first + 5 + n, net.rel(1))

    def finish(self):
        net = self.net
        for n, piece in enumerate((net.slice ^ 1, net.slice ^ 3)):
            net.landed(self.out.at[piece], self.first + 5 + n)


def layer_kernel(eps, masked, used, *refs):
    (
        inp, cot, w_q, w_o, w_d, w_u, vec_0, vec_1, vec_2, vec_3, vec_4, vec_5, parents, b_up, b_qv,
        res_out, grad_out, out_a, out_b, out_o, out_d, out_u, out_tok, out_small,
        xs, e1, g, e2, gb, wf, wq, wd, wu, mixed_all, grad_all, links, vec_in, vec, bias,
        q_buf, k_buf, v_buf, p_buf, mix, mix_b,
        part_a, hops_a, kept_a, last_a, part_b, hops_b, kept_b, last_b, one, two, three,
        hid, gp, gm, dk_acc, dv_acc, dqkv, mid, gmid, back_a, back_b,
        dw_a, dw_b, dw_o, dw_d, dw_u, ly_a, ly_b, ly_o, ly_d, ly_u,
        yh_a, yh_b, yh_o, yh_d, yh_u, lz_a, lz_b, lz_o, lz_d, lz_u,
        fin_a, fin_b, fin_o, fin_d, fin_u,
        tok, tok_one, tok_sum, tok_two, small, small_land, small_sum,
        ssem, rsem, lsem,
    ) = refs
    net = Net(ssem, rsem)
    y, k, zh, zl, x, row = net.y, net.k, net.zh, net.zl, net.x, net.row
    shard, width = xs.shape
    tokens = 8 * shard
    quarter = width // 4
    head = q_buf.shape[1]

    greet = [
        net.peer(dy=dy, dk=dk, dz=dz)
        for dy in (0, 1)
        for dk in (0, 1)
        for dz in (0, 1, 2, 3)
        if dy + dk + dz
    ]
    greet += [net.peer(dk=dk, dz=dz, dx=1) for dk in (0, 1) for dz in (0, 1)]
    barrier = pltpu.get_barrier_semaphore()
    for device in greet:
        pl.semaphore_signal(barrier, inc=1, device_id=device, device_id_type=MESH)
    vec_parts = (vec_0, vec_1, vec_2, vec_3, vec_4, vec_5)
    for n, part in enumerate(vec_parts):
        pltpu.make_async_copy(part, vec_in.at[pl.ds(n, 1), :], lsem.at[9]).start()
    seg_count = parents.shape[0]
    half_at = lax.broadcasted_iota(jnp.int32, links.shape[1:], 0)
    mine = jnp.zeros(links.shape[1:], F32)
    for s in range(1, seg_count):
        parent = parents[s] - net.dp * seg_count
        mine = jnp.where(half_at == s + 3, parent.astype(F32), mine)
    links[0] = mine

    pl.semaphore_wait(barrier, len(greet))

    def send_home(src, dst_of, first):
        for s in range(4):
            low, core = s // 2, s % 2
            target = 2 * k + low
            net.send(
                src.at[span(s, shard), :],
                dst_of(s).at[:, span(row, quarter)],
                first + s,
                (y * 2 + core, target, net.col),
                recv_site=first + 4 + row,
                skip=(target == row) & (k == core),
            )

    def home_ready(dst, first):
        for z in range(4):
            net.landed(dst.at[:, span(z, quarter)], first + 4 + z)

    vec_site = net.sites(3)
    pltpu.make_async_copy(vec_in.at[pl.ds(0, 6), :], vec_in.at[pl.ds(0, 6), :], lsem.at[9]).wait()
    for o in (1, 2, 3):
        net.send(
            vec_in.at[pl.ds(0, 8), :], vec.at[:, span(row, quarter)], vec_site + o - 1, net.peer(dz=o)
        )
    links_site = net.sites(1)
    net.send(links.at[0], links.at[1], links_site, net.rel(1))
    home_x, home_g = net.sites(8), net.sites(8)
    send_home(inp, lambda s: xs, home_x)

    def slices(w_ref, full, axis):
        if axis == 0:
            rows = full.shape[0] // 4
            return rows, lambda z: full.at[span(z, rows), :]
        cols = full.shape[1] // 4
        return full.shape[0], lambda z: full.at[:, span(z, cols)]

    class Weight:
        def __init__(self, src_of, full, axis, local):
            self.src_of, self.full = src_of, full
            self.rows, self.place = slices(None, full, axis)
            self.first = net.sites(6)
            self.local = local

        def half(self, ref, which):
            rows = self.rows // 2
            return ref.at[span(which, rows), :]

        def start(self):
            own = pltpu.make_async_copy(
                self.place(row), self.place(row), lsem.at[self.local]
            )
            for src, cols in self.src_of(net.slice):
                pltpu.make_async_copy(
                    src, self.place(row).at[:, cols], lsem.at[self.local]
                ).start()
            for o in (1, 2, 3):
                far = (zl ^ (o & 1)) * 2 + k
                for src, cols in self.src_of(far):
                    net.send(
                        self.half(src, y),
                        self.half(self.place(row), y).at[:, cols],
                        self.first + o - 1,
                        net.peer(dz=o),
                    )
            self.own = own

        def relay(self):
            for o in (1, 2, 3):
                part = self.half(self.place(row ^ o), y)
                net.landed(part, self.first + o - 1)
                net.send(part, part, self.first + 2 + o, net.peer(dy=1))

        def ready(self):
            for o in (1, 2, 3):
                net.landed(self.half(self.place(row ^ o), 1 - y), self.first + 2 + o)
            self.own.wait()

    hidden = hid.shape[1]
    whole = slice(None)

    def qkv_parts(s):
        return [
            (w_q.at[n, :, span(s, head)], pl.ds(n * head, head)) for n in range(3)
        ]

    weight_q = Weight(qkv_parts, wq, 0, 0)
    weight_d = Weight(lambda s: [(w_d.at[span(s, hidden), :], whole)], wd, 1, 2)
    weight_u = Weight(lambda s: [(w_u.at[:, span(s, hidden)], whole)], wu, 0, 3)
    weight_q.start()

    gather_w = Gather(net, wf, shard // 2, over_y=True)
    wf_own = wf.at[gather_w.slot]
    wf_site = net.sites(3)
    wf_src = w_o.at[span(y * 2 + k, shard), :]
    wf_copy = pltpu.make_async_copy(wf_src, wf_own.at[:, span(row, quarter)], lsem.at[1])
    wf_copy.start()
    for o in (1, 2, 3):
        net.send(wf_src, wf_own.at[:, span(row, quarter)], wf_site + o - 1, net.peer(dz=o))

    vec[:, span(row, quarter)] = vec_in[...]
    for o in (1, 2, 3):
        net.landed(vec.at[:, span(row ^ o, quarter)], vec_site + o - 1)

    def norm_stats(values):
        mean = jnp.sum(values, axis=1, keepdims=True) * (1.0 / width)
        msq = jnp.sum(values * values, axis=1, keepdims=True) * (1.0 / width)
        inv = lax.rsqrt(msq - mean * mean + eps)
        return (values - mean) * inv, inv

    home_ready(xs, home_x)
    normed, _ = norm_stats(xs[...].astype(F32))
    e1[net.slot] = (normed * vec[0:1, :] + vec[1:2, :]).astype(BF)
    gather_e1 = Gather(net, e1, 0)
    gather_e1.start()
    gather_g = Gather(net, g, 0)
    send_home(cot, lambda s: g.at[x * 4 + s], home_g)
    weight_q.relay()

    net.landed(links.at[1], links_site)
    parent = jnp.where(zh == k, links[0], links[1])[:, 0:1]
    seg_len = tokens // 16
    key_at = lax.broadcasted_iota(jnp.int32, (1, tokens), 1)
    key_half = key_at // seg_len
    key_seg = jnp.maximum(key_half - 3, 0)
    half_row = lax.broadcasted_iota(jnp.int32, (16, 1), 0)
    seg_row = jnp.maximum(half_row - 3, 0)
    key_parent = jnp.sum(jnp.where(key_half == half_row, parent, 0.0), axis=0, keepdims=True)
    start = jnp.where(key_parent > 0.0, 5 * seg_len, 4 * seg_len)
    depth = jnp.where(key_seg == 0, key_at, start + key_at % seg_len)
    allowed = (key_seg == 0) | (key_seg == seg_row) | (key_seg == parent.astype(jnp.int32))
    exponent = jnp.full((1, tokens), -(x * 4 + net.slice + 1), jnp.int32).astype(F32)
    slope = jnp.exp2(exponent)
    bias[...] = jnp.where(allowed, slope * depth.astype(F32), masked)

    b_q = b_qv[0:1, span(net.slice, head)]
    b_v = b_qv[1:2, span(net.slice, head)]
    gather_e1.relay(1)
    gather_e1.relay(2)
    weight_u.start()
    weight_d.start()
    weight_q.ready()
    for j in range(4):
        if j == 3:
            for o in (1, 2, 3):
                net.landed(wf_own.at[:, span(row ^ o, quarter)], wf_site + o - 1)
            wf_copy.wait()
            gather_w.start()
            gather_e1.relay(3)
        gather_e1.ready(j)
        rows = pl.ds((net.chip ^ (RELS[j] >> 1)) * 2 * shard, 2 * shard)
        proj = dot_nn(gather_e1.block(j), wq[...])
        q_buf[rows, :] = (proj[:, :head] + b_q).astype(BF)
        k_buf[rows, :] = proj[:, head : 2 * head].astype(BF)
        v_buf[rows, :] = (proj[:, 2 * head :] + b_v).astype(BF)

    scale = head ** (-0.5)

    def attend(i, carry):
        first = pl.multiple_of(i * shard, shard)
        raw = dot_nt(q_buf[pl.ds(first, shard), :], k_buf[...])
        parts = []
        for half in (0, 1):
            at = 2 * i + half
            seg = jnp.maximum(at - 3, 0)
            later = jnp.where(key_seg == seg, key_at, -1)
            query_at = first + half * seg_len + lax.broadcasted_iota(jnp.int32, (seg_len, 1), 0)
            scores = raw[half * seg_len : (half + 1) * seg_len] * scale + bias[pl.ds(at, 1), :]
            scores = jnp.where(later > query_at, masked, scores)
            top = jnp.max(scores, axis=1, keepdims=True)
            weights = jnp.exp(scores - top)
            norm = 1.0 / jnp.sum(weights, axis=1, keepdims=True)
            parts.append((weights * norm).astype(BF))
        probs = jnp.concatenate(parts, axis=0)
        p_buf[pl.ds(first, shard), :] = probs
        mixed = dot_nn(probs, v_buf[...])
        mix[pl.ds(first, shard), :] = mixed
        mix_b[pl.ds(first, shard), :] = mixed.astype(BF)
        return carry

    lax.fori_loop(0, 6, attend, 0)
    gather_w.relay(1)
    gather_w.relay(2)
    lax.fori_loop(6, 8, attend, 0)

    def rows_of(j):
        return span(net.chip ^ (RELS[j] >> 1), 2 * shard)

    order = (3, 1, 2, 0)
    part_set_a = (part_a, hops_a, kept_a, last_a)
    part_set_b = (part_b, hops_b, kept_b, last_b)

    def landings(n):
        return (one.at[n], two.at[n], three.at[n])

    swap = Exchange(
        net, lambda q: mix_b.at[span(q, shard), :], lambda h: mixed_all.at[:, span(h, head)]
    )
    swap.start()
    mixed_all[:, span(net.slot, head)] = mix_b[span(net.slot, shard), :]
    home_ready(g.at[net.slot], home_g)
    gather_g.start()
    gather_w.relay(3)
    weight_u.relay()
    for j in range(4):
        gather_w.ready(j)
    swap.ready()
    w_out = wf[...].reshape(width, width)

    middle = xs[...].astype(F32) + dot_nn(mixed_all[...], w_out) + vec[2:3, :]
    mid[...] = middle
    normed, _ = norm_stats(middle)
    e2[net.slot] = (normed * vec[3:4, :] + vec[4:5, :]).astype(BF)
    gather_e2 = Gather(net, e2, shard // 2)
    gather_e2.start()
    weight_d.relay()
    gather_g.relay(1)
    gather_g.relay(2)
    gather_e2.relay(1)
    gather_e2.relay(2)


    b_u = b_up[0:1, span(net.slice, hidden)]
    weight_u.ready()
    scatter_two = Scatter(net, part_set_a, landings(0), shard // 2)
    for j in range(4):
        if j == 3:
            gather_e2.relay(3)
        gather_e2.ready(j)
        pre = dot_nn(gather_e2.block(j), wu[...]) + b_u
        bell = 0.5 * (1.0 + lax.erf(pre * (1.0 / math.sqrt(2.0))))
        hid[rows_of(j), :] = (pre * bell).astype(BF)
        if j == 0:
            weight_d.ready()
        if j == 3:
            gather_g.relay(3)
        gather_g.ready(j)
        rise = bell + pre * jnp.exp(-0.5 * pre * pre) * (1.0 / math.sqrt(2.0 * math.pi))
        gp[rows_of(j), :] = (dot_nt(gather_g.block(j), wd[...]) * rise).astype(BF)
        scatter_two.put(j, dot_nt(gp[rows_of(j), :], wu[...]))
        if j == 2:
            scatter_two.hop(1)
    scatter_two.hop(2)
    scatter_two.hop(3)

    sums = {
        name: TreeSum(net, own, land_y, hop, land_z, done, out, lsem.at[4 + n], name in "o")
        for n, (name, own, land_y, hop, land_z, done, out) in enumerate(
            (
                ("a", dw_a, ly_a, yh_a, lz_a, fin_a, out_a),
                ("b", dw_b, ly_b, yh_b, lz_b, fin_b, out_b),
                ("o", dw_o, ly_o, yh_o, lz_o, fin_o, out_o),
                ("d", dw_d, ly_d, yh_d, lz_d, fin_d, out_d),
                ("u", dw_u, ly_u, yh_u, lz_u, fin_u, out_u),
            )
        )
    }

    def columns(buf, z):
        part = buf[:, :, span(z, quarter)]
        return part.reshape(tokens, quarter)

    def grad_down(z, carry):
        sums["d"].put(z, dot_tn(hid[...], columns(g, z)))
        return carry

    def grad_up(z, carry):
        sums["u"].put(z, dot_tn(columns(e2, z), gp[...]))
        return carry

    def grad_qkv(z, carry):
        value = dot_tn(columns(e1, z), dqkv[...])
        sums["a"].put(z, value[:, :head])
        sums["b"].put(z, value[:, head:])
        return carry

    def grad_o(z, carry):
        sums["o"].put(z, dot_tn(mix_b[...], columns(gb, z)))
        return carry

    lax.fori_loop(0, 4, grad_down, 0)
    sums["d"].start()
    scatter_two.hop_on()
    lax.fori_loop(0, 4, grad_up, 0)
    sums["u"].start()

    grad = scatter_two.total()
    middle = mid[...]
    normed, inv = norm_stats(middle)
    spread = grad * vec[3:4, :]
    mean_one = jnp.sum(spread, axis=1, keepdims=True) * (1.0 / width)
    mean_two = jnp.sum(spread * normed, axis=1, keepdims=True) * (1.0 / width)
    cot_own = g[net.slot].astype(F32)
    total = cot_own + inv * (spread - mean_one - normed * mean_two)
    gmid[...] = total
    branch = total.astype(BF)
    gb[net.slot] = branch
    grad_all[...] = dot_nt(branch, w_out).astype(BF)
    swap_back = Exchange(
        net, lambda h: grad_all.at[:, span(h, head)], lambda q: gm.at[span(q, shard), :]
    )
    swap_back.start()
    gm[span(net.slot, shard), :] = grad_all[:, span(net.slot, head)]
    tok[2:3, :] = jnp.sum(grad * normed, axis=0, keepdims=True)
    tok[3:4, :] = jnp.sum(grad, axis=0, keepdims=True)
    tok[4:5, :] = jnp.sum(branch.astype(F32), axis=0, keepdims=True)
    tok[5:6, :] = jnp.sum(cot_own, axis=0, keepdims=True)
    tok[6:8, :] = jnp.zeros((2, width), F32)
    dk_acc[...] = jnp.zeros_like(dk_acc)
    dv_acc[...] = jnp.zeros_like(dv_acc)
    small[...] = jnp.zeros_like(small)
    small[0:1, :] = jnp.sum(gp[...].astype(F32), axis=0, keepdims=True)
    gather_gb = Gather(net, gb, 0)

    def tile_back(t, carry):
        rows = span(t, shard)
        grad_mix = gm[rows, :]
        probs = p_buf[rows, :]
        grad_probs = dot_nt(grad_mix, v_buf[...])
        centre = jnp.sum(mix[rows, :] * grad_mix.astype(F32), axis=1, keepdims=True)
        grad_scores = (probs.astype(F32) * (grad_probs - centre)).astype(BF)
        dqkv[rows, :head] = (dot_nn(grad_scores, k_buf[...]) * scale).astype(BF)
        dk_acc[...] += dot_tn(grad_scores, q_buf[rows, :])
        dv_acc[...] += dot_tn(probs, grad_mix)
        return carry

    swap_back.ready()
    gather_gb.start()
    lax.fori_loop(0, 8, tile_back, 0)
    dqkv[:, head : 2 * head] = (dk_acc[...] * scale).astype(BF)
    dqkv[:, 2 * head :] = dv_acc[...].astype(BF)

    scatter_four = Scatter(net, part_set_a, landings(1), shard // 2)
    scatter_two.left()
    for j in order:
        scatter_four.put(j, dot_nt(dqkv[rows_of(j), :], wq[...]))
    for j in (3, 1, 2):
        scatter_four.hop(j)
    sums["d"].across()
    gather_gb.relay(1)
    gather_gb.relay(2)
    lax.fori_loop(0, 4, grad_qkv, 0)
    scatter_four.hop_on()
    sums["u"].across()
    sums["b"].start()
    sums["a"].start()
    sums["d"].hand_out()

    small[1:2, :head] = jnp.sum(dqkv[:, :head].astype(F32), axis=0, keepdims=True)
    small[1:2, head : 2 * head] = jnp.sum(dqkv[:, 2 * head :].astype(F32), axis=0, keepdims=True)
    small_site = net.sites(6)
    others = ((1, 0), (0, 2), (1, 2))
    for n, (dy, dz) in enumerate(others):
        net.send(small, small_land.at[n], small_site + n, net.peer(dy=dy, dz=dz))
    gather_gb.relay(3)
    for j in range(4):
        gather_gb.ready(j)
    lax.fori_loop(0, 4, grad_o, 0)
    sums["o"].start()

    def send_out(src, dst, first):
        for z in range(4):
            net.send(
                src.at[:, span(z, quarter)],
                dst.at[span(net.slice, shard), :],
                first + z,
                (y * 2 + zh, z, net.col),
                recv_site=first + 4 + net.slice,
                skip=(row == z) & (k == zh),
            )

    def out_ready(dst, first):
        for s in range(4):
            net.landed(dst.at[span(s, shard), :], first + 4 + s)

    res_site, grad_site = net.sites(8), net.sites(8)
    grad = scatter_four.total()
    normed, inv = norm_stats(xs[...].astype(F32))
    tok[0:1, :] = jnp.sum(grad * normed, axis=0, keepdims=True)
    tok[1:2, :] = jnp.sum(grad, axis=0, keepdims=True)
    tok_site = net.sites(10)
    for n in range(1, 8):
        net.send(tok, tok_one.at[n - 1], tok_site + n - 1, net.rel(n))
    spread = grad * vec[0:1, :]
    mean_one = jnp.sum(spread, axis=1, keepdims=True) * (1.0 / width)
    mean_two = jnp.sum(spread * normed, axis=1, keepdims=True) * (1.0 / width)
    back_b[...] = (gmid[...] + inv * (spread - mean_one - normed * mean_two)).astype(BF)
    send_out(back_b, grad_out, grad_site)

    scatter_three = Scatter(net, part_set_b, landings(2), shard)
    for j in order:
        scatter_three.put(j, dot_nn(hid[rows_of(j), :], wd[...]))
    for j in (3, 1, 2):
        scatter_three.hop(j)
    sums["d"].pass_on()
    sums["b"].across()
    sums["a"].across()
    sums["u"].hand_out()
    scatter_three.hop_on()
    sums["o"].across()
    sums["b"].hand_out()
    sums["a"].hand_out()
    sums["u"].pass_on()
    sums["d"].share()
    sums["o"].hand_out()
    back_a[...] = (mid[...] + scatter_three.total() + vec[5:6, :]).astype(BF)
    send_out(back_a, res_out, res_site)
    sums["b"].pass_on()
    sums["a"].pass_on()
    sums["u"].share()
    acc = small[...]
    for n in range(3):
        net.landed(small_land.at[n], small_site + n)
        acc = acc + small_land[n]
    small_sum[...] = acc
    out_small[net.slice] = acc
    for n, (dk, dz) in enumerate(((1, 0), (0, 1), (1, 1))):
        net.send(
            small_sum, out_small.at[net.slice], small_site + 3 + n, net.peer(dk=dk, dz=dz)
        )
    acc = tok[...]
    for n in range(7):
        net.landed(tok_one.at[n], tok_site + n)
        acc = acc + tok_one[n]
    tok_sum[...] = acc
    tok_sent = [
        net.send(tok_sum, tok_two.at[n], tok_site + 7 + n, net.peer(dy=dy, dz=dz))
        for n, (dy, dz) in enumerate(others)
    ]
    gone = {id(remote) for remote in tok_sent}
    net.pending = [p for p in net.pending if id(p[0]) not in gone]
    sums["b"].share()
    sums["a"].share()
    sums["o"].pass_on()
    sums["o"].share()
    for n in range(3):
        net.landed(tok_two.at[n], tok_site + 7 + n)
        acc = acc + tok_two[n]
    for remote in tok_sent:
        remote.wait_send()
    tok_sum[...] = acc
    out_tok[...] = tok_sum[:, span(row, quarter)]
    for n, flip in enumerate((1, 2, 3)):
        net.landed(out_small.at[net.slice ^ flip], small_site + 3 + n)
    for one_sum in sums.values():
        one_sum.finish()
    out_ready(res_out, res_site)
    out_ready(grad_out, grad_site)
    net.drain()
    used.append(net.used)


def layer_on_square(
    inputs, cotangent, seg_parent, token_depth, ln1_gain, ln1_bias, w_qkv, b_qv, w_out, b_out,
    ln2_gain, ln2_bias, w_up, b_up, w_down, b_down,
):
    half_tokens, quarter = inputs.shape
    tokens, width = token_depth.shape[0], 4 * quarter
    shard = tokens // 8
    head = HD
    slices = w_qkv.shape[2] // head
    hidden = w_up.shape[1] // slices
    row = lax.axis_index("row")

    any_ = pl.BlockSpec(memory_space=pl.ANY)
    vmem = pl.BlockSpec(memory_space=pltpu.VMEM)
    sds = jax.ShapeDtypeStruct

    def vm(*dims, dtype=BF):
        return pltpu.VMEM(dims, dtype)

    blocks = {
        "a": (quarter, head), "b": (quarter, 2 * head), "o": (head, quarter),
        "d": (hidden, quarter), "u": (quarter, hidden),
    }
    names = ("a", "b", "o", "d", "u")
    halves = {n: (blocks[n][0] // 2, blocks[n][1]) for n in names}
    scratch = [
        vm(shard, width),
        *[vm(8, shard, width) for _ in range(5)],
        vm(width, 3 * head), vm(hidden, width), vm(width, hidden),
        vm(shard, width), vm(shard, width),
        vm(2, 16, 128, dtype=F32), vm(8, quarter, dtype=F32), vm(8, width, dtype=F32),
        vm(16, tokens, dtype=F32),
        *[vm(tokens, head) for _ in range(3)], vm(tokens, tokens),
        vm(tokens, head, dtype=F32), vm(tokens, head),
        *[
            spec
            for _ in range(2)
            for spec in (
                vm(8, shard, width), vm(2, shard, width),
                vm(shard, width, dtype=F32), vm(shard, width),
            )
        ],
        vm(3, 4, shard, width), vm(3, 2, shard, width), vm(3, shard, width),
        vm(tokens, hidden), vm(tokens, hidden),
        vm(tokens, head), vm(tokens, head, dtype=F32), vm(tokens, head, dtype=F32),
        vm(tokens, 3 * head),
        vm(shard, width, dtype=F32), vm(shard, width, dtype=F32), vm(shard, width), vm(shard, width),
        *[vm(2, 2, 2, *halves[n]) for n in names],
        *[vm(2, 2, *halves[n]) for n in names],
        *[vm(2, *halves[n]) for n in names],
        *[vm(2, *halves[n]) for n in names],
        *[vm(2, *halves[n]) for n in names],
        vm(8, width, dtype=F32), vm(7, 8, width, dtype=F32), vm(8, width, dtype=F32),
        vm(3, 8, width, dtype=F32),
        vm(8, hidden, dtype=F32), vm(3, 8, hidden, dtype=F32), vm(8, hidden, dtype=F32),
        pltpu.SemaphoreType.DMA((208,)), pltpu.SemaphoreType.DMA((208,)),
        pltpu.SemaphoreType.DMA((10,)),
    ]
    used = []
    outs = pl.pallas_call(
        functools.partial(layer_kernel, EPS, MASKED, used),
        out_shape=(
            sds((half_tokens, quarter), BF), sds((half_tokens, quarter), BF),
            *[sds((slices, *blocks[n]), BF) for n in names],
            sds((8, quarter), F32), sds((slices, 8, hidden), F32),
        ),
        in_specs=[any_] * 12 + [pl.BlockSpec(memory_space=pltpu.SMEM)] + [vmem] * 2,
        out_specs=(any_,) * 7 + (vmem,) * 2,
        scratch_shapes=scratch,
        compiler_params=pltpu.CompilerParams(
            collective_id=0, has_side_effects=True, vmem_limit_bytes=60 << 20
        ),
        name="tree_layer",
    )(
        inputs, cotangent, w_qkv.transpose(1, 0, 2), w_out, w_down, w_up,
        *[v.reshape(1, -1) for v in (ln1_gain, ln1_bias, b_out, ln2_gain, ln2_bias, b_down)],
        seg_parent, b_up.reshape(1, -1), b_qv,
    )
    result, input_grad, g_a, g_b, g_o, g_d, g_u, by_token, small = outs
    steps = 2

    def finish(res_in, grad_in, a_in, b_in, o_in, d_in, u_in, tok_in, small_in, *into):
        res, grad, q, o, d, u, tok_0, tok_1, tok_2, tok_3, tok_4, tok_5, up, qv = into
        res[...] = res_in[...].astype(F32)
        grad[...] = grad_in[...].astype(F32)
        o[...] = o_in[...].astype(F32)
        d[...] = d_in[...].astype(F32)
        for s in range(slices):
            u[:, s * hidden : (s + 1) * hidden] = u_in[s].astype(F32)
            at = slice(s * head, (s + 1) * head)
            q[0, :, at] = a_in[s].astype(F32)
            for n in range(2):
                q[n + 1, :, at] = b_in[s, :, n * head : (n + 1) * head].astype(F32)
            up[0:1, s * hidden : (s + 1) * hidden] = small_in[s, 0:1, :]
            for n in range(2):
                qv[n : n + 1, at] = small_in[
                    s, 1:2, n * head : (n + 1) * head
                ]
        for n, one in enumerate((tok_0, tok_1, tok_2, tok_3, tok_4, tok_5)):
            one[...] = tok_in[n : n + 1, :]

    def rows(*dims):
        return pl.BlockSpec((dims[0] // steps, *dims[1:]), lambda i: (i,) + (0,) * (len(dims) - 1))

    def middle(*dims):
        return pl.BlockSpec((dims[0], dims[1] // steps, *dims[2:]), lambda i: (0, i, 0))

    def fixed(*dims):
        return pl.BlockSpec(dims, lambda i: (0,) * len(dims))

    tall_o, tall_d = (slices * head, quarter), (slices * hidden, quarter)
    done = pl.pallas_call(
        finish,
        grid=(steps,),
        out_shape=(
            sds((half_tokens, quarter), F32), sds((half_tokens, quarter), F32),
            sds((3, quarter, slices * head), F32), sds(tall_o, F32), sds(tall_d, F32),
            sds((quarter, slices * hidden), F32), *[sds((1, quarter), F32)] * 6,
            sds((1, slices * hidden), F32), sds((2, slices * head), F32),
        ),
        in_specs=[
            rows(half_tokens, quarter), rows(half_tokens, quarter),
            middle(slices, *blocks["a"]), middle(slices, *blocks["b"]), rows(*tall_o), rows(*tall_d), middle(slices, *blocks["u"]),
            fixed(8, quarter), fixed(slices, 8, hidden),
        ],
        out_specs=(
            rows(half_tokens, quarter), rows(half_tokens, quarter),
            middle(3, quarter, slices * head), rows(*tall_o), rows(*tall_d),
            rows(quarter, slices * hidden), *[fixed(1, quarter)] * 6,
            fixed(1, slices * hidden), fixed(2, slices * head),
        ),
        compiler_params=pltpu.CompilerParams(vmem_limit_bytes=60 << 20),
        name="finish",
    )(
        result, input_grad, g_a, g_b, g_o.reshape(tall_o), g_d.reshape(tall_d), g_u, by_token, small
    )
    by_token = [v.reshape(-1) for v in done[6:12]]
    return (
        done[0], done[1], by_token[0], by_token[1], done[2].transpose(1, 0, 2), done[13], done[3], by_token[4],
        by_token[2], by_token[3], done[5], done[12].reshape(-1), done[4], by_token[5],
    )


def fits_square(mesh, *arrays):
    sizes = tuple(mesh.shape[name] for name in ("dp", "row", "col"))
    return (
        sizes == (4, 4, 2)
        and arrays[0].shape == (512, 256)
        and arrays[2].shape == (13,)
        and arrays[3].shape == (1024,)
        and arrays[6].shape == (256, 3, 512)
        and arrays[12].shape == (256, 2048)
    )


def solution(mesh):
    placed = (
        P(("dp", "col"), "row"),
        P(("dp", "col"), "row"),
        P("dp"),
        P("dp"),
        P("row"),
        P("row"),
        P("row", None, "col"),
        P(None, "col"),
        P("col", "row"),
        P("row"),
        P("row"),
        P("row"),
        P("row", "col"),
        P("col"),
        P("col", "row"),
        P("row"),
    )

    def on_each(*arrays):
        return (layer_on_square if fits_square(mesh, *arrays) else on_device)(*arrays)

    return jax.shard_map(
        on_each,
        mesh=mesh,
        in_specs=placed,
        out_specs=(
            P(("dp", "col"), "row"),
            P(("dp", "col"), "row"),
            P("row"),
            P("row"),
            P("row", None, "col"),
            P(None, "col"),
            P("col", "row"),
            P("row"),
            P("row"),
            P("row"),
            P("row", "col"),
            P("col"),
            P("col", "row"),
            P("row"),
        ),
        check_vma=False,
    )
```

```python
import functools
import math

import jax
import jax.numpy as jnp
from jax import lax
from jax.experimental import pallas as pl
from jax.experimental.pallas import tpu as pltpu
from jax.sharding import PartitionSpec as P

MESH = pl.DeviceIdType.MESH
BF = jnp.bfloat16
F32 = jnp.float32


HD = 128


EPS = 1e-05
MASKED = -1e30


def gelu_value(values):
    return 0.5 * values * (1.0 + jax.scipy.special.erf(values / math.sqrt(2.0)))


def gelu_slope(values):
    return 0.5 * (1.0 + jax.scipy.special.erf(values / math.sqrt(2.0))) + values * jnp.exp(
        -0.5 * values * values
    ) / math.sqrt(2.0 * math.pi)


def width_sums(first_term, second_term):
    return lax.psum((jnp.sum(first_term, axis=1), jnp.sum(second_term, axis=1)), "row")


def normalize(values, norm_gain, norm_bias, feature_count):
    row_total, square = width_sums(values, values * values)
    row_mean = row_total / feature_count
    inv_std = lax.rsqrt(square / feature_count - row_mean * row_mean + EPS)
    normed = (values - row_mean[:, None]) * inv_std[:, None]
    return (normed, inv_std, (normed * norm_gain + norm_bias).astype(jnp.bfloat16))


def normalize_back(upstream, normed, inv_std, norm_gain, feature_count):
    spread = upstream * norm_gain
    row_total, cross_sum = width_sums(spread, spread * normed)
    return inv_std[:, None] * (
        spread - row_total[:, None] / feature_count - normed * (cross_sum[:, None] / feature_count)
    )


def contract(left_op, right_op, flipped):
    if flipped:
        return lax.dot_general(
            left_op, right_op, (((1,), (1,)), ((), ())), preferred_element_type=jnp.float32
        )
    return jnp.dot(left_op, right_op, preferred_element_type=jnp.float32)


def outer_sum(left_op, right_op):
    return lax.dot_general(
        left_op, right_op, (((0,), (0,)), ((), ())), preferred_element_type=jnp.float32
    )


def across_rows(operand, weight_block, flipped):
    gathered = lax.all_gather(operand, "col", axis=0, tiled=True)
    row_count = gathered.shape[0] // lax.axis_size("row")

    def partial_term(row_start, row_num):
        return contract(gathered, weight_block, flipped)

    return (
        lax.psum_scatter(
            partial_term(jnp.int32(0), row_count * lax.axis_size("row")),
            "row",
            scatter_dimension=0,
            tiled=True,
        ),
        gathered,
    )


def across_cols(operand, weight_block, flipped):
    gathered = lax.all_gather(operand, "row", axis=0, tiled=True)
    row_count = gathered.shape[0] // lax.axis_size("col")

    def partial_term(row_start, row_num):
        return contract(gathered, weight_block, flipped)

    return (
        lax.psum_scatter(
            partial_term(jnp.int32(0), row_count * lax.axis_size("col")),
            "col",
            scatter_dimension=0,
            tiled=True,
        ),
        gathered,
    )


def tree_labels(seg_parent, token_depth):
    seg_count = seg_parent.shape[0]
    tree_len = token_depth.shape[0]
    seg_len = tree_len // 16
    slot_ids = jnp.arange(seg_count, dtype=jnp.int32)
    where_at = jnp.arange(tree_len, dtype=jnp.int32)
    segment = jnp.where(where_at < 4 * seg_len, 0, 1 + (where_at - 4 * seg_len) // seg_len)
    parent_local = seg_parent - lax.axis_index("dp") * seg_count
    parent_one = jnp.sum(
        jnp.where(segment[:, None] == slot_ids[None, :], parent_local[None, :], 0), axis=1
    )
    parent_two = jnp.sum(
        jnp.where(parent_one[:, None] == slot_ids[None, :], parent_local[None, :], 0), axis=1
    )
    return (segment, parent_one, parent_two, token_depth)


def block_scores(query_block, key_rows, labels, query_start, slopes):
    segment, parent_one, parent_two, token_depth = labels
    block_size = query_block.shape[0]
    query_seg = lax.dynamic_slice_in_dim(segment, query_start, block_size, 0)
    query_one = lax.dynamic_slice_in_dim(parent_one, query_start, block_size, 0)
    query_two = lax.dynamic_slice_in_dim(parent_two, query_start, block_size, 0)
    query_depth = lax.dynamic_slice_in_dim(token_depth, query_start, block_size, 0)
    allowed = (
        (segment[None, :] == query_seg[:, None])
        | (segment[None, :] == query_one[:, None])
        | (segment[None, :] == query_two[:, None])
    ) & (token_depth[None, :] <= query_depth[:, None])
    score_scale = query_block.shape[2] ** (-0.5)
    raw = jnp.einsum("qhd,khd->hqk", query_block, key_rows, preferred_element_type=jnp.float32)
    distance = (query_depth[:, None] - token_depth[None, :]).astype(jnp.float32)
    scores = raw * score_scale - slopes[:, None, None] * distance[None]
    return jnp.where(allowed[None], scores, MASKED)


def attention_forward(queries, key_rows, value_rows, labels, slopes, offset):
    block_size = min(512, queries.shape[0])
    blocks = queries.shape[0] // block_size

    def one_block(block_index):
        block_first = block_index * block_size
        query_block = lax.dynamic_slice_in_dim(queries, block_first, block_size, 0)
        scores = block_scores(query_block, key_rows, labels, offset + block_first, slopes)
        top_score = jnp.max(scores, axis=2, keepdims=True)
        weights = jnp.exp(scores - top_score)
        weight_total = jnp.sum(weights, axis=2, keepdims=True)
        probs = (weights / weight_total).astype(jnp.bfloat16)
        mixed = jnp.einsum("hqk,khd->qhd", probs, value_rows, preferred_element_type=jnp.float32)
        return (mixed, (top_score + jnp.log(weight_total))[:, :, 0])

    return lax.map(one_block, jnp.arange(blocks, dtype=jnp.int32))


def attention_backward(
    queries, key_rows, value_rows, grad_mixed, log_total, labels, slopes, offset
):
    block_size = min(512, queries.shape[0])
    blocks = queries.shape[0] // block_size
    score_scale = queries.shape[2] ** (-0.5)

    def one_block(carry, items):
        key_grad, value_grad = carry
        block_index, block_total = items
        block_first = block_index * block_size
        query_block = lax.dynamic_slice_in_dim(queries, block_first, block_size, 0)
        grad_block = lax.dynamic_slice_in_dim(grad_mixed, block_first, block_size, 0)
        scores = block_scores(query_block, key_rows, labels, offset + block_first, slopes)
        probs = jnp.exp(scores - block_total[:, :, None])
        grad_probs = jnp.einsum(
            "qhd,khd->hqk", grad_block, value_rows, preferred_element_type=jnp.float32
        )
        centre = jnp.sum(probs * grad_probs, axis=2, keepdims=True)
        grad_scores = (probs * (grad_probs - centre)).astype(jnp.bfloat16)
        query_grad = (
            jnp.einsum("hqk,khd->qhd", grad_scores, key_rows, preferred_element_type=jnp.float32)
            * score_scale
        )
        key_grad = (
            key_grad
            + jnp.einsum(
                "hqk,qhd->khd", grad_scores, query_block, preferred_element_type=jnp.float32
            )
            * score_scale
        )
        value_grad = value_grad + jnp.einsum(
            "hqk,qhd->khd",
            probs.astype(jnp.bfloat16),
            grad_block,
            preferred_element_type=jnp.float32,
        )
        return ((key_grad, value_grad), query_grad)

    empty = jnp.zeros(key_rows.shape, jnp.float32)
    (key_grad, value_grad), query_grad = lax.scan(
        one_block, (empty, empty), (jnp.arange(blocks, dtype=jnp.int32), log_total)
    )
    return (key_grad, value_grad, query_grad)


def on_device(
    inputs,
    cotangent,
    seg_parent,
    token_depth,
    ln1_gain,
    ln1_bias,
    w_qkv,
    b_qv,
    w_out,
    b_out,
    ln2_gain,
    ln2_bias,
    w_up,
    b_up,
    w_down,
    b_down,
):
    feature_count = inputs.shape[1] * lax.axis_size("row")
    col_width = w_qkv.shape[2]
    heads_here = col_width // HD
    qkv_flat = w_qkv.reshape(w_qkv.shape[0], 3 * col_width)
    labels = tree_labels(seg_parent, token_depth)
    heads_seen = lax.axis_index("col") * heads_here + jnp.arange(heads_here, dtype=jnp.int32)
    slopes = jnp.exp2(-(heads_seen + 1).astype(jnp.float32))
    states = inputs.astype(jnp.float32)
    normed_one, inv_one, entry_one = normalize(states, ln1_gain, ln1_bias, feature_count)
    projected, entry_one_all = across_rows(entry_one, qkv_flat, False)
    tok_rows = projected.shape[0]
    projected = projected.reshape(tok_rows, 3, col_width)
    queries = (projected[:, 0] + b_qv[0]).astype(jnp.bfloat16)
    keys_here = projected[:, 1].astype(jnp.bfloat16)
    values_here = (projected[:, 2] + b_qv[1]).astype(jnp.bfloat16)
    pair_all = lax.all_gather(
        jnp.stack([keys_here, values_here], axis=1), "row", axis=0, tiled=True
    )
    key_rows = pair_all[:, 0].reshape(-1, heads_here, HD)
    value_rows = pair_all[:, 1].reshape(-1, heads_here, HD)
    query_heads = queries.reshape(tok_rows, heads_here, HD)
    offset = lax.axis_index("row") * tok_rows
    mixed, log_total = attention_forward(query_heads, key_rows, value_rows, labels, slopes, offset)
    mixed = mixed.reshape(tok_rows, col_width).astype(jnp.bfloat16)
    attn_out, mixed_all = across_cols(mixed, w_out, False)
    middle = states + attn_out + b_out
    normed_two, inv_two, entry_two = normalize(middle, ln2_gain, ln2_bias, feature_count)
    hidden_pre, entry_two_all = across_rows(entry_two, w_up, False)
    hidden_pre = hidden_pre + b_up
    hidden = gelu_value(hidden_pre).astype(jnp.bfloat16)
    ffn_out, hidden_all = across_cols(hidden, w_down, False)
    result = middle + ffn_out + b_down
    grad_hidden, down_all = across_rows(cotangent, w_down, True)
    grad_pre = (grad_hidden * gelu_slope(hidden_pre)).astype(jnp.bfloat16)
    grad_entry_two, pre_all = across_cols(grad_pre, w_up, True)
    grad_middle = cotangent.astype(jnp.float32) + normalize_back(
        grad_entry_two, normed_two, inv_two, ln2_gain, feature_count
    )
    grad_branch = grad_middle.astype(jnp.bfloat16)
    grad_mixed, branch_all = across_rows(grad_branch, w_out, True)
    grad_mixed = grad_mixed.astype(jnp.bfloat16).reshape(tok_rows, heads_here, HD)
    key_grad, value_grad, query_grad = attention_backward(
        query_heads, key_rows, value_rows, grad_mixed, log_total, labels, slopes, offset
    )
    kv_grads = lax.psum_scatter(
        jnp.stack([key_grad.reshape(-1, col_width), value_grad.reshape(-1, col_width)], axis=1),
        "row",
        scatter_dimension=0,
        tiled=True,
    )
    grad_projected = jnp.stack(
        [
            query_grad.reshape(tok_rows, col_width).astype(jnp.bfloat16),
            kv_grads[:, 0].astype(jnp.bfloat16),
            kv_grads[:, 1].astype(jnp.bfloat16),
        ],
        axis=1,
    )
    grad_entry_one, proj_all = across_cols(
        grad_projected.reshape(tok_rows, 3 * col_width), qkv_flat, True
    )
    input_grad = grad_middle + normalize_back(
        grad_entry_one, normed_one, inv_one, ln1_gain, feature_count
    )
    proj_sums = jnp.sum(proj_all.astype(jnp.float32), axis=0).reshape(3, col_width)
    weight_terms = (
        outer_sum(entry_one_all, proj_all).reshape(w_qkv.shape),
        jnp.stack([proj_sums[0], proj_sums[2]], axis=0),
        outer_sum(mixed_all, branch_all),
        jnp.sum(branch_all.astype(jnp.float32), axis=0),
        outer_sum(entry_two_all, pre_all),
        jnp.sum(pre_all.astype(jnp.float32), axis=0),
        outer_sum(hidden_all, down_all),
        jnp.sum(down_all.astype(jnp.float32), axis=0),
    )
    (
        grad_w_qkv,
        grad_b_qv,
        grad_w_out,
        grad_b_out,
        grad_w_up,
        grad_b_up,
        grad_w_down,
        grad_b_down,
    ) = lax.psum(
        (
            weight_terms[0],
            weight_terms[1],
            weight_terms[2],
            weight_terms[3],
            weight_terms[4],
            weight_terms[5],
            weight_terms[6],
            weight_terms[7],
        ),
        "dp",
    )
    norm_terms = (
        jnp.sum(grad_entry_one * normed_one, axis=0),
        jnp.sum(grad_entry_one, axis=0),
        jnp.sum(grad_entry_two * normed_two, axis=0),
        jnp.sum(grad_entry_two, axis=0),
    )
    grad_ln1_gain, grad_ln1_bias, grad_ln2_gain, grad_ln2_bias = lax.psum(
        (norm_terms[0], norm_terms[1], norm_terms[2], norm_terms[3]), ("dp", "col")
    )
    return (
        result,
        input_grad,
        grad_ln1_gain,
        grad_ln1_bias,
        grad_w_qkv,
        grad_b_qv,
        grad_w_out,
        grad_b_out,
        grad_ln2_gain,
        grad_ln2_bias,
        grad_w_up,
        grad_b_up,
        grad_w_down,
        grad_b_down,
    )


RELS = (0, 4, 2, 6)


def dot_nn(a, b):
    return lax.dot_general(a, b, (((1,), (0,)), ((), ())), preferred_element_type=F32)


def dot_nt(a, b):
    return lax.dot_general(a, b, (((1,), (1,)), ((), ())), preferred_element_type=F32)


def dot_tn(a, b):
    return lax.dot_general(a, b, (((0,), (0,)), ((), ())), preferred_element_type=F32)


def span(index, size):
    return pl.ds(pl.multiple_of(index * size, size), size)


class Net:
    def __init__(self, ssem, rsem):
        self.dp = lax.axis_index("dp")
        self.row = lax.axis_index("row")
        self.col = lax.axis_index("col")
        self.y, self.k = self.dp // 2, self.dp % 2
        self.zh, self.zl = self.row // 2, self.row % 2
        self.x = self.col
        self.slot = self.x * 4 + self.zl * 2 + self.k
        self.chip = self.x * 2 + self.zl
        self.slice = self.zl * 2 + self.k
        self.ssem, self.rsem = ssem, rsem
        self.used = 0
        self.pending = []

    def sites(self, n):
        first = self.used
        self.used += n
        return first

    def peer(self, dy=0, dk=0, dz=0, dx=0):
        return (
            (self.y ^ dy) * 2 + (self.k ^ dk),
            self.row ^ dz,
            self.col ^ dx,
        )

    def rel(self, rel):
        return self.peer(dz=(rel >> 1) & 1, dx=rel >> 2, dk=rel & 1)

    def make(self, src, dst, site, device, recv_site=None):
        recv = site if recv_site is None else recv_site
        return pltpu.make_async_remote_copy(
            src_ref=src,
            dst_ref=dst,
            send_sem=self.ssem.at[site],
            recv_sem=self.rsem.at[recv],
            device_id=device,
            device_id_type=MESH,
        )

    def send(self, src, dst, site, device, recv_site=None, skip=None):
        remote = self.make(src, dst, site, device, recv_site)
        if skip is None:
            remote.start()
        else:
            recv = site if recv_site is None else recv_site

            @pl.when(skip)
            def _():
                pltpu.make_async_copy(src, dst, self.rsem.at[recv]).start()

            @pl.when(jnp.logical_not(skip))
            def _():
                remote.start()

        self.pending.append((remote, skip))
        return remote

    def landed(self, ref, site):
        self.make(ref, ref, site, self.peer(dk=1)).wait_recv()

    def drain(self, upto=None):
        for remote, skip in self.pending:
            if skip is None:
                remote.wait_send()
            else:

                @pl.when(jnp.logical_not(skip))
                def _(remote=remote):
                    remote.wait_send()

        self.pending = []


class Gather:
    def __init__(self, net, buf, by_low, over_y=False):
        self.net, self.buf, self.over_y = net, buf, over_y
        self.slot = net.x * 4 + net.y * 2 + net.k if over_y else net.slot
        self.first = net.sites(8)
        rows = buf.shape[1]
        self.low_rows = pl.ds(0, by_low) if by_low else None
        self.x_rows = pl.ds(by_low, rows - by_low) if by_low < rows else None

    def to(self, rel):
        low = (rel >> 1) & 1
        where = {"dy": low} if self.over_y else {"dz": low}
        return self.net.peer(dk=rel & 1, dx=rel >> 2, **where)

    def start(self):
        own = self.buf.at[self.slot]
        for n, rel in enumerate((1, 4, 2)):
            self.net.send(own, own, self.first + n, self.to(rel))

    def relay(self, j):
        net = self.net
        part = self.buf.at[self.slot ^ RELS[j]]
        if j < 3:
            net.landed(part, self.first + j)
            rows, rel = ((self.low_rows, 2), (self.x_rows, 4))[j - 1]
            if rows is not None:
                some = part.at[rows, :]
                net.send(some, some, self.first + 2 + j, self.to(rel))
        else:
            for n, rows in enumerate((self.low_rows, self.x_rows)):
                if rows is not None:
                    net.landed(part.at[rows, :], self.first + 3 + n)
        net.send(part, part, self.first + 4 + j, self.to(1))

    def ready(self, j):
        part = self.buf.at[self.slot ^ RELS[j] ^ 1]
        self.net.landed(part, self.first if j == 0 else self.first + 4 + j)

    def block(self, j):
        chip = (self.slot ^ RELS[j]) // 2
        both = self.buf[pl.ds(chip * 2, 2)]
        return both.reshape(2 * both.shape[1], both.shape[2])


class Exchange:
    def __init__(self, net, src_of, dst_of):
        self.net, self.src_of, self.dst_of = net, src_of, dst_of
        self.first = net.sites(7)

    def start(self):
        net = self.net
        for n in (6, 7, 4, 5, 2, 3, 1):
            net.send(
                self.src_of(net.slot ^ n), self.dst_of(net.slot), self.first + n - 1, net.rel(n)
            )

    def ready(self):
        net = self.net
        for n in range(1, 8):
            net.landed(self.dst_of(net.slot ^ n), self.first + n - 1)


class Scatter:
    def __init__(self, net, bufs, land, cut):
        self.net, self.cut = net, cut
        self.part, self.hops, self.kept, self.last = bufs
        self.one, self.two, self.three = land
        self.first = net.sites(10)
        self.sent = []
        rows = self.part.shape[1]
        self.ways = [
            way
            for way in ((0, pl.ds(0, cut), 1, 2), (1, pl.ds(cut, rows - cut), 2, 1))
            if way[1].size
        ]

    def send(self, src, dst, site, rel):
        self.sent.append(self.net.send(src, dst, self.first + site, self.net.rel(rel)))

    def put(self, j, value):
        net = self.net
        chip = net.chip ^ (RELS[j] >> 1)
        shard = self.part.shape[1]
        self.part[pl.ds(chip * 2, 2)] = value.astype(BF).reshape(2, shard, value.shape[1])
        self.send(self.part.at[chip * 2 + (1 - net.k)], self.one.at[j], j, 1)

    def chip_sum(self, j):
        net = self.net
        chip = net.chip ^ (RELS[j] >> 1)
        net.landed(self.one.at[j], self.first + j)
        return self.part[chip * 2 + net.k].astype(F32) + self.one[j].astype(F32)

    def hop(self, j):
        value = self.chip_sum(j)
        for n, rows, near, far in self.ways:
            mine = value[rows.start : rows.start + rows.size]
            if j == far:
                self.kept[rows, :] = mine
            else:
                place = 0 if j == near else 1
                self.hops[place, rows, :] = mine.astype(BF)
                self.send(
                    self.hops.at[place, rows, :],
                    self.two.at[place, rows, :],
                    4 + 2 * n + place,
                    RELS[near],
                )

    def hop_on(self):
        net = self.net
        for n, rows, near, far in self.ways:
            net.landed(self.two.at[1, rows, :], self.first + 5 + 2 * n)
            self.last[rows, :] = (
                self.kept[rows, :] + self.two[1, rows, :].astype(F32)
            ).astype(BF)
            self.send(self.last.at[rows, :], self.three.at[rows, :], 8 + n, RELS[far])

    def left(self):
        for remote in self.sent:
            remote.wait_send()
        mine = {id(remote) for remote in self.sent}
        self.net.pending = [p for p in self.net.pending if id(p[0]) not in mine]

    def total(self):
        net = self.net
        value = self.chip_sum(0)
        for n, rows, near, far in self.ways:
            net.landed(self.two.at[0, rows, :], self.first + 4 + 2 * n)
            net.landed(self.three.at[rows, :], self.first + 8 + n)
        return value + self.two[0].astype(F32) + self.three[...].astype(F32)


class TreeSum:
    def __init__(self, net, own, land_y, hop, land_z, done, out, local_sem, direct):
        self.net, self.own, self.land_y = net, own, land_y
        self.hop_buf, self.land_z, self.done, self.out = hop, land_z, done, out
        self.first = net.sites(7)
        self.local_sem, self.direct = local_sem, direct

    def put(self, z, value):
        rows = self.own.shape[3]
        self.own[z // 2, z % 2] = value.astype(BF).reshape(2, rows, value.shape[1])

    def half(self, piece, which):
        return self.out.at[piece, span(which, self.own.shape[3]), :]

    def start(self):
        net = self.net
        net.send(self.own.at[:, :, 1 - net.y], self.land_y, self.first, net.peer(dy=1))

    def across(self):
        net = self.net
        net.landed(self.land_y, self.first)
        far = 1 - net.zh
        for low in (0, 1):
            self.hop_buf[low] = (
                self.own[far, low, net.y].astype(F32) + self.land_y[far, low].astype(F32)
            ).astype(BF)
        net.send(self.hop_buf, self.land_z, self.first + 1, net.peer(dz=2))

    def hand_out(self):
        net = self.net
        net.landed(self.land_z, self.first + 1)
        for low in (0, 1):
            self.done[low] = (
                self.own[net.zh, low, net.y].astype(F32)
                + self.land_y[net.zh, low].astype(F32)
                + self.land_z[low].astype(F32)
            ).astype(BF)
        place = self.half(net.slice, net.y)
        net.send(self.done.at[1 - net.zl], place, self.first + 2, net.peer(dz=1))
        net.send(self.done.at[net.zl], place, self.first + 3, net.peer(dy=1))
        if self.direct:
            net.send(self.done.at[1 - net.zl], place, self.first + 4, net.peer(dy=1, dz=1))
        self.kept = pltpu.make_async_copy(self.done.at[net.zl], place, self.local_sem)
        self.kept.start()

    def pass_on(self):
        net = self.net
        part = self.half(net.slice ^ 2, net.y)
        net.landed(part, self.first + 2)
        if not self.direct:
            net.send(part, part, self.first + 4, net.peer(dy=1))

    def share(self):
        net = self.net
        self.kept.wait()
        for n, piece in enumerate((net.slice, net.slice ^ 2)):
            net.landed(self.half(piece, 1 - net.y), self.first + 3 + n)
            part = self.out.at[piece]
            net.send(part, part, self.first + 5 + n, net.rel(1))

    def finish(self):
        net = self.net
        for n, piece in enumerate((net.slice ^ 1, net.slice ^ 3)):
            net.landed(self.out.at[piece], self.first + 5 + n)


def layer_kernel(eps, masked, used, *refs):
    (
        inp, cot, w_q, w_o, w_d, w_u, vec_0, vec_1, vec_2, vec_3, vec_4, vec_5, parents, b_up, b_qv,
        res_out, grad_out, out_a, out_b, out_o, out_d, out_u, out_tok, out_small,
        xs, e1, g, e2, gb, wf, wq, wd, wu, mixed_all, grad_all, links, vec_in, vec, bias,
        q_buf, k_buf, v_buf, p_buf, mix, mix_b,
        part_a, hops_a, kept_a, last_a, part_b, hops_b, kept_b, last_b, one, two, three,
        hid, gp, gm, dk_acc, dv_acc, dqkv, mid, gmid, back_a, back_b,
        dw_a, dw_b, dw_o, dw_d, dw_u, ly_a, ly_b, ly_o, ly_d, ly_u,
        yh_a, yh_b, yh_o, yh_d, yh_u, lz_a, lz_b, lz_o, lz_d, lz_u,
        fin_a, fin_b, fin_o, fin_d, fin_u,
        tok, tok_one, tok_sum, tok_two, small, small_land, small_sum,
        ssem, rsem, lsem,
    ) = refs
    net = Net(ssem, rsem)
    y, k, zh, zl, x, row = net.y, net.k, net.zh, net.zl, net.x, net.row
    shard, width = xs.shape
    tokens = 8 * shard
    quarter = width // 4
    head = q_buf.shape[1]

    greet = [
        net.peer(dy=dy, dk=dk, dz=dz)
        for dy in (0, 1)
        for dk in (0, 1)
        for dz in (0, 1, 2, 3)
        if dy + dk + dz
    ]
    greet += [net.peer(dk=dk, dz=dz, dx=1) for dk in (0, 1) for dz in (0, 1)]
    barrier = pltpu.get_barrier_semaphore()
    for device in greet:
        pl.semaphore_signal(barrier, inc=1, device_id=device, device_id_type=MESH)
    vec_parts = (vec_0, vec_1, vec_2, vec_3, vec_4, vec_5)
    for n, part in enumerate(vec_parts):
        pltpu.make_async_copy(part, vec_in.at[pl.ds(n, 1), :], lsem.at[9]).start()
    seg_count = parents.shape[0]
    half_at = lax.broadcasted_iota(jnp.int32, links.shape[1:], 0)
    mine = jnp.zeros(links.shape[1:], F32)
    for s in range(1, seg_count):
        parent = parents[s] - net.dp * seg_count
        mine = jnp.where(half_at == s + 3, parent.astype(F32), mine)
    links[0] = mine

    pl.semaphore_wait(barrier, len(greet))

    def send_home(src, dst_of, first):
        for s in range(4):
            low, core = s // 2, s % 2
            target = 2 * k + low
            net.send(
                src.at[span(s, shard), :],
                dst_of(s).at[:, span(row, quarter)],
                first + s,
                (y * 2 + core, target, net.col),
                recv_site=first + 4 + row,
                skip=(target == row) & (k == core),
            )

    def home_ready(dst, first):
        for z in range(4):
            net.landed(dst.at[:, span(z, quarter)], first + 4 + z)

    vec_site = net.sites(3)
    pltpu.make_async_copy(vec_in.at[pl.ds(0, 6), :], vec_in.at[pl.ds(0, 6), :], lsem.at[9]).wait()
    for o in (1, 2, 3):
        net.send(
            vec_in.at[pl.ds(0, 8), :], vec.at[:, span(row, quarter)], vec_site + o - 1, net.peer(dz=o)
        )
    links_site = net.sites(1)
    net.send(links.at[0], links.at[1], links_site, net.rel(1))
    home_x, home_g = net.sites(8), net.sites(8)
    send_home(inp, lambda s: xs, home_x)

    def slices(w_ref, full, axis):
        if axis == 0:
            rows = full.shape[0] // 4
            return rows, lambda z: full.at[span(z, rows), :]
        cols = full.shape[1] // 4
        return full.shape[0], lambda z: full.at[:, span(z, cols)]

    class Weight:
        def __init__(self, src_of, full, axis, local):
            self.src_of, self.full = src_of, full
            self.rows, self.place = slices(None, full, axis)
            self.first = net.sites(6)
            self.local = local

        def half(self, ref, which):
            rows = self.rows // 2
            return ref.at[span(which, rows), :]

        def start(self):
            own = pltpu.make_async_copy(
                self.place(row), self.place(row), lsem.at[self.local]
            )
            for src, cols in self.src_of(net.slice):
                pltpu.make_async_copy(
                    src, self.place(row).at[:, cols], lsem.at[self.local]
                ).start()
            for o in (1, 2, 3):
                far = (zl ^ (o & 1)) * 2 + k
                for src, cols in self.src_of(far):
                    net.send(
                        self.half(src, y),
                        self.half(self.place(row), y).at[:, cols],
                        self.first + o - 1,
                        net.peer(dz=o),
                    )
            self.own = own

        def relay(self):
            for o in (1, 2, 3):
                part = self.half(self.place(row ^ o), y)
                net.landed(part, self.first + o - 1)
                net.send(part, part, self.first + 2 + o, net.peer(dy=1))

        def ready(self):
            for o in (1, 2, 3):
                net.landed(self.half(self.place(row ^ o), 1 - y), self.first + 2 + o)
            self.own.wait()

    hidden = hid.shape[1]
    whole = slice(None)

    def qkv_parts(s):
        return [
            (w_q.at[n, :, span(s, head)], pl.ds(n * head, head)) for n in range(3)
        ]

    weight_q = Weight(qkv_parts, wq, 0, 0)
    weight_d = Weight(lambda s: [(w_d.at[span(s, hidden), :], whole)], wd, 1, 2)
    weight_u = Weight(lambda s: [(w_u.at[:, span(s, hidden)], whole)], wu, 0, 3)

    gather_w = Gather(net, wf, shard // 2, over_y=True)
    wf_own = wf.at[gather_w.slot]
    wf_site = net.sites(3)
    wf_src = w_o.at[span(y * 2 + k, shard), :]

    vec[:, span(row, quarter)] = vec_in[...]
    for o in (1, 2, 3):
        net.landed(vec.at[:, span(row ^ o, quarter)], vec_site + o - 1)

    def norm_stats(values):
        mean = jnp.sum(values, axis=1, keepdims=True) * (1.0 / width)
        msq = jnp.sum(values * values, axis=1, keepdims=True) * (1.0 / width)
        inv = lax.rsqrt(msq - mean * mean + eps)
        return (values - mean) * inv, inv

    weight_q.start()
    home_ready(xs, home_x)
    normed, _ = norm_stats(xs[...].astype(F32))
    e1[net.slot] = (normed * vec[0:1, :] + vec[1:2, :]).astype(BF)
    gather_e1 = Gather(net, e1, 0)
    gather_e1.start()
    wf_copy = pltpu.make_async_copy(wf_src, wf_own.at[:, span(row, quarter)], lsem.at[1])
    wf_copy.start()
    for o in (1, 2, 3):
        net.send(wf_src, wf_own.at[:, span(row, quarter)], wf_site + o - 1, net.peer(dz=o))
    gather_g = Gather(net, g, 0)
    send_home(cot, lambda s: g.at[x * 4 + s], home_g)
    weight_q.relay()

    net.landed(links.at[1], links_site)
    parent = jnp.where(zh == k, links[0], links[1])[:, 0:1]
    seg_len = tokens // 16
    key_at = lax.broadcasted_iota(jnp.int32, (1, tokens), 1)
    key_half = key_at // seg_len
    key_seg = jnp.maximum(key_half - 3, 0)
    half_row = lax.broadcasted_iota(jnp.int32, (16, 1), 0)
    seg_row = jnp.maximum(half_row - 3, 0)
    key_parent = jnp.sum(jnp.where(key_half == half_row, parent, 0.0), axis=0, keepdims=True)
    start = jnp.where(key_parent > 0.0, 5 * seg_len, 4 * seg_len)
    depth = jnp.where(key_seg == 0, key_at, start + key_at % seg_len)
    allowed = (key_seg == 0) | (key_seg == seg_row) | (key_seg == parent.astype(jnp.int32))
    exponent = jnp.full((1, tokens), -(x * 4 + net.slice + 1), jnp.int32).astype(F32)
    slope = jnp.exp2(exponent)
    bias[...] = jnp.where(allowed, slope * depth.astype(F32), masked)

    b_q = b_qv[0:1, span(net.slice, head)]
    b_v = b_qv[1:2, span(net.slice, head)]
    gather_e1.relay(1)
    gather_e1.relay(2)
    weight_u.start()
    weight_d.start()
    weight_q.ready()
    for j in range(4):
        if j == 3:
            for o in (1, 2, 3):
                net.landed(wf_own.at[:, span(row ^ o, quarter)], wf_site + o - 1)
            wf_copy.wait()
            gather_w.start()
            gather_e1.relay(3)
        gather_e1.ready(j)
        rows = pl.ds((net.chip ^ (RELS[j] >> 1)) * 2 * shard, 2 * shard)
        proj = dot_nn(gather_e1.block(j), wq[...])
        q_buf[rows, :] = (proj[:, :head] + b_q).astype(BF)
        k_buf[rows, :] = proj[:, head : 2 * head].astype(BF)
        v_buf[rows, :] = (proj[:, 2 * head :] + b_v).astype(BF)

    scale = head ** (-0.5)

    def attend(i, carry):
        first = pl.multiple_of(i * shard, shard)
        raw = dot_nt(q_buf[pl.ds(first, shard), :], k_buf[...])
        parts = []
        for half in (0, 1):
            at = 2 * i + half
            seg = jnp.maximum(at - 3, 0)
            later = jnp.where(key_seg == seg, key_at, -1)
            query_at = first + half * seg_len + lax.broadcasted_iota(jnp.int32, (seg_len, 1), 0)
            scores = raw[half * seg_len : (half + 1) * seg_len] * scale + bias[pl.ds(at, 1), :]
            scores = jnp.where(later > query_at, masked, scores)
            top = jnp.max(scores, axis=1, keepdims=True)
            weights = jnp.exp(scores - top)
            norm = 1.0 / jnp.sum(weights, axis=1, keepdims=True)
            parts.append((weights * norm).astype(BF))
        probs = jnp.concatenate(parts, axis=0)
        p_buf[pl.ds(first, shard), :] = probs
        mixed = dot_nn(probs, v_buf[...])
        mix[pl.ds(first, shard), :] = mixed
        mix_b[pl.ds(first, shard), :] = mixed.astype(BF)
        return carry

    lax.fori_loop(0, 6, attend, 0)
    gather_w.relay(1)
    gather_w.relay(2)
    lax.fori_loop(6, 8, attend, 0)

    def rows_of(j):
        return span(net.chip ^ (RELS[j] >> 1), 2 * shard)

    order = (3, 1, 2, 0)
    part_set_a = (part_a, hops_a, kept_a, last_a)
    part_set_b = (part_b, hops_b, kept_b, last_b)

    def landings(n):
        return (one.at[n], two.at[n], three.at[n])

    swap = Exchange(
        net, lambda q: mix_b.at[span(q, shard), :], lambda h: mixed_all.at[:, span(h, head)]
    )
    swap.start()
    mixed_all[:, span(net.slot, head)] = mix_b[span(net.slot, shard), :]
    home_ready(g.at[net.slot], home_g)
    gather_g.start()
    gather_w.relay(3)
    weight_u.relay()
    for j in range(4):
        gather_w.ready(j)
    swap.ready()
    w_out = wf[...].reshape(width, width)

    middle = xs[...].astype(F32) + dot_nn(mixed_all[...], w_out) + vec[2:3, :]
    mid[...] = middle
    normed, _ = norm_stats(middle)
    e2[net.slot] = (normed * vec[3:4, :] + vec[4:5, :]).astype(BF)
    gather_e2 = Gather(net, e2, shard // 2)
    gather_e2.start()
    weight_d.relay()
    gather_g.relay(1)
    gather_g.relay(2)
    gather_e2.relay(1)
    gather_e2.relay(2)


    b_u = b_up[0:1, span(net.slice, hidden)]
    weight_u.ready()
    scatter_two = Scatter(net, part_set_a, landings(0), shard // 2)
    for j in range(4):
        if j == 3:
            gather_e2.relay(3)
        gather_e2.ready(j)
        pre = dot_nn(gather_e2.block(j), wu[...]) + b_u
        bell = 0.5 * (1.0 + lax.erf(pre * (1.0 / math.sqrt(2.0))))
        hid[rows_of(j), :] = (pre * bell).astype(BF)
        if j == 0:
            weight_d.ready()
        if j == 3:
            gather_g.relay(3)
        gather_g.ready(j)
        rise = bell + pre * jnp.exp(-0.5 * pre * pre) * (1.0 / math.sqrt(2.0 * math.pi))
        gp[rows_of(j), :] = (dot_nt(gather_g.block(j), wd[...]) * rise).astype(BF)
        scatter_two.put(j, dot_nt(gp[rows_of(j), :], wu[...]))
        if j == 2:
            scatter_two.hop(1)
    scatter_two.hop(2)
    scatter_two.hop(3)

    sums = {
        name: TreeSum(net, own, land_y, hop, land_z, done, out, lsem.at[4 + n], name in "o")
        for n, (name, own, land_y, hop, land_z, done, out) in enumerate(
            (
                ("a", dw_a, ly_a, yh_a, lz_a, fin_a, out_a),
                ("b", dw_b, ly_b, yh_b, lz_b, fin_b, out_b),
                ("o", dw_o, ly_o, yh_o, lz_o, fin_o, out_o),
                ("d", dw_d, ly_d, yh_d, lz_d, fin_d, out_d),
                ("u", dw_u, ly_u, yh_u, lz_u, fin_u, out_u),
            )
        )
    }

    def columns(buf, z):
        part = buf[:, :, span(z, quarter)]
        return part.reshape(tokens, quarter)

    def grad_down(z, carry):
        sums["d"].put(z, dot_tn(hid[...], columns(g, z)))
        return carry

    def grad_up(z, carry):
        sums["u"].put(z, dot_tn(columns(e2, z), gp[...]))
        return carry

    def grad_qkv(z, carry):
        value = dot_tn(columns(e1, z), dqkv[...])
        sums["a"].put(z, value[:, :head])
        sums["b"].put(z, value[:, head:])
        return carry

    def grad_o(z, carry):
        sums["o"].put(z, dot_tn(mix_b[...], columns(gb, z)))
        return carry

    lax.fori_loop(0, 4, grad_down, 0)
    sums["d"].start()
    scatter_two.hop_on()
    lax.fori_loop(0, 4, grad_up, 0)
    sums["u"].start()

    grad = scatter_two.total()
    middle = mid[...]
    normed, inv = norm_stats(middle)
    spread = grad * vec[3:4, :]
    mean_one = jnp.sum(spread, axis=1, keepdims=True) * (1.0 / width)
    mean_two = jnp.sum(spread * normed, axis=1, keepdims=True) * (1.0 / width)
    cot_own = g[net.slot].astype(F32)
    total = cot_own + inv * (spread - mean_one - normed * mean_two)
    gmid[...] = total
    branch = total.astype(BF)
    gb[net.slot] = branch
    grad_all[...] = dot_nt(branch, w_out).astype(BF)
    swap_back = Exchange(
        net, lambda h: grad_all.at[:, span(h, head)], lambda q: gm.at[span(q, shard), :]
    )
    swap_back.start()
    gm[span(net.slot, shard), :] = grad_all[:, span(net.slot, head)]
    tok[2:3, :] = jnp.sum(grad * normed, axis=0, keepdims=True)
    tok[3:4, :] = jnp.sum(grad, axis=0, keepdims=True)
    tok[4:5, :] = jnp.sum(branch.astype(F32), axis=0, keepdims=True)
    tok[5:6, :] = jnp.sum(cot_own, axis=0, keepdims=True)
    tok[6:8, :] = jnp.zeros((2, width), F32)
    dk_acc[...] = jnp.zeros_like(dk_acc)
    dv_acc[...] = jnp.zeros_like(dv_acc)
    small[...] = jnp.zeros_like(small)
    small[0:1, :] = jnp.sum(gp[...].astype(F32), axis=0, keepdims=True)
    gather_gb = Gather(net, gb, 0)

    def tile_back(t, carry):
        rows = span(t, shard)
        grad_mix = gm[rows, :]
        probs = p_buf[rows, :]
        grad_probs = dot_nt(grad_mix, v_buf[...])
        centre = jnp.sum(mix[rows, :] * grad_mix.astype(F32), axis=1, keepdims=True)
        grad_scores = (probs.astype(F32) * (grad_probs - centre)).astype(BF)
        dqkv[rows, :head] = (dot_nn(grad_scores, k_buf[...]) * scale).astype(BF)
        dk_acc[...] += dot_tn(grad_scores, q_buf[rows, :])
        dv_acc[...] += dot_tn(probs, grad_mix)
        return carry

    swap_back.ready()
    gather_gb.start()
    lax.fori_loop(0, 8, tile_back, 0)
    dqkv[:, head : 2 * head] = (dk_acc[...] * scale).astype(BF)
    dqkv[:, 2 * head :] = dv_acc[...].astype(BF)

    scatter_four = Scatter(net, part_set_a, landings(1), shard // 2)
    scatter_two.left()
    for j in order:
        scatter_four.put(j, dot_nt(dqkv[rows_of(j), :], wq[...]))
    for j in (3, 1, 2):
        scatter_four.hop(j)
    sums["d"].across()
    gather_gb.relay(1)
    gather_gb.relay(2)
    lax.fori_loop(0, 4, grad_qkv, 0)
    scatter_four.hop_on()
    sums["u"].across()
    sums["b"].start()
    sums["a"].start()
    sums["d"].hand_out()

    small[1:2, :head] = jnp.sum(dqkv[:, :head].astype(F32), axis=0, keepdims=True)
    small[1:2, head : 2 * head] = jnp.sum(dqkv[:, 2 * head :].astype(F32), axis=0, keepdims=True)
    small_site = net.sites(6)
    others = ((1, 0), (0, 2), (1, 2))
    for n, (dy, dz) in enumerate(others):
        net.send(small, small_land.at[n], small_site + n, net.peer(dy=dy, dz=dz))
    gather_gb.relay(3)
    for j in range(4):
        gather_gb.ready(j)
    lax.fori_loop(0, 4, grad_o, 0)
    sums["o"].start()

    def send_out(src, dst, first):
        for z in range(4):
            net.send(
                src.at[:, span(z, quarter)],
                dst.at[span(net.slice, shard), :],
                first + z,
                (y * 2 + zh, z, net.col),
                recv_site=first + 4 + net.slice,
                skip=(row == z) & (k == zh),
            )

    def out_ready(dst, first):
        for s in range(4):
            net.landed(dst.at[span(s, shard), :], first + 4 + s)

    res_site, grad_site = net.sites(8), net.sites(8)
    grad = scatter_four.total()
    normed, inv = norm_stats(xs[...].astype(F32))
    tok[0:1, :] = jnp.sum(grad * normed, axis=0, keepdims=True)
    tok[1:2, :] = jnp.sum(grad, axis=0, keepdims=True)
    tok_site = net.sites(10)
    for n in range(1, 8):
        net.send(tok, tok_one.at[n - 1], tok_site + n - 1, net.rel(n))
    spread = grad * vec[0:1, :]
    mean_one = jnp.sum(spread, axis=1, keepdims=True) * (1.0 / width)
    mean_two = jnp.sum(spread * normed, axis=1, keepdims=True) * (1.0 / width)
    back_b[...] = (gmid[...] + inv * (spread - mean_one - normed * mean_two)).astype(BF)
    send_out(back_b, grad_out, grad_site)

    scatter_three = Scatter(net, part_set_b, landings(2), shard)
    for j in order:
        scatter_three.put(j, dot_nn(hid[rows_of(j), :], wd[...]))
    for j in (3, 1, 2):
        scatter_three.hop(j)
    sums["d"].pass_on()
    sums["b"].across()
    sums["a"].across()
    sums["u"].hand_out()
    scatter_three.hop_on()
    sums["o"].across()
    sums["b"].hand_out()
    sums["a"].hand_out()
    sums["u"].pass_on()
    sums["d"].share()
    sums["o"].hand_out()
    acc = tok[...]
    for n in range(7):
        net.landed(tok_one.at[n], tok_site + n)
        acc = acc + tok_one[n]
    tok_sum[...] = acc
    tok_sent = [
        net.send(tok_sum, tok_two.at[n], tok_site + 7 + n, net.peer(dy=dy, dz=dz))
        for n, (dy, dz) in enumerate(others)
    ]
    gone = {id(remote) for remote in tok_sent}
    net.pending = [p for p in net.pending if id(p[0]) not in gone]
    back_a[...] = (mid[...] + scatter_three.total() + vec[5:6, :]).astype(BF)
    send_out(back_a, res_out, res_site)
    sums["b"].pass_on()
    sums["a"].pass_on()
    sums["u"].share()
    acc_s = small[...]
    for n in range(3):
        net.landed(small_land.at[n], small_site + n)
        acc_s = acc_s + small_land[n]
    small_sum[...] = acc_s
    out_small[net.slice] = acc_s
    for n, (dk, dz) in enumerate(((1, 0), (0, 1), (1, 1))):
        net.send(
            small_sum, out_small.at[net.slice], small_site + 3 + n, net.peer(dk=dk, dz=dz)
        )
    sums["b"].share()
    sums["a"].share()
    sums["o"].pass_on()
    sums["o"].share()
    for n in range(3):
        net.landed(tok_two.at[n], tok_site + 7 + n)
        acc = acc + tok_two[n]
    for remote in tok_sent:
        remote.wait_send()
    tok_sum[...] = acc
    out_tok[...] = tok_sum[:, span(row, quarter)]
    for n, flip in enumerate((1, 2, 3)):
        net.landed(out_small.at[net.slice ^ flip], small_site + 3 + n)
    for one_sum in sums.values():
        one_sum.finish()
    out_ready(res_out, res_site)
    out_ready(grad_out, grad_site)
    net.drain()
    used.append(net.used)


def layer_on_square(
    inputs, cotangent, seg_parent, token_depth, ln1_gain, ln1_bias, w_qkv, b_qv, w_out, b_out,
    ln2_gain, ln2_bias, w_up, b_up, w_down, b_down,
):
    half_tokens, quarter = inputs.shape
    tokens, width = token_depth.shape[0], 4 * quarter
    shard = tokens // 8
    head = HD
    slices = w_qkv.shape[2] // head
    hidden = w_up.shape[1] // slices
    row = lax.axis_index("row")

    any_ = pl.BlockSpec(memory_space=pl.ANY)
    vmem = pl.BlockSpec(memory_space=pltpu.VMEM)
    sds = jax.ShapeDtypeStruct

    def vm(*dims, dtype=BF):
        return pltpu.VMEM(dims, dtype)

    blocks = {
        "a": (quarter, head), "b": (quarter, 2 * head), "o": (head, quarter),
        "d": (hidden, quarter), "u": (quarter, hidden),
    }
    names = ("a", "b", "o", "d", "u")
    halves = {n: (blocks[n][0] // 2, blocks[n][1]) for n in names}
    scratch = [
        vm(shard, width),
        *[vm(8, shard, width) for _ in range(5)],
        vm(width, 3 * head), vm(hidden, width), vm(width, hidden),
        vm(shard, width), vm(shard, width),
        vm(2, 16, 128, dtype=F32), vm(8, quarter, dtype=F32), vm(8, width, dtype=F32),
        vm(16, tokens, dtype=F32),
        *[vm(tokens, head) for _ in range(3)], vm(tokens, tokens),
        vm(tokens, head, dtype=F32), vm(tokens, head),
        *[
            spec
            for _ in range(2)
            for spec in (
                vm(8, shard, width), vm(2, shard, width),
                vm(shard, width, dtype=F32), vm(shard, width),
            )
        ],
        vm(3, 4, shard, width), vm(3, 2, shard, width), vm(3, shard, width),
        vm(tokens, hidden), vm(tokens, hidden),
        vm(tokens, head), vm(tokens, head, dtype=F32), vm(tokens, head, dtype=F32),
        vm(tokens, 3 * head),
        vm(shard, width, dtype=F32), vm(shard, width, dtype=F32), vm(shard, width), vm(shard, width),
        *[vm(2, 2, 2, *halves[n]) for n in names],
        *[vm(2, 2, *halves[n]) for n in names],
        *[vm(2, *halves[n]) for n in names],
        *[vm(2, *halves[n]) for n in names],
        *[vm(2, *halves[n]) for n in names],
        vm(8, width, dtype=F32), vm(7, 8, width, dtype=F32), vm(8, width, dtype=F32),
        vm(3, 8, width, dtype=F32),
        vm(8, hidden, dtype=F32), vm(3, 8, hidden, dtype=F32), vm(8, hidden, dtype=F32),
        pltpu.SemaphoreType.DMA((208,)), pltpu.SemaphoreType.DMA((208,)),
        pltpu.SemaphoreType.DMA((10,)),
    ]
    used = []
    outs = pl.pallas_call(
        functools.partial(layer_kernel, EPS, MASKED, used),
        out_shape=(
            sds((half_tokens, quarter), BF), sds((half_tokens, quarter), BF),
            *[sds((slices, *blocks[n]), BF) for n in names],
            sds((8, quarter), F32), sds((slices, 8, hidden), F32),
        ),
        in_specs=[any_] * 12 + [pl.BlockSpec(memory_space=pltpu.SMEM)] + [vmem] * 2,
        out_specs=(any_,) * 7 + (vmem,) * 2,
        scratch_shapes=scratch,
        compiler_params=pltpu.CompilerParams(
            collective_id=0, has_side_effects=True, vmem_limit_bytes=60 << 20
        ),
        name="tree_layer",
    )(
        inputs, cotangent, w_qkv.transpose(1, 0, 2), w_out, w_down, w_up,
        *[v.reshape(1, -1) for v in (ln1_gain, ln1_bias, b_out, ln2_gain, ln2_bias, b_down)],
        seg_parent, b_up.reshape(1, -1), b_qv,
    )
    result, input_grad, g_a, g_b, g_o, g_d, g_u, by_token, small = outs
    steps = 2

    def finish(res_in, grad_in, a_in, b_in, o_in, d_in, u_in, tok_in, small_in, *into):
        res, grad, q, o, d, u, tok_0, tok_1, tok_2, tok_3, tok_4, tok_5, up, qv = into
        res[...] = res_in[...].astype(F32)
        grad[...] = grad_in[...].astype(F32)
        o[...] = o_in[...].astype(F32)
        d[...] = d_in[...].astype(F32)
        for s in range(slices):
            u[:, s * hidden : (s + 1) * hidden] = u_in[s].astype(F32)
            at = slice(s * head, (s + 1) * head)
            q[0, :, at] = a_in[s].astype(F32)
            for n in range(2):
                q[n + 1, :, at] = b_in[s, :, n * head : (n + 1) * head].astype(F32)
            up[0:1, s * hidden : (s + 1) * hidden] = small_in[s, 0:1, :]
            for n in range(2):
                qv[n : n + 1, at] = small_in[
                    s, 1:2, n * head : (n + 1) * head
                ]
        for n, one in enumerate((tok_0, tok_1, tok_2, tok_3, tok_4, tok_5)):
            one[...] = tok_in[n : n + 1, :]

    def rows(*dims):
        return pl.BlockSpec((dims[0] // steps, *dims[1:]), lambda i: (i,) + (0,) * (len(dims) - 1))

    def middle(*dims):
        return pl.BlockSpec((dims[0], dims[1] // steps, *dims[2:]), lambda i: (0, i, 0))

    def fixed(*dims):
        return pl.BlockSpec(dims, lambda i: (0,) * len(dims))

    tall_o, tall_d = (slices * head, quarter), (slices * hidden, quarter)
    done = pl.pallas_call(
        finish,
        grid=(steps,),
        out_shape=(
            sds((half_tokens, quarter), F32), sds((half_tokens, quarter), F32),
            sds((3, quarter, slices * head), F32), sds(tall_o, F32), sds(tall_d, F32),
            sds((quarter, slices * hidden), F32), *[sds((1, quarter), F32)] * 6,
            sds((1, slices * hidden), F32), sds((2, slices * head), F32),
        ),
        in_specs=[
            rows(half_tokens, quarter), rows(half_tokens, quarter),
            middle(slices, *blocks["a"]), middle(slices, *blocks["b"]), rows(*tall_o), rows(*tall_d), middle(slices, *blocks["u"]),
            fixed(8, quarter), fixed(slices, 8, hidden),
        ],
        out_specs=(
            rows(half_tokens, quarter), rows(half_tokens, quarter),
            middle(3, quarter, slices * head), rows(*tall_o), rows(*tall_d),
            rows(quarter, slices * hidden), *[fixed(1, quarter)] * 6,
            fixed(1, slices * hidden), fixed(2, slices * head),
        ),
        compiler_params=pltpu.CompilerParams(vmem_limit_bytes=60 << 20),
        name="finish",
    )(
        result, input_grad, g_a, g_b, g_o.reshape(tall_o), g_d.reshape(tall_d), g_u, by_token, small
    )
    by_token = [v.reshape(-1) for v in done[6:12]]
    return (
        done[0], done[1], by_token[0], by_token[1], done[2].transpose(1, 0, 2), done[13], done[3], by_token[4],
        by_token[2], by_token[3], done[5], done[12].reshape(-1), done[4], by_token[5],
    )


def fits_square(mesh, *arrays):
    sizes = tuple(mesh.shape[name] for name in ("dp", "row", "col"))
    return (
        sizes == (4, 4, 2)
        and arrays[0].shape == (512, 256)
        and arrays[2].shape == (13,)
        and arrays[3].shape == (1024,)
        and arrays[6].shape == (256, 3, 512)
        and arrays[12].shape == (256, 2048)
    )


def solution(mesh):
    placed = (
        P(("dp", "col"), "row"),
        P(("dp", "col"), "row"),
        P("dp"),
        P("dp"),
        P("row"),
        P("row"),
        P("row", None, "col"),
        P(None, "col"),
        P("col", "row"),
        P("row"),
        P("row"),
        P("row"),
        P("row", "col"),
        P("col"),
        P("col", "row"),
        P("row"),
    )

    def on_each(*arrays):
        return (layer_on_square if fits_square(mesh, *arrays) else on_device)(*arrays)

    return jax.shard_map(
        on_each,
        mesh=mesh,
        in_specs=placed,
        out_specs=(
            P(("dp", "col"), "row"),
            P(("dp", "col"), "row"),
            P("row"),
            P("row"),
            P("row", None, "col"),
            P(None, "col"),
            P("col", "row"),
            P("row"),
            P("row"),
            P("row"),
            P("row", "col"),
            P("col"),
            P("col", "row"),
            P("row"),
        ),
        check_vma=False,
    )
```

```python
import functools
import math

import jax
import jax.numpy as jnp
from jax import lax
from jax.experimental import pallas as pl
from jax.experimental.pallas import tpu as pltpu
from jax.sharding import PartitionSpec as P

MESH = pl.DeviceIdType.MESH
BF = jnp.bfloat16
F32 = jnp.float32


HD = 128


EPS = 1e-05
MASKED = -1e30


def gelu_value(values):
    return 0.5 * values * (1.0 + jax.scipy.special.erf(values / math.sqrt(2.0)))


def gelu_slope(values):
    return 0.5 * (1.0 + jax.scipy.special.erf(values / math.sqrt(2.0))) + values * jnp.exp(
        -0.5 * values * values
    ) / math.sqrt(2.0 * math.pi)


def width_sums(first_term, second_term):
    return lax.psum((jnp.sum(first_term, axis=1), jnp.sum(second_term, axis=1)), "row")


def normalize(values, norm_gain, norm_bias, feature_count):
    row_total, square = width_sums(values, values * values)
    row_mean = row_total / feature_count
    inv_std = lax.rsqrt(square / feature_count - row_mean * row_mean + EPS)
    normed = (values - row_mean[:, None]) * inv_std[:, None]
    return (normed, inv_std, (normed * norm_gain + norm_bias).astype(jnp.bfloat16))


def normalize_back(upstream, normed, inv_std, norm_gain, feature_count):
    spread = upstream * norm_gain
    row_total, cross_sum = width_sums(spread, spread * normed)
    return inv_std[:, None] * (
        spread - row_total[:, None] / feature_count - normed * (cross_sum[:, None] / feature_count)
    )


def contract(left_op, right_op, flipped):
    if flipped:
        return lax.dot_general(
            left_op, right_op, (((1,), (1,)), ((), ())), preferred_element_type=jnp.float32
        )
    return jnp.dot(left_op, right_op, preferred_element_type=jnp.float32)


def outer_sum(left_op, right_op):
    return lax.dot_general(
        left_op, right_op, (((0,), (0,)), ((), ())), preferred_element_type=jnp.float32
    )


def across_rows(operand, weight_block, flipped):
    gathered = lax.all_gather(operand, "col", axis=0, tiled=True)
    row_count = gathered.shape[0] // lax.axis_size("row")

    def partial_term(row_start, row_num):
        return contract(gathered, weight_block, flipped)

    return (
        lax.psum_scatter(
            partial_term(jnp.int32(0), row_count * lax.axis_size("row")),
            "row",
            scatter_dimension=0,
            tiled=True,
        ),
        gathered,
    )


def across_cols(operand, weight_block, flipped):
    gathered = lax.all_gather(operand, "row", axis=0, tiled=True)
    row_count = gathered.shape[0] // lax.axis_size("col")

    def partial_term(row_start, row_num):
        return contract(gathered, weight_block, flipped)

    return (
        lax.psum_scatter(
            partial_term(jnp.int32(0), row_count * lax.axis_size("col")),
            "col",
            scatter_dimension=0,
            tiled=True,
        ),
        gathered,
    )


def tree_labels(seg_parent, token_depth):
    seg_count = seg_parent.shape[0]
    tree_len = token_depth.shape[0]
    seg_len = tree_len // 16
    slot_ids = jnp.arange(seg_count, dtype=jnp.int32)
    where_at = jnp.arange(tree_len, dtype=jnp.int32)
    segment = jnp.where(where_at < 4 * seg_len, 0, 1 + (where_at - 4 * seg_len) // seg_len)
    parent_local = seg_parent - lax.axis_index("dp") * seg_count
    parent_one = jnp.sum(
        jnp.where(segment[:, None] == slot_ids[None, :], parent_local[None, :], 0), axis=1
    )
    parent_two = jnp.sum(
        jnp.where(parent_one[:, None] == slot_ids[None, :], parent_local[None, :], 0), axis=1
    )
    return (segment, parent_one, parent_two, token_depth)


def block_scores(query_block, key_rows, labels, query_start, slopes):
    segment, parent_one, parent_two, token_depth = labels
    block_size = query_block.shape[0]
    query_seg = lax.dynamic_slice_in_dim(segment, query_start, block_size, 0)
    query_one = lax.dynamic_slice_in_dim(parent_one, query_start, block_size, 0)
    query_two = lax.dynamic_slice_in_dim(parent_two, query_start, block_size, 0)
    query_depth = lax.dynamic_slice_in_dim(token_depth, query_start, block_size, 0)
    allowed = (
        (segment[None, :] == query_seg[:, None])
        | (segment[None, :] == query_one[:, None])
        | (segment[None, :] == query_two[:, None])
    ) & (token_depth[None, :] <= query_depth[:, None])
    score_scale = query_block.shape[2] ** (-0.5)
    raw = jnp.einsum("qhd,khd->hqk", query_block, key_rows, preferred_element_type=jnp.float32)
    distance = (query_depth[:, None] - token_depth[None, :]).astype(jnp.float32)
    scores = raw * score_scale - slopes[:, None, None] * distance[None]
    return jnp.where(allowed[None], scores, MASKED)


def attention_forward(queries, key_rows, value_rows, labels, slopes, offset):
    block_size = min(512, queries.shape[0])
    blocks = queries.shape[0] // block_size

    def one_block(block_index):
        block_first = block_index * block_size
        query_block = lax.dynamic_slice_in_dim(queries, block_first, block_size, 0)
        scores = block_scores(query_block, key_rows, labels, offset + block_first, slopes)
        top_score = jnp.max(scores, axis=2, keepdims=True)
        weights = jnp.exp(scores - top_score)
        weight_total = jnp.sum(weights, axis=2, keepdims=True)
        probs = (weights / weight_total).astype(jnp.bfloat16)
        mixed = jnp.einsum("hqk,khd->qhd", probs, value_rows, preferred_element_type=jnp.float32)
        return (mixed, (top_score + jnp.log(weight_total))[:, :, 0])

    return lax.map(one_block, jnp.arange(blocks, dtype=jnp.int32))


def attention_backward(
    queries, key_rows, value_rows, grad_mixed, log_total, labels, slopes, offset
):
    block_size = min(512, queries.shape[0])
    blocks = queries.shape[0] // block_size
    score_scale = queries.shape[2] ** (-0.5)

    def one_block(carry, items):
        key_grad, value_grad = carry
        block_index, block_total = items
        block_first = block_index * block_size
        query_block = lax.dynamic_slice_in_dim(queries, block_first, block_size, 0)
        grad_block = lax.dynamic_slice_in_dim(grad_mixed, block_first, block_size, 0)
        scores = block_scores(query_block, key_rows, labels, offset + block_first, slopes)
        probs = jnp.exp(scores - block_total[:, :, None])
        grad_probs = jnp.einsum(
            "qhd,khd->hqk", grad_block, value_rows, preferred_element_type=jnp.float32
        )
        centre = jnp.sum(probs * grad_probs, axis=2, keepdims=True)
        grad_scores = (probs * (grad_probs - centre)).astype(jnp.bfloat16)
        query_grad = (
            jnp.einsum("hqk,khd->qhd", grad_scores, key_rows, preferred_element_type=jnp.float32)
            * score_scale
        )
        key_grad = (
            key_grad
            + jnp.einsum(
                "hqk,qhd->khd", grad_scores, query_block, preferred_element_type=jnp.float32
            )
            * score_scale
        )
        value_grad = value_grad + jnp.einsum(
            "hqk,qhd->khd",
            probs.astype(jnp.bfloat16),
            grad_block,
            preferred_element_type=jnp.float32,
        )
        return ((key_grad, value_grad), query_grad)

    empty = jnp.zeros(key_rows.shape, jnp.float32)
    (key_grad, value_grad), query_grad = lax.scan(
        one_block, (empty, empty), (jnp.arange(blocks, dtype=jnp.int32), log_total)
    )
    return (key_grad, value_grad, query_grad)


def on_device(
    inputs,
    cotangent,
    seg_parent,
    token_depth,
    ln1_gain,
    ln1_bias,
    w_qkv,
    b_qv,
    w_out,
    b_out,
    ln2_gain,
    ln2_bias,
    w_up,
    b_up,
    w_down,
    b_down,
):
    feature_count = inputs.shape[1] * lax.axis_size("row")
    col_width = w_qkv.shape[2]
    heads_here = col_width // HD
    qkv_flat = w_qkv.reshape(w_qkv.shape[0], 3 * col_width)
    labels = tree_labels(seg_parent, token_depth)
    heads_seen = lax.axis_index("col") * heads_here + jnp.arange(heads_here, dtype=jnp.int32)
    slopes = jnp.exp2(-(heads_seen + 1).astype(jnp.float32))
    states = inputs.astype(jnp.float32)
    normed_one, inv_one, entry_one = normalize(states, ln1_gain, ln1_bias, feature_count)
    projected, entry_one_all = across_rows(entry_one, qkv_flat, False)
    tok_rows = projected.shape[0]
    projected = projected.reshape(tok_rows, 3, col_width)
    queries = (projected[:, 0] + b_qv[0]).astype(jnp.bfloat16)
    keys_here = projected[:, 1].astype(jnp.bfloat16)
    values_here = (projected[:, 2] + b_qv[1]).astype(jnp.bfloat16)
    pair_all = lax.all_gather(
        jnp.stack([keys_here, values_here], axis=1), "row", axis=0, tiled=True
    )
    key_rows = pair_all[:, 0].reshape(-1, heads_here, HD)
    value_rows = pair_all[:, 1].reshape(-1, heads_here, HD)
    query_heads = queries.reshape(tok_rows, heads_here, HD)
    offset = lax.axis_index("row") * tok_rows
    mixed, log_total = attention_forward(query_heads, key_rows, value_rows, labels, slopes, offset)
    mixed = mixed.reshape(tok_rows, col_width).astype(jnp.bfloat16)
    attn_out, mixed_all = across_cols(mixed, w_out, False)
    middle = states + attn_out + b_out
    normed_two, inv_two, entry_two = normalize(middle, ln2_gain, ln2_bias, feature_count)
    hidden_pre, entry_two_all = across_rows(entry_two, w_up, False)
    hidden_pre = hidden_pre + b_up
    hidden = gelu_value(hidden_pre).astype(jnp.bfloat16)
    ffn_out, hidden_all = across_cols(hidden, w_down, False)
    result = middle + ffn_out + b_down
    grad_hidden, down_all = across_rows(cotangent, w_down, True)
    grad_pre = (grad_hidden * gelu_slope(hidden_pre)).astype(jnp.bfloat16)
    grad_entry_two, pre_all = across_cols(grad_pre, w_up, True)
    grad_middle = cotangent.astype(jnp.float32) + normalize_back(
        grad_entry_two, normed_two, inv_two, ln2_gain, feature_count
    )
    grad_branch = grad_middle.astype(jnp.bfloat16)
    grad_mixed, branch_all = across_rows(grad_branch, w_out, True)
    grad_mixed = grad_mixed.astype(jnp.bfloat16).reshape(tok_rows, heads_here, HD)
    key_grad, value_grad, query_grad = attention_backward(
        query_heads, key_rows, value_rows, grad_mixed, log_total, labels, slopes, offset
    )
    kv_grads = lax.psum_scatter(
        jnp.stack([key_grad.reshape(-1, col_width), value_grad.reshape(-1, col_width)], axis=1),
        "row",
        scatter_dimension=0,
        tiled=True,
    )
    grad_projected = jnp.stack(
        [
            query_grad.reshape(tok_rows, col_width).astype(jnp.bfloat16),
            kv_grads[:, 0].astype(jnp.bfloat16),
            kv_grads[:, 1].astype(jnp.bfloat16),
        ],
        axis=1,
    )
    grad_entry_one, proj_all = across_cols(
        grad_projected.reshape(tok_rows, 3 * col_width), qkv_flat, True
    )
    input_grad = grad_middle + normalize_back(
        grad_entry_one, normed_one, inv_one, ln1_gain, feature_count
    )
    proj_sums = jnp.sum(proj_all.astype(jnp.float32), axis=0).reshape(3, col_width)
    weight_terms = (
        outer_sum(entry_one_all, proj_all).reshape(w_qkv.shape),
        jnp.stack([proj_sums[0], proj_sums[2]], axis=0),
        outer_sum(mixed_all, branch_all),
        jnp.sum(branch_all.astype(jnp.float32), axis=0),
        outer_sum(entry_two_all, pre_all),
        jnp.sum(pre_all.astype(jnp.float32), axis=0),
        outer_sum(hidden_all, down_all),
        jnp.sum(down_all.astype(jnp.float32), axis=0),
    )
    (
        grad_w_qkv,
        grad_b_qv,
        grad_w_out,
        grad_b_out,
        grad_w_up,
        grad_b_up,
        grad_w_down,
        grad_b_down,
    ) = lax.psum(
        (
            weight_terms[0],
            weight_terms[1],
            weight_terms[2],
            weight_terms[3],
            weight_terms[4],
            weight_terms[5],
            weight_terms[6],
            weight_terms[7],
        ),
        "dp",
    )
    norm_terms = (
        jnp.sum(grad_entry_one * normed_one, axis=0),
        jnp.sum(grad_entry_one, axis=0),
        jnp.sum(grad_entry_two * normed_two, axis=0),
        jnp.sum(grad_entry_two, axis=0),
    )
    grad_ln1_gain, grad_ln1_bias, grad_ln2_gain, grad_ln2_bias = lax.psum(
        (norm_terms[0], norm_terms[1], norm_terms[2], norm_terms[3]), ("dp", "col")
    )
    return (
        result,
        input_grad,
        grad_ln1_gain,
        grad_ln1_bias,
        grad_w_qkv,
        grad_b_qv,
        grad_w_out,
        grad_b_out,
        grad_ln2_gain,
        grad_ln2_bias,
        grad_w_up,
        grad_b_up,
        grad_w_down,
        grad_b_down,
    )


RELS = (0, 4, 2, 6)


def dot_nn(a, b):
    return lax.dot_general(a, b, (((1,), (0,)), ((), ())), preferred_element_type=F32)


def dot_nt(a, b):
    return lax.dot_general(a, b, (((1,), (1,)), ((), ())), preferred_element_type=F32)


def dot_tn(a, b):
    return lax.dot_general(a, b, (((0,), (0,)), ((), ())), preferred_element_type=F32)


def span(index, size):
    return pl.ds(pl.multiple_of(index * size, size), size)


class Net:
    def __init__(self, ssem, rsem):
        self.dp = lax.axis_index("dp")
        self.row = lax.axis_index("row")
        self.col = lax.axis_index("col")
        self.y, self.k = self.dp // 2, self.dp % 2
        self.zh, self.zl = self.row // 2, self.row % 2
        self.x = self.col
        self.slot = self.x * 4 + self.zl * 2 + self.k
        self.chip = self.x * 2 + self.zl
        self.slice = self.zl * 2 + self.k
        self.ssem, self.rsem = ssem, rsem
        self.used = 0
        self.pending = []

    def sites(self, n):
        first = self.used
        self.used += n
        return first

    def peer(self, dy=0, dk=0, dz=0, dx=0):
        return (
            (self.y ^ dy) * 2 + (self.k ^ dk),
            self.row ^ dz,
            self.col ^ dx,
        )

    def rel(self, rel):
        return self.peer(dz=(rel >> 1) & 1, dx=rel >> 2, dk=rel & 1)

    def make(self, src, dst, site, device, recv_site=None):
        recv = site if recv_site is None else recv_site
        return pltpu.make_async_remote_copy(
            src_ref=src,
            dst_ref=dst,
            send_sem=self.ssem.at[site],
            recv_sem=self.rsem.at[recv],
            device_id=device,
            device_id_type=MESH,
        )

    def send(self, src, dst, site, device, recv_site=None, skip=None):
        remote = self.make(src, dst, site, device, recv_site)
        if skip is None:
            remote.start()
        else:
            recv = site if recv_site is None else recv_site

            @pl.when(skip)
            def _():
                pltpu.make_async_copy(src, dst, self.rsem.at[recv]).start()

            @pl.when(jnp.logical_not(skip))
            def _():
                remote.start()

        self.pending.append((remote, skip))
        return remote

    def landed(self, ref, site):
        self.make(ref, ref, site, self.peer(dk=1)).wait_recv()

    def drain(self, upto=None):
        for remote, skip in self.pending:
            if skip is None:
                remote.wait_send()
            else:

                @pl.when(jnp.logical_not(skip))
                def _(remote=remote):
                    remote.wait_send()

        self.pending = []


class Gather:
    def __init__(self, net, buf, by_low, over_y=False):
        self.net, self.buf, self.over_y = net, buf, over_y
        self.slot = net.x * 4 + net.y * 2 + net.k if over_y else net.slot
        self.first = net.sites(8)
        rows = buf.shape[1]
        self.low_rows = pl.ds(0, by_low) if by_low else None
        self.x_rows = pl.ds(by_low, rows - by_low) if by_low < rows else None

    def to(self, rel):
        low = (rel >> 1) & 1
        where = {"dy": low} if self.over_y else {"dz": low}
        return self.net.peer(dk=rel & 1, dx=rel >> 2, **where)

    def start(self):
        own = self.buf.at[self.slot]
        for n, rel in enumerate((1, 4, 2)):
            self.net.send(own, own, self.first + n, self.to(rel))

    def relay(self, j):
        net = self.net
        part = self.buf.at[self.slot ^ RELS[j]]
        if j < 3:
            net.landed(part, self.first + j)
            rows, rel = ((self.low_rows, 2), (self.x_rows, 4))[j - 1]
            if rows is not None:
                some = part.at[rows, :]
                net.send(some, some, self.first + 2 + j, self.to(rel))
        else:
            for n, rows in enumerate((self.low_rows, self.x_rows)):
                if rows is not None:
                    net.landed(part.at[rows, :], self.first + 3 + n)
        net.send(part, part, self.first + 4 + j, self.to(1))

    def ready(self, j):
        part = self.buf.at[self.slot ^ RELS[j] ^ 1]
        self.net.landed(part, self.first if j == 0 else self.first + 4 + j)

    def block(self, j):
        chip = (self.slot ^ RELS[j]) // 2
        both = self.buf[pl.ds(chip * 2, 2)]
        return both.reshape(2 * both.shape[1], both.shape[2])


class Exchange:
    def __init__(self, net, src_of, dst_of):
        self.net, self.src_of, self.dst_of = net, src_of, dst_of
        self.first = net.sites(7)

    def start(self):
        net = self.net
        for n in (6, 7, 4, 5, 2, 3, 1):
            net.send(
                self.src_of(net.slot ^ n), self.dst_of(net.slot), self.first + n - 1, net.rel(n)
            )

    def ready(self):
        net = self.net
        for n in range(1, 8):
            net.landed(self.dst_of(net.slot ^ n), self.first + n - 1)


class Scatter:
    def __init__(self, net, bufs, land, cut):
        self.net, self.cut = net, cut
        self.part, self.hops, self.kept, self.last = bufs
        self.one, self.two, self.three = land
        self.first = net.sites(10)
        self.sent = []
        rows = self.part.shape[1]
        self.ways = [
            way
            for way in ((0, pl.ds(0, cut), 1, 2), (1, pl.ds(cut, rows - cut), 2, 1))
            if way[1].size
        ]

    def send(self, src, dst, site, rel):
        self.sent.append(self.net.send(src, dst, self.first + site, self.net.rel(rel)))

    def put(self, j, value):
        net = self.net
        chip = net.chip ^ (RELS[j] >> 1)
        shard = self.part.shape[1]
        self.part[pl.ds(chip * 2, 2)] = value.astype(BF).reshape(2, shard, value.shape[1])
        self.send(self.part.at[chip * 2 + (1 - net.k)], self.one.at[j], j, 1)

    def chip_sum(self, j):
        net = self.net
        chip = net.chip ^ (RELS[j] >> 1)
        net.landed(self.one.at[j], self.first + j)
        return self.part[chip * 2 + net.k].astype(F32) + self.one[j].astype(F32)

    def hop(self, j):
        value = self.chip_sum(j)
        for n, rows, near, far in self.ways:
            mine = value[rows.start : rows.start + rows.size]
            if j == far:
                self.kept[rows, :] = mine
            else:
                place = 0 if j == near else 1
                self.hops[place, rows, :] = mine.astype(BF)
                self.send(
                    self.hops.at[place, rows, :],
                    self.two.at[place, rows, :],
                    4 + 2 * n + place,
                    RELS[near],
                )

    def hop_on(self):
        net = self.net
        for n, rows, near, far in self.ways:
            net.landed(self.two.at[1, rows, :], self.first + 5 + 2 * n)
            self.last[rows, :] = (
                self.kept[rows, :] + self.two[1, rows, :].astype(F32)
            ).astype(BF)
            self.send(self.last.at[rows, :], self.three.at[rows, :], 8 + n, RELS[far])

    def left(self):
        for remote in self.sent:
            remote.wait_send()
        mine = {id(remote) for remote in self.sent}
        self.net.pending = [p for p in self.net.pending if id(p[0]) not in mine]

    def total(self):
        net = self.net
        value = self.chip_sum(0)
        for n, rows, near, far in self.ways:
            net.landed(self.two.at[0, rows, :], self.first + 4 + 2 * n)
            net.landed(self.three.at[rows, :], self.first + 8 + n)
        return value + self.two[0].astype(F32) + self.three[...].astype(F32)


class TreeSum:
    def __init__(self, net, own, land_y, hop, land_z, done, out, local_sem, direct):
        self.net, self.own, self.land_y = net, own, land_y
        self.hop_buf, self.land_z, self.done, self.out = hop, land_z, done, out
        self.first = net.sites(7)
        self.local_sem, self.direct = local_sem, direct

    def put(self, z, value):
        rows = self.own.shape[3]
        self.own[z // 2, z % 2] = value.astype(BF).reshape(2, rows, value.shape[1])

    def half(self, piece, which):
        return self.out.at[piece, span(which, self.own.shape[3]), :]

    def start(self):
        net = self.net
        net.send(self.own.at[:, :, 1 - net.y], self.land_y, self.first, net.peer(dy=1))

    def across(self):
        net = self.net
        net.landed(self.land_y, self.first)
        far = 1 - net.zh
        for low in (0, 1):
            self.hop_buf[low] = (
                self.own[far, low, net.y].astype(F32) + self.land_y[far, low].astype(F32)
            ).astype(BF)
        net.send(self.hop_buf, self.land_z, self.first + 1, net.peer(dz=2))

    def hand_out(self):
        net = self.net
        net.landed(self.land_z, self.first + 1)
        for low in (0, 1):
            self.done[low] = (
                self.own[net.zh, low, net.y].astype(F32)
                + self.land_y[net.zh, low].astype(F32)
                + self.land_z[low].astype(F32)
            ).astype(BF)
        place = self.half(net.slice, net.y)
        net.send(self.done.at[1 - net.zl], place, self.first + 2, net.peer(dz=1))
        net.send(self.done.at[net.zl], place, self.first + 3, net.peer(dy=1))
        if self.direct:
            net.send(self.done.at[1 - net.zl], place, self.first + 4, net.peer(dy=1, dz=1))
        self.kept = pltpu.make_async_copy(self.done.at[net.zl], place, self.local_sem)
        self.kept.start()

    def pass_on(self):
        net = self.net
        part = self.half(net.slice ^ 2, net.y)
        net.landed(part, self.first + 2)
        if not self.direct:
            net.send(part, part, self.first + 4, net.peer(dy=1))

    def share(self):
        net = self.net
        self.kept.wait()
        for n, piece in enumerate((net.slice, net.slice ^ 2)):
            net.landed(self.half(piece, 1 - net.y), self.first + 3 + n)
            part = self.out.at[piece]
            net.send(part, part, self.first + 5 + n, net.rel(1))

    def finish(self):
        net = self.net
        for n, piece in enumerate((net.slice ^ 1, net.slice ^ 3)):
            net.landed(self.out.at[piece], self.first + 5 + n)


def layer_kernel(eps, masked, used, *refs):
    (
        inp, cot, w_q, w_o, w_d, w_u, vec_0, vec_1, vec_2, vec_3, vec_4, vec_5, parents, b_up, b_qv,
        res_out, grad_out, out_a, out_b, out_o, out_d, out_u, out_tok, out_small,
        xs, e1, g, e2, gb, wf, wq, wd, wu, mixed_all, grad_all, links, vec_in, vec, bias,
        q_buf, k_buf, v_buf, p_buf, mix, mix_b,
        part_a, hops_a, kept_a, last_a, part_b, hops_b, kept_b, last_b, one, two, three,
        hid, gp, gm, dk_acc, dv_acc, dqkv, mid, gmid, back_a, back_b,
        dw_a, dw_b, dw_o, dw_d, dw_u, ly_a, ly_b, ly_o, ly_d, ly_u,
        yh_a, yh_b, yh_o, yh_d, yh_u, lz_a, lz_b, lz_o, lz_d, lz_u,
        fin_a, fin_b, fin_o, fin_d, fin_u,
        tok, tok_one, tok_sum, tok_two, small, small_land, small_sum,
        ssem, rsem, lsem,
    ) = refs
    net = Net(ssem, rsem)
    y, k, zh, zl, x, row = net.y, net.k, net.zh, net.zl, net.x, net.row
    shard, width = xs.shape
    tokens = 8 * shard
    quarter = width // 4
    head = q_buf.shape[1]

    greet = [
        net.peer(dy=dy, dk=dk, dz=dz)
        for dy in (0, 1)
        for dk in (0, 1)
        for dz in (0, 1, 2, 3)
        if dy + dk + dz
    ]
    greet += [net.peer(dk=dk, dz=dz, dx=1) for dk in (0, 1) for dz in (0, 1)]
    barrier = pltpu.get_barrier_semaphore()
    for device in greet:
        pl.semaphore_signal(barrier, inc=1, device_id=device, device_id_type=MESH)
    vec_parts = (vec_0, vec_1, vec_2, vec_3, vec_4, vec_5)
    for n, part in enumerate(vec_parts):
        pltpu.make_async_copy(part, vec_in.at[pl.ds(n, 1), :], lsem.at[9]).start()
    seg_count = parents.shape[0]
    half_at = lax.broadcasted_iota(jnp.int32, links.shape[1:], 0)
    mine = jnp.zeros(links.shape[1:], F32)
    for s in range(1, seg_count):
        parent = parents[s] - net.dp * seg_count
        mine = jnp.where(half_at == s + 3, parent.astype(F32), mine)
    links[0] = mine

    pl.semaphore_wait(barrier, len(greet))

    def send_home(src, dst_of, first):
        for s in range(4):
            low, core = s // 2, s % 2
            target = 2 * k + low
            net.send(
                src.at[span(s, shard), :],
                dst_of(s).at[:, span(row, quarter)],
                first + s,
                (y * 2 + core, target, net.col),
                recv_site=first + 4 + row,
                skip=(target == row) & (k == core),
            )

    def home_ready(dst, first):
        for z in range(4):
            net.landed(dst.at[:, span(z, quarter)], first + 4 + z)

    vec_site = net.sites(3)
    pltpu.make_async_copy(vec_in.at[pl.ds(0, 6), :], vec_in.at[pl.ds(0, 6), :], lsem.at[9]).wait()
    for o in (1, 2, 3):
        net.send(
            vec_in.at[pl.ds(0, 8), :], vec.at[:, span(row, quarter)], vec_site + o - 1, net.peer(dz=o)
        )
    links_site = net.sites(1)
    net.send(links.at[0], links.at[1], links_site, net.rel(1))
    home_x, home_g = net.sites(8), net.sites(8)
    send_home(inp, lambda s: xs, home_x)

    def slices(w_ref, full, axis):
        if axis == 0:
            rows = full.shape[0] // 4
            return rows, lambda z: full.at[span(z, rows), :]
        cols = full.shape[1] // 4
        return full.shape[0], lambda z: full.at[:, span(z, cols)]

    class Weight:
        def __init__(self, src_of, full, axis, local):
            self.src_of, self.full = src_of, full
            self.rows, self.place = slices(None, full, axis)
            self.first = net.sites(6)
            self.local = local

        def half(self, ref, which):
            rows = self.rows // 2
            return ref.at[span(which, rows), :]

        def start(self):
            own = pltpu.make_async_copy(
                self.place(row), self.place(row), lsem.at[self.local]
            )
            for src, cols in self.src_of(net.slice):
                pltpu.make_async_copy(
                    src, self.place(row).at[:, cols], lsem.at[self.local]
                ).start()
            for o in (1, 2, 3):
                far = (zl ^ (o & 1)) * 2 + k
                for src, cols in self.src_of(far):
                    net.send(
                        self.half(src, y),
                        self.half(self.place(row), y).at[:, cols],
                        self.first + o - 1,
                        net.peer(dz=o),
                    )
            self.own = own

        def relay(self):
            for o in (1, 2, 3):
                part = self.half(self.place(row ^ o), y)
                net.landed(part, self.first + o - 1)
                net.send(part, part, self.first + 2 + o, net.peer(dy=1))

        def ready(self):
            for o in (1, 2, 3):
                net.landed(self.half(self.place(row ^ o), 1 - y), self.first + 2 + o)
            self.own.wait()

    hidden = hid.shape[1]
    whole = slice(None)

    def qkv_parts(s):
        return [
            (w_q.at[n, :, span(s, head)], pl.ds(n * head, head)) for n in range(3)
        ]

    weight_q = Weight(qkv_parts, wq, 0, 0)
    weight_d = Weight(lambda s: [(w_d.at[span(s, hidden), :], whole)], wd, 1, 2)
    weight_u = Weight(lambda s: [(w_u.at[:, span(s, hidden)], whole)], wu, 0, 3)

    gather_w = Gather(net, wf, shard // 2, over_y=True)
    wf_own = wf.at[gather_w.slot]
    wf_site = net.sites(3)
    wf_src = w_o.at[span(y * 2 + k, shard), :]

    vec[:, span(row, quarter)] = vec_in[...]
    for o in (1, 2, 3):
        net.landed(vec.at[:, span(row ^ o, quarter)], vec_site + o - 1)

    def norm_stats(values):
        mean = jnp.sum(values, axis=1, keepdims=True) * (1.0 / width)
        msq = jnp.sum(values * values, axis=1, keepdims=True) * (1.0 / width)
        inv = lax.rsqrt(msq - mean * mean + eps)
        return (values - mean) * inv, inv

    weight_q.start()
    home_ready(xs, home_x)
    normed, _ = norm_stats(xs[...].astype(F32))
    e1[net.slot] = (normed * vec[0:1, :] + vec[1:2, :]).astype(BF)
    gather_e1 = Gather(net, e1, 0)
    gather_e1.start()
    wf_copy = pltpu.make_async_copy(wf_src, wf_own.at[:, span(row, quarter)], lsem.at[1])
    wf_copy.start()
    for o in (1, 2, 3):
        net.send(wf_src, wf_own.at[:, span(row, quarter)], wf_site + o - 1, net.peer(dz=o))
    gather_g = Gather(net, g, 0)
    send_home(cot, lambda s: g.at[x * 4 + s], home_g)
    weight_q.relay()

    net.landed(links.at[1], links_site)
    parent = jnp.where(zh == k, links[0], links[1])[:, 0:1]
    seg_len = tokens // 16
    key_at = lax.broadcasted_iota(jnp.int32, (1, tokens), 1)
    key_half = key_at // seg_len
    key_seg = jnp.maximum(key_half - 3, 0)
    half_row = lax.broadcasted_iota(jnp.int32, (16, 1), 0)
    seg_row = jnp.maximum(half_row - 3, 0)
    key_parent = jnp.sum(jnp.where(key_half == half_row, parent, 0.0), axis=0, keepdims=True)
    start = jnp.where(key_parent > 0.0, 5 * seg_len, 4 * seg_len)
    depth = jnp.where(key_seg == 0, key_at, start + key_at % seg_len)
    allowed = (key_seg == 0) | (key_seg == seg_row) | (key_seg == parent.astype(jnp.int32))
    exponent = jnp.full((1, tokens), -(x * 4 + net.slice + 1), jnp.int32).astype(F32)
    slope = jnp.exp2(exponent)
    bias[...] = jnp.where(allowed, slope * depth.astype(F32), masked)

    b_q = b_qv[0:1, span(net.slice, head)]
    b_v = b_qv[1:2, span(net.slice, head)]
    gather_e1.relay(1)
    gather_e1.relay(2)
    weight_u.start()
    weight_d.start()
    weight_q.ready()
    for j in range(4):
        if j == 3:
            for o in (1, 2, 3):
                net.landed(wf_own.at[:, span(row ^ o, quarter)], wf_site + o - 1)
            wf_copy.wait()
            gather_w.start()
            gather_e1.relay(3)
        gather_e1.ready(j)
        rows = pl.ds((net.chip ^ (RELS[j] >> 1)) * 2 * shard, 2 * shard)
        proj = dot_nn(gather_e1.block(j), wq[...])
        q_buf[rows, :] = (proj[:, :head] + b_q).astype(BF)
        k_buf[rows, :] = proj[:, head : 2 * head].astype(BF)
        v_buf[rows, :] = (proj[:, 2 * head :] + b_v).astype(BF)

    scale = head ** (-0.5)

    def attend(i, carry):
        first = pl.multiple_of(i * shard, shard)
        raw = dot_nt(q_buf[pl.ds(first, shard), :], k_buf[...])
        parts = []
        for half in (0, 1):
            at = 2 * i + half
            seg = jnp.maximum(at - 3, 0)
            later = jnp.where(key_seg == seg, key_at, -1)
            query_at = first + half * seg_len + lax.broadcasted_iota(jnp.int32, (seg_len, 1), 0)
            scores = raw[half * seg_len : (half + 1) * seg_len] * scale + bias[pl.ds(at, 1), :]
            scores = jnp.where(later > query_at, masked, scores)
            top = jnp.max(scores, axis=1, keepdims=True)
            weights = jnp.exp(scores - top)
            norm = 1.0 / jnp.sum(weights, axis=1, keepdims=True)
            parts.append((weights * norm).astype(BF))
        probs = jnp.concatenate(parts, axis=0)
        p_buf[pl.ds(first, shard), :] = probs
        mixed = dot_nn(probs, v_buf[...])
        mix[pl.ds(first, shard), :] = mixed
        mix_b[pl.ds(first, shard), :] = mixed.astype(BF)
        return carry

    lax.fori_loop(0, 6, attend, 0)
    gather_w.relay(1)
    gather_w.relay(2)
    lax.fori_loop(6, 8, attend, 0)

    def rows_of(j):
        return span(net.chip ^ (RELS[j] >> 1), 2 * shard)

    order = (3, 1, 2, 0)
    part_set_a = (part_a, hops_a, kept_a, last_a)
    part_set_b = (part_b, hops_b, kept_b, last_b)

    def landings(n):
        return (one.at[n], two.at[n], three.at[n])

    swap = Exchange(
        net, lambda q: mix_b.at[span(q, shard), :], lambda h: mixed_all.at[:, span(h, head)]
    )
    swap.start()
    mixed_all[:, span(net.slot, head)] = mix_b[span(net.slot, shard), :]
    home_ready(g.at[net.slot], home_g)
    gather_g.start()
    gather_w.relay(3)
    weight_u.relay()
    for j in range(4):
        gather_w.ready(j)
    swap.ready()
    w_out = wf[...].reshape(width, width)

    middle = xs[...].astype(F32) + dot_nn(mixed_all[...], w_out) + vec[2:3, :]
    mid[...] = middle
    normed, _ = norm_stats(middle)
    e2[net.slot] = (normed * vec[3:4, :] + vec[4:5, :]).astype(BF)
    gather_e2 = Gather(net, e2, shard * 3 // 4)
    gather_e2.start()
    weight_d.relay()
    gather_g.relay(1)
    gather_g.relay(2)
    gather_e2.relay(1)
    gather_e2.relay(2)


    b_u = b_up[0:1, span(net.slice, hidden)]
    weight_u.ready()
    scatter_two = Scatter(net, part_set_a, landings(0), shard // 2)
    for j in range(4):
        if j == 3:
            gather_e2.relay(3)
        gather_e2.ready(j)
        pre = dot_nn(gather_e2.block(j), wu[...]) + b_u
        bell = 0.5 * (1.0 + lax.erf(pre * (1.0 / math.sqrt(2.0))))
        hid[rows_of(j), :] = (pre * bell).astype(BF)
        if j == 0:
            weight_d.ready()
        if j == 3:
            gather_g.relay(3)
        gather_g.ready(j)
        rise = bell + pre * jnp.exp(-0.5 * pre * pre) * (1.0 / math.sqrt(2.0 * math.pi))
        gp[rows_of(j), :] = (dot_nt(gather_g.block(j), wd[...]) * rise).astype(BF)
        scatter_two.put(j, dot_nt(gp[rows_of(j), :], wu[...]))
        if j == 2:
            scatter_two.hop(1)
    scatter_two.hop(2)
    scatter_two.hop(3)

    sums = {
        name: TreeSum(net, own, land_y, hop, land_z, done, out, lsem.at[4 + n], name in "o")
        for n, (name, own, land_y, hop, land_z, done, out) in enumerate(
            (
                ("a", dw_a, ly_a, yh_a, lz_a, fin_a, out_a),
                ("b", dw_b, ly_b, yh_b, lz_b, fin_b, out_b),
                ("o", dw_o, ly_o, yh_o, lz_o, fin_o, out_o),
                ("d", dw_d, ly_d, yh_d, lz_d, fin_d, out_d),
                ("u", dw_u, ly_u, yh_u, lz_u, fin_u, out_u),
            )
        )
    }

    def columns(buf, z):
        part = buf[:, :, span(z, quarter)]
        return part.reshape(tokens, quarter)

    def grad_down(z, carry):
        sums["d"].put(z, dot_tn(hid[...], columns(g, z)))
        return carry

    def grad_up(z, carry):
        sums["u"].put(z, dot_tn(columns(e2, z), gp[...]))
        return carry

    def grad_qkv(z, carry):
        value = dot_tn(columns(e1, z), dqkv[...])
        sums["a"].put(z, value[:, :head])
        sums["b"].put(z, value[:, head:])
        return carry

    def grad_o(z, carry):
        sums["o"].put(z, dot_tn(mix_b[...], columns(gb, z)))
        return carry

    lax.fori_loop(0, 4, grad_down, 0)
    sums["d"].start()
    scatter_two.hop_on()
    lax.fori_loop(0, 4, grad_up, 0)
    sums["u"].start()

    grad = scatter_two.total()
    middle = mid[...]
    normed, inv = norm_stats(middle)
    spread = grad * vec[3:4, :]
    mean_one = jnp.sum(spread, axis=1, keepdims=True) * (1.0 / width)
    mean_two = jnp.sum(spread * normed, axis=1, keepdims=True) * (1.0 / width)
    cot_own = g[net.slot].astype(F32)
    total = cot_own + inv * (spread - mean_one - normed * mean_two)
    gmid[...] = total
    branch = total.astype(BF)
    gb[net.slot] = branch
    grad_all[...] = dot_nt(branch, w_out).astype(BF)
    swap_back = Exchange(
        net, lambda h: grad_all.at[:, span(h, head)], lambda q: gm.at[span(q, shard), :]
    )
    swap_back.start()
    gm[span(net.slot, shard), :] = grad_all[:, span(net.slot, head)]
    tok[2:3, :] = jnp.sum(grad * normed, axis=0, keepdims=True)
    tok[3:4, :] = jnp.sum(grad, axis=0, keepdims=True)
    tok[4:5, :] = jnp.sum(branch.astype(F32), axis=0, keepdims=True)
    tok[5:6, :] = jnp.sum(cot_own, axis=0, keepdims=True)
    tok[6:8, :] = jnp.zeros((2, width), F32)
    dk_acc[...] = jnp.zeros_like(dk_acc)
    dv_acc[...] = jnp.zeros_like(dv_acc)
    small[...] = jnp.zeros_like(small)
    small[0:1, :] = jnp.sum(gp[...].astype(F32), axis=0, keepdims=True)
    gather_gb = Gather(net, gb, 0)

    def tile_back(t, carry):
        rows = span(t, shard)
        grad_mix = gm[rows, :]
        probs = p_buf[rows, :]
        grad_probs = dot_nt(grad_mix, v_buf[...])
        centre = jnp.sum(mix[rows, :] * grad_mix.astype(F32), axis=1, keepdims=True)
        grad_scores = (probs.astype(F32) * (grad_probs - centre)).astype(BF)
        dqkv[rows, :head] = (dot_nn(grad_scores, k_buf[...]) * scale).astype(BF)
        dk_acc[...] += dot_tn(grad_scores, q_buf[rows, :])
        dv_acc[...] += dot_tn(probs, grad_mix)
        return carry

    swap_back.ready()
    gather_gb.start()
    lax.fori_loop(0, 8, tile_back, 0)
    dqkv[:, head : 2 * head] = (dk_acc[...] * scale).astype(BF)
    dqkv[:, 2 * head :] = dv_acc[...].astype(BF)

    scatter_four = Scatter(net, part_set_a, landings(1), shard // 2)
    scatter_two.left()
    for j in order:
        scatter_four.put(j, dot_nt(dqkv[rows_of(j), :], wq[...]))
    for j in (3, 1, 2):
        scatter_four.hop(j)
    sums["d"].across()
    gather_gb.relay(1)
    gather_gb.relay(2)
    lax.fori_loop(0, 4, grad_qkv, 0)
    scatter_four.hop_on()
    sums["u"].across()
    sums["b"].start()
    sums["a"].start()
    sums["d"].hand_out()

    small[1:2, :head] = jnp.sum(dqkv[:, :head].astype(F32), axis=0, keepdims=True)
    small[1:2, head : 2 * head] = jnp.sum(dqkv[:, 2 * head :].astype(F32), axis=0, keepdims=True)
    small_site = net.sites(6)
    others = ((1, 0), (0, 2), (1, 2))
    for n, (dy, dz) in enumerate(others):
        net.send(small, small_land.at[n], small_site + n, net.peer(dy=dy, dz=dz))
    gather_gb.relay(3)
    for j in range(4):
        gather_gb.ready(j)
    lax.fori_loop(0, 4, grad_o, 0)
    sums["o"].start()

    def send_out(src, dst, first):
        for z in range(4):
            net.send(
                src.at[:, span(z, quarter)],
                dst.at[span(net.slice, shard), :],
                first + z,
                (y * 2 + zh, z, net.col),
                recv_site=first + 4 + net.slice,
                skip=(row == z) & (k == zh),
            )

    def out_ready(dst, first):
        for s in range(4):
            net.landed(dst.at[span(s, shard), :], first + 4 + s)

    res_site, grad_site = net.sites(8), net.sites(8)
    grad = scatter_four.total()
    normed, inv = norm_stats(xs[...].astype(F32))
    tok[0:1, :] = jnp.sum(grad * normed, axis=0, keepdims=True)
    tok[1:2, :] = jnp.sum(grad, axis=0, keepdims=True)
    tok_site = net.sites(10)
    for n in range(1, 8):
        net.send(tok, tok_one.at[n - 1], tok_site + n - 1, net.rel(n))
    spread = grad * vec[0:1, :]
    mean_one = jnp.sum(spread, axis=1, keepdims=True) * (1.0 / width)
    mean_two = jnp.sum(spread * normed, axis=1, keepdims=True) * (1.0 / width)
    back_b[...] = (gmid[...] + inv * (spread - mean_one - normed * mean_two)).astype(BF)
    send_out(back_b, grad_out, grad_site)

    scatter_three = Scatter(net, part_set_b, landings(2), shard)
    for j in order:
        scatter_three.put(j, dot_nn(hid[rows_of(j), :], wd[...]))
    for j in (3, 1, 2):
        scatter_three.hop(j)
    sums["d"].pass_on()
    sums["b"].across()
    sums["a"].across()
    sums["u"].hand_out()
    scatter_three.hop_on()
    sums["o"].across()
    sums["b"].hand_out()
    sums["a"].hand_out()
    sums["u"].pass_on()
    sums["d"].share()
    sums["o"].hand_out()
    acc = tok[...]
    for n in range(7):
        net.landed(tok_one.at[n], tok_site + n)
        acc = acc + tok_one[n]
    tok_sum[...] = acc
    tok_sent = [
        net.send(tok_sum, tok_two.at[n], tok_site + 7 + n, net.peer(dy=dy, dz=dz))
        for n, (dy, dz) in enumerate(others)
    ]
    gone = {id(remote) for remote in tok_sent}
    net.pending = [p for p in net.pending if id(p[0]) not in gone]
    back_a[...] = (mid[...] + scatter_three.total() + vec[5:6, :]).astype(BF)
    send_out(back_a, res_out, res_site)
    sums["b"].pass_on()
    sums["a"].pass_on()
    sums["u"].share()
    acc_s = small[...]
    for n in range(3):
        net.landed(small_land.at[n], small_site + n)
        acc_s = acc_s + small_land[n]
    small_sum[...] = acc_s
    out_small[net.slice] = acc_s
    for n, (dk, dz) in enumerate(((1, 0), (0, 1), (1, 1))):
        net.send(
            small_sum, out_small.at[net.slice], small_site + 3 + n, net.peer(dk=dk, dz=dz)
        )
    sums["b"].share()
    sums["a"].share()
    sums["o"].pass_on()
    sums["o"].share()
    for n in range(3):
        net.landed(tok_two.at[n], tok_site + 7 + n)
        acc = acc + tok_two[n]
    for remote in tok_sent:
        remote.wait_send()
    tok_sum[...] = acc
    out_tok[...] = tok_sum[:, span(row, quarter)]
    for n, flip in enumerate((1, 2, 3)):
        net.landed(out_small.at[net.slice ^ flip], small_site + 3 + n)
    for one_sum in sums.values():
        one_sum.finish()
    out_ready(res_out, res_site)
    out_ready(grad_out, grad_site)
    net.drain()
    used.append(net.used)


def layer_on_square(
    inputs, cotangent, seg_parent, token_depth, ln1_gain, ln1_bias, w_qkv, b_qv, w_out, b_out,
    ln2_gain, ln2_bias, w_up, b_up, w_down, b_down,
):
    half_tokens, quarter = inputs.shape
    tokens, width = token_depth.shape[0], 4 * quarter
    shard = tokens // 8
    head = HD
    slices = w_qkv.shape[2] // head
    hidden = w_up.shape[1] // slices
    row = lax.axis_index("row")

    any_ = pl.BlockSpec(memory_space=pl.ANY)
    vmem = pl.BlockSpec(memory_space=pltpu.VMEM)
    sds = jax.ShapeDtypeStruct

    def vm(*dims, dtype=BF):
        return pltpu.VMEM(dims, dtype)

    blocks = {
        "a": (quarter, head), "b": (quarter, 2 * head), "o": (head, quarter),
        "d": (hidden, quarter), "u": (quarter, hidden),
    }
    names = ("a", "b", "o", "d", "u")
    halves = {n: (blocks[n][0] // 2, blocks[n][1]) for n in names}
    scratch = [
        vm(shard, width),
        *[vm(8, shard, width) for _ in range(5)],
        vm(width, 3 * head), vm(hidden, width), vm(width, hidden),
        vm(shard, width), vm(shard, width),
        vm(2, 16, 128, dtype=F32), vm(8, quarter, dtype=F32), vm(8, width, dtype=F32),
        vm(16, tokens, dtype=F32),
        *[vm(tokens, head) for _ in range(3)], vm(tokens, tokens),
        vm(tokens, head, dtype=F32), vm(tokens, head),
        *[
            spec
            for _ in range(2)
            for spec in (
                vm(8, shard, width), vm(2, shard, width),
                vm(shard, width, dtype=F32), vm(shard, width),
            )
        ],
        vm(3, 4, shard, width), vm(3, 2, shard, width), vm(3, shard, width),
        vm(tokens, hidden), vm(tokens, hidden),
        vm(tokens, head), vm(tokens, head, dtype=F32), vm(tokens, head, dtype=F32),
        vm(tokens, 3 * head),
        vm(shard, width, dtype=F32), vm(shard, width, dtype=F32), vm(shard, width), vm(shard, width),
        *[vm(2, 2, 2, *halves[n]) for n in names],
        *[vm(2, 2, *halves[n]) for n in names],
        *[vm(2, *halves[n]) for n in names],
        *[vm(2, *halves[n]) for n in names],
        *[vm(2, *halves[n]) for n in names],
        vm(8, width, dtype=F32), vm(7, 8, width, dtype=F32), vm(8, width, dtype=F32),
        vm(3, 8, width, dtype=F32),
        vm(8, hidden, dtype=F32), vm(3, 8, hidden, dtype=F32), vm(8, hidden, dtype=F32),
        pltpu.SemaphoreType.DMA((208,)), pltpu.SemaphoreType.DMA((208,)),
        pltpu.SemaphoreType.DMA((10,)),
    ]
    used = []
    outs = pl.pallas_call(
        functools.partial(layer_kernel, EPS, MASKED, used),
        out_shape=(
            sds((half_tokens, quarter), BF), sds((half_tokens, quarter), BF),
            *[sds((slices, *blocks[n]), BF) for n in names],
            sds((8, quarter), F32), sds((slices, 8, hidden), F32),
        ),
        in_specs=[any_] * 12 + [pl.BlockSpec(memory_space=pltpu.SMEM)] + [vmem] * 2,
        out_specs=(any_,) * 7 + (vmem,) * 2,
        scratch_shapes=scratch,
        compiler_params=pltpu.CompilerParams(
            collective_id=0, has_side_effects=True, vmem_limit_bytes=60 << 20
        ),
        name="tree_layer",
    )(
        inputs, cotangent, w_qkv.transpose(1, 0, 2), w_out, w_down, w_up,
        *[v.reshape(1, -1) for v in (ln1_gain, ln1_bias, b_out, ln2_gain, ln2_bias, b_down)],
        seg_parent, b_up.reshape(1, -1), b_qv,
    )
    result, input_grad, g_a, g_b, g_o, g_d, g_u, by_token, small = outs
    steps = 2

    def finish(res_in, grad_in, a_in, b_in, o_in, d_in, u_in, tok_in, small_in, *into):
        res, grad, q, o, d, u, tok_0, tok_1, tok_2, tok_3, tok_4, tok_5, up, qv = into
        res[...] = res_in[...].astype(F32)
        grad[...] = grad_in[...].astype(F32)
        o[...] = o_in[...].astype(F32)
        d[...] = d_in[...].astype(F32)
        for s in range(slices):
            u[:, s * hidden : (s + 1) * hidden] = u_in[s].astype(F32)
            at = slice(s * head, (s + 1) * head)
            q[0, :, at] = a_in[s].astype(F32)
            for n in range(2):
                q[n + 1, :, at] = b_in[s, :, n * head : (n + 1) * head].astype(F32)
            up[0:1, s * hidden : (s + 1) * hidden] = small_in[s, 0:1, :]
            for n in range(2):
                qv[n : n + 1, at] = small_in[
                    s, 1:2, n * head : (n + 1) * head
                ]
        for n, one in enumerate((tok_0, tok_1, tok_2, tok_3, tok_4, tok_5)):
            one[...] = tok_in[n : n + 1, :]

    def rows(*dims):
        return pl.BlockSpec((dims[0] // steps, *dims[1:]), lambda i: (i,) + (0,) * (len(dims) - 1))

    def middle(*dims):
        return pl.BlockSpec((dims[0], dims[1] // steps, *dims[2:]), lambda i: (0, i, 0))

    def fixed(*dims):
        return pl.BlockSpec(dims, lambda i: (0,) * len(dims))

    tall_o, tall_d = (slices * head, quarter), (slices * hidden, quarter)
    done = pl.pallas_call(
        finish,
        grid=(steps,),
        out_shape=(
            sds((half_tokens, quarter), F32), sds((half_tokens, quarter), F32),
            sds((3, quarter, slices * head), F32), sds(tall_o, F32), sds(tall_d, F32),
            sds((quarter, slices * hidden), F32), *[sds((1, quarter), F32)] * 6,
            sds((1, slices * hidden), F32), sds((2, slices * head), F32),
        ),
        in_specs=[
            rows(half_tokens, quarter), rows(half_tokens, quarter),
            middle(slices, *blocks["a"]), middle(slices, *blocks["b"]), rows(*tall_o), rows(*tall_d), middle(slices, *blocks["u"]),
            fixed(8, quarter), fixed(slices, 8, hidden),
        ],
        out_specs=(
            rows(half_tokens, quarter), rows(half_tokens, quarter),
            middle(3, quarter, slices * head), rows(*tall_o), rows(*tall_d),
            rows(quarter, slices * hidden), *[fixed(1, quarter)] * 6,
            fixed(1, slices * hidden), fixed(2, slices * head),
        ),
        compiler_params=pltpu.CompilerParams(vmem_limit_bytes=60 << 20),
        name="finish",
    )(
        result, input_grad, g_a, g_b, g_o.reshape(tall_o), g_d.reshape(tall_d), g_u, by_token, small
    )
    by_token = [v.reshape(-1) for v in done[6:12]]
    return (
        done[0], done[1], by_token[0], by_token[1], done[2].transpose(1, 0, 2), done[13], done[3], by_token[4],
        by_token[2], by_token[3], done[5], done[12].reshape(-1), done[4], by_token[5],
    )


def fits_square(mesh, *arrays):
    sizes = tuple(mesh.shape[name] for name in ("dp", "row", "col"))
    return (
        sizes == (4, 4, 2)
        and arrays[0].shape == (512, 256)
        and arrays[2].shape == (13,)
        and arrays[3].shape == (1024,)
        and arrays[6].shape == (256, 3, 512)
        and arrays[12].shape == (256, 2048)
    )


def solution(mesh):
    placed = (
        P(("dp", "col"), "row"),
        P(("dp", "col"), "row"),
        P("dp"),
        P("dp"),
        P("row"),
        P("row"),
        P("row", None, "col"),
        P(None, "col"),
        P("col", "row"),
        P("row"),
        P("row"),
        P("row"),
        P("row", "col"),
        P("col"),
        P("col", "row"),
        P("row"),
    )

    def on_each(*arrays):
        return (layer_on_square if fits_square(mesh, *arrays) else on_device)(*arrays)

    return jax.shard_map(
        on_each,
        mesh=mesh,
        in_specs=placed,
        out_specs=(
            P(("dp", "col"), "row"),
            P(("dp", "col"), "row"),
            P("row"),
            P("row"),
            P("row", None, "col"),
            P(None, "col"),
            P("col", "row"),
            P("row"),
            P("row"),
            P("row"),
            P("row", "col"),
            P("col"),
            P("col", "row"),
            P("row"),
        ),
        check_vma=False,
    )
```
